32 devices in a mesh: ctx: 16 (over z, x, core), fsdp: 2 (over y).
Axes of the slice: x: 2, y: 2, z: 4, core: 2. Of those that a mesh axis runs over, the one named last changes fastest.
Arguments:
- tokens: bfloat16 [2, 4096, 512], P('fsdp', 'ctx'), may hold values from -6 to 6
- memory: bfloat16 [2, 2048, 512], P('fsdp', 'ctx'), may hold values from -6 to 6
- token_seg: int32 [2, 4096], P('fsdp'), may hold values from 0 to 7, as said below
- memory_seg: int32 [2, 2048], P('fsdp'), may hold values from 0 to 7, as said below
- out_grad: bfloat16 [2, 4096, 512], P('fsdp', 'ctx'), may hold values from -6 to 6
- in_proj: float32 [6, 512, 512], P(None, 'fsdp'), may hold values from -0.25 to 0.25
- out_proj: float32 [2, 512, 512], P(None, 'fsdp'), may hold values from -1 to 1
- ffn_in: float32 [512, 2048], P('fsdp'), may hold values from -0.25 to 0.25
- ffn_out: float32 [2048, 512], P('fsdp'), may hold values from -0.125 to 0.125
- norm_gain: float32 [3, 512], P(None, 'fsdp'), may hold values from 0.5 to 1.5
- bias_rows: float32 [10, 512], P(None, 'fsdp'), may hold values from -1.8 to 1.8
- ffn_bias: float32 [2048], P('fsdp'), may hold values from -3 to 3
Outputs:
- layer_out: float32 [2, 4096, 512], P('fsdp', 'ctx')
- tokens_grad: float32 [2, 4096, 512], P('fsdp', 'ctx')
- memory_grad: float32 [2, 2048, 512], P('fsdp', 'ctx')
- in_proj_grad: float32 [6, 512, 512], P(None, 'fsdp')
- out_proj_grad: float32 [2, 512, 512], P(None, 'fsdp')
- ffn_in_grad: float32 [512, 2048], P('fsdp')
- ffn_out_grad: float32 [2048, 512], P('fsdp')
- norm_gain_grad: float32 [3, 512], P(None, 'fsdp')
- bias_rows_grad: float32 [10, 512], P(None, 'fsdp')
- ffn_bias_grad: float32 [2048], P('fsdp')
The draws below stay inside these ranges and needn't reach their ends.
Inputs may be any that keep to these rules, and one draw needn't show every extreme that they name: `token_seg`: along a sequence the ids never fall, and every document 0 to 7 occurs. In each sequence one document holds target tokens on every index of ctx. `memory_seg`: along a sequence the ids never fall; every document 0 to 7 has between 1 and 512 memory tokens, and the document that holds target tokens on every index of ctx has exactly 512.
All inputs are finite; a program needn't handle non-finite values.
Results may differ from the reference program's by a relative error of at most 0.022.
Values may be sent and summed in bfloat16 or wider, within the bound.
No kernel may reach another device: no remote copies, remote signals or barrier semaphores. Data moves between devices by JAX's collectives and lax.ppermute only.
A program may use at most 192 MiB of HBM per device.

```python
import math
import jax
import jax.numpy as jnp
from jax import lax

D = 512
HEADS = 8
FF = 2048
HD = 64
TOK_DEV = 256
MEM_MOST = 512
SEQ = 4096
MEMLEN = 2048
DOCS = 8
SEQS = 2


def doc_layout(key):
    base = jax.random.fold_in(key, 101)
    head_key, tail_key, count_key = jax.random.split(base, 3)
    head_len = jax.random.randint(head_key, (SEQS,), DOCS, TOK_DEV, dtype=jnp.int32)
    tail_len = jax.random.randint(tail_key, (SEQS,), DOCS, TOK_DEV, dtype=jnp.int32)
    before_docs = jax.random.randint(count_key, (SEQS,), 1, DOCS - 1, dtype=jnp.int32)
    return (head_len, tail_len, before_docs)


def draw_token_seg(key, part):
    head_len, tail_len, before_docs = doc_layout(key)
    position = jnp.arange(SEQ, dtype=jnp.int32)[None, :]
    head_col = head_len[:, None]
    tail_col = tail_len[:, None]
    before_col = before_docs[:, None]
    after_docs = DOCS - 1 - before_col
    tail_start = SEQ - tail_col
    first_ids = position * before_col // head_col
    last_ids = before_col + 1 + (position - tail_start) * after_docs // tail_col
    result = jnp.where(position < head_col, first_ids, jnp.where(position >= tail_start, last_ids, before_col))
    return result.astype(jnp.int32)


def draw_memory_seg(key, part):
    head_len, tail_len, before_docs = doc_layout(key)
    position = jnp.arange(MEMLEN, dtype=jnp.int32)[None, :]
    before_col = before_docs[:, None]
    after_docs = DOCS - 1 - before_col
    rest_len = MEMLEN - MEM_MOST
    lead_len = rest_len * before_col // (DOCS - 1)
    trail_len = rest_len - lead_len
    trail_start = lead_len + MEM_MOST
    first_ids = position * before_col // jnp.maximum(lead_len, 1)
    last_ids = before_col + 1 + (position - trail_start) * after_docs // jnp.maximum(trail_len, 1)
    result = jnp.where(position < lead_len, first_ids, jnp.where(position >= trail_start, last_ids, before_col))
    return result.astype(jnp.int32)


def block_levels(key, extent, pieces, least, largest):
    factor_of = 1.0
    for dim, blocks in pieces:
        steps = jax.random.uniform(jax.random.fold_in(jax.random.fold_in(key, 6), dim), (blocks,), jnp.float32, least / len(pieces), largest / len(pieces))
        factor_of = factor_of * jnp.repeat(jnp.exp(steps), extent[dim] // blocks).reshape((-1,) + (1,) * (len(extent) - 1 - dim))
    return factor_of


def normal_values(own_key, shape, width, bound, cuts=(), held_as=jnp.bfloat16):
    gain = block_levels(own_key, shape, cuts, -0.22, 0.18) if cuts else 1.0
    values = jax.random.normal(own_key, shape, jnp.float32) * width * gain
    return jnp.minimum(jnp.maximum(values, -bound), bound).astype(held_as)


def setup_inputs(seed: int = 0) -> dict:
    keys = jax.random.split(jax.random.key(seed), 13)
    return {
        "tokens": normal_values(keys[0], (SEQS, SEQ, D), 1.0, 6.0, ((0, 2), (1, 16))),
        "memory": normal_values(keys[1], (SEQS, MEMLEN, D), 1.0, 6.0, ((0, 2), (1, 16))),
        "token_seg": draw_token_seg(jax.random.fold_in(keys[12], 71), 0),
        "memory_seg": draw_memory_seg(jax.random.fold_in(keys[12], 71), 0),
        "out_grad": normal_values(keys[4], (SEQS, SEQ, D), 1.0, 6.0, ((0, 2), (1, 16))),
        "in_proj": normal_values(keys[5], (6, D, D), D ** -0.5, 0.25, ((1, 2),), jnp.float32),
        "out_proj": normal_values(keys[6], (2, D, D), (D // 16) ** -0.5, 1.0, ((1, 2),), jnp.float32),
        "ffn_in": normal_values(keys[7], (D, FF), D ** -0.5, 0.25, ((0, 2),), jnp.float32),
        "ffn_out": normal_values(keys[8], (FF, D), FF ** -0.5, 0.125, ((0, 2),), jnp.float32),
        "norm_gain": jnp.clip(1.0 + 0.1 * jax.random.normal(keys[9], (3, D), jnp.float32), 0.5, 1.5),
        "bias_rows": normal_values(keys[10], (10, D), 0.3, 1.8, ((1, 2),), jnp.float32),
        "ffn_bias": normal_values(keys[11], (FF,), 0.5, 3.0, ((0, 2),), jnp.float32),
    }


@jax.custom_vjp
def low(v):
    return lax.optimization_barrier(v.astype(jnp.bfloat16)).astype(jnp.float32)

@jax.custom_vjp
def low_back(v):
    return v

def low_keep(v):
    return (low(v), None)

def low_pass(kept, grad):
    return (grad,)

def back_keep(v):
    return (v, None)

def back_low(kept, grad):
    return (low(grad),)
low.defvjp(low_keep, low_pass)
low_back.defvjp(back_keep, back_low)
neg_fill = -1e+30
eps_norm = 1e-05
query_block = 512

def matmul(first_op, second_op):
    return jnp.dot(first_op, second_op, precision=lax.Precision.HIGHEST, preferred_element_type=jnp.float32)

def layer_norm(residual, gain_row, shift_row):
    centre = residual - lax.optimization_barrier(jnp.mean(residual, axis=-1, keepdims=True))
    spread = lax.optimization_barrier(jnp.mean(centre * centre, axis=-1, keepdims=True))
    return centre * lax.rsqrt(spread + eps_norm) * gain_row + shift_row

def attention(queries, key_rows, value_rows, query_seg, key_seg, causal):
    length = queries.shape[0]
    block_len = min(query_block, length)
    block_count = length // block_len
    score_scale = 1.0 / math.sqrt(HD)
    key_pos = jnp.arange(key_rows.shape[0], dtype=jnp.int32)
    key_heads = key_rows.reshape(key_rows.shape[0], HEADS, HD)
    value_heads = value_rows.reshape(value_rows.shape[0], HEADS, HD)

    def one_block(block_items):
        block_query, block_seg, block_pos = block_items
        query_heads = block_query.reshape(block_len, HEADS, HD)
        scores = jnp.einsum('qhd,khd->hqk', query_heads, key_heads, precision=lax.Precision.HIGHEST) * score_scale
        allowed = block_seg[:, None] == key_seg[None, :]
        if causal:
            allowed = allowed & (key_pos[None, :] <= block_pos[:, None])
        scores = low_back(jnp.where(allowed[None], scores, neg_fill))
        attn_prob = jax.nn.softmax(scores, axis=-1)
        mixed_rows = jnp.einsum('hqk,khd->qhd', low(attn_prob), value_heads, precision=lax.Precision.HIGHEST)
        return mixed_rows.reshape(block_len, HEADS * HD)
    query_pos = jnp.arange(length, dtype=jnp.int32)
    result = lax.map(jax.checkpoint(one_block), (queries.reshape(block_count, block_len, -1), query_seg.reshape(block_count, block_len), query_pos.reshape(block_count, block_len)))
    return result.reshape(length, HEADS * HD)

def decoder_layer(params, tok_rows, mem_rows, token_segs, memory_segs):
    proj_in, proj_out, ffn_up, ffn_down, gain_rows, biases, ffn_shift = [low(member) for member in params]
    query_self = low(low_back(matmul(tok_rows, proj_in[0]) + biases[0]))
    keys_self = low(low_back(matmul(tok_rows, proj_in[1])))
    values_self = low(low_back(matmul(tok_rows, proj_in[2]) + biases[1]))
    attn_self = low(low_back(attention(query_self, keys_self, values_self, token_segs, token_segs, True)))
    hidden_one = layer_norm(tok_rows + low_back(matmul(attn_self, proj_out[0]) + biases[2]), gain_rows[0], biases[3])
    query_cross = low(low_back(matmul(low(hidden_one), proj_in[3]) + biases[4]))
    keys_cross = low(low_back(matmul(mem_rows, proj_in[4])))
    values_cross = low(low_back(matmul(mem_rows, proj_in[5]) + biases[5]))
    attn_cross = low(low_back(attention(query_cross, keys_cross, values_cross, token_segs, memory_segs, False)))
    hidden_two = layer_norm(hidden_one + low_back(matmul(attn_cross, proj_out[1]) + biases[6]), gain_rows[1], biases[7])
    ffn_pre = low_back(matmul(low(hidden_two), ffn_up) + ffn_shift)
    ffn_act = low(jax.nn.silu(ffn_pre))
    return layer_norm(hidden_two + low_back(matmul(ffn_act, ffn_down) + biases[8]), gain_rows[2], biases[9])

def reference(tokens, memory, token_seg, memory_seg, out_grad, in_proj, out_proj, ffn_in, ffn_out, norm_gain, bias_rows, ffn_bias):
    params = (in_proj, out_proj, ffn_in, ffn_out, norm_gain, bias_rows, ffn_bias)

    def per_seq(grad_total, seq_items):
        tok_rows, mem_rows, token_segs, memory_segs, seq_grad = seq_items
        layer_rows, pull_back = jax.vjp(lambda weights, inputs, sources: decoder_layer(weights, inputs, sources, token_segs, memory_segs), params, tok_rows.astype(jnp.float32), mem_rows.astype(jnp.float32))
        param_grads, tok_grad, mem_grad = pull_back(seq_grad.astype(jnp.float32))
        grad_total = jax.tree.map(lambda first_op, second_op: first_op + second_op, grad_total, param_grads)
        return (grad_total, (layer_rows, tok_grad, mem_grad))
    grad_start = jax.tree.map(jnp.zeros_like, params)
    grad_total, stacked = lax.scan(per_seq, grad_start, (tokens, memory, token_seg, memory_seg, out_grad))
    return (stacked[0], stacked[1], stacked[2], grad_total[0], grad_total[1], grad_total[2], grad_total[3], grad_total[4], grad_total[5], grad_total[6])
```

```python
import math

import jax
import jax.numpy as jnp
from jax import lax
from jax.experimental import pallas as pl
from jax.experimental.pallas import tpu as pltpu
from jax.sharding import PartitionSpec as P

HEADS = 8
PAIRS = HEADS // 2
neg_fill = -1e30
eps_norm = 1e-05
self_block = 512
bf16 = jnp.bfloat16
f32 = jnp.float32
vmem_bytes = 60 * 1024 * 1024
half_rows = 256


def dot_nn(first_op, second_op):
    return jnp.dot(first_op, second_op, preferred_element_type=f32)


def dot_nt(first_op, second_op):
    return lax.dot_general(
        first_op, second_op, (((1,), (1,)), ((), ())), preferred_element_type=f32
    )


def dot_tn(first_op, second_op):
    return lax.dot_general(
        first_op, second_op, (((0,), (0,)), ((), ())), preferred_element_type=f32
    )


def stack_heads(tile):
    lane = lax.broadcasted_iota(jnp.int32, tile.shape, 1)
    half = tile.shape[1] // 2
    zero = jnp.zeros_like(tile)
    return jnp.concatenate(
        [jnp.where(lane < half, tile, zero), jnp.where(lane >= half, tile, zero)], axis=0
    )


def merge_heads(stacked):
    rows = stacked.shape[0] // 2
    lane = lax.broadcasted_iota(jnp.int32, (rows, stacked.shape[1]), 1)
    return jnp.where(lane < stacked.shape[1] // 2, stacked[:rows], stacked[rows:])


def tile_of(value, pair, tile_width):
    return value[:, pair * tile_width : (pair + 1) * tile_width]


def attend(q_block, kv_ref, low_col, high_col, first, last, key_rows, factor, scratch):
    max_ref, sum_ref, acc_ref = scratch
    width = q_block.shape[1]
    tile_width = width // PAIRS
    stacked = [stack_heads(tile_of(q_block, pair, tile_width)) for pair in range(PAIRS)]
    low2 = jnp.concatenate([low_col, low_col], axis=0)
    high2 = jnp.concatenate([high_col, high_col], axis=0)
    max_ref[...] = jnp.full(max_ref.shape, neg_fill, f32)
    sum_ref[...] = jnp.zeros(sum_ref.shape, f32)
    acc_ref[...] = jnp.zeros(acc_ref.shape, f32)

    def step(index, carry):
        base = pl.multiple_of(index * key_rows, key_rows)
        key_pos = base + lax.broadcasted_iota(jnp.int32, (1, key_rows), 1)
        allowed = (key_pos >= low2) & (key_pos <= high2)
        for pair in range(PAIRS):
            start = pair * tile_width
            keys = kv_ref[pl.ds(base, key_rows), start : start + tile_width]
            values = kv_ref[pl.ds(base, key_rows), width + start : width + start + tile_width]
            scores = jnp.where(allowed, dot_nt(stacked[pair], keys), neg_fill)
            old_max = max_ref[pair]
            new_max = jnp.maximum(old_max, jnp.max(scores, axis=1, keepdims=True))
            probs = jnp.exp2((scores - new_max) * factor)
            rescale = jnp.exp2((old_max - new_max) * factor)
            sum_ref[pair] = sum_ref[pair] * rescale + jnp.sum(probs, axis=1, keepdims=True)
            acc_ref[pair] = acc_ref[pair] * rescale + dot_nn(probs.astype(bf16), values)
            max_ref[pair] = new_max
        return carry

    lax.fori_loop(first, last, step, 0)
    outputs, log_sums = [], []
    for pair in range(PAIRS):
        outputs.append(merge_heads(acc_ref[pair] / sum_ref[pair]))
        log_sums.append(max_ref[pair] * factor + jnp.log2(sum_ref[pair]))
    return jnp.concatenate(outputs, axis=1), log_sums


def columns_to_rows(columns):
    rows = columns[0].shape[0]
    lane = lax.broadcasted_iota(jnp.int32, (rows, 128), 1)
    packed = jnp.zeros((rows, 128), f32)
    for index, column in enumerate(columns):
        packed = jnp.where(lane == index, column, packed)
    return jnp.transpose(packed)


def head_sums(product):
    width = product.shape[1]
    head = lax.broadcasted_iota(jnp.int32, (HEADS, width), 0)
    lane = lax.broadcasted_iota(jnp.int32, (HEADS, width), 1)
    pick = (lane // (width // HEADS) == head).astype(f32)
    return lax.dot_general(
        pick,
        product,
        (((1,), (1,)), ((), ())),
        precision=lax.Precision.HIGHEST,
        preferred_element_type=f32,
    )


def attend_back(
    q_block, g_block, kv_ref, dkv_ref, low_row, high_row, log_rows, delta_rows,
    first, last, key_rows, factor, scale, dq_ref, adding,
):
    width = q_block.shape[1]
    tile_width = width // PAIRS
    rows = q_block.shape[0]
    q2 = [stack_heads(tile_of(q_block, pair, tile_width)) for pair in range(PAIRS)]
    g2 = [stack_heads(tile_of(g_block, pair, tile_width)) for pair in range(PAIRS)]
    low2 = jnp.concatenate([low_row, low_row], axis=1)
    high2 = jnp.concatenate([high_row, high_row], axis=1)
    dq_ref[...] = jnp.zeros(dq_ref.shape, f32)

    def step(index, carry):
        base = pl.multiple_of(index * key_rows, key_rows)
        key_pos = base + lax.broadcasted_iota(jnp.int32, (key_rows, 1), 0)
        allowed = (key_pos >= low2) & (key_pos <= high2)
        for pair in range(PAIRS):
            key_at = (pl.ds(base, key_rows), slice(pair * tile_width, (pair + 1) * tile_width))
            value_at = (
                pl.ds(base, key_rows),
                slice(width + pair * tile_width, width + (pair + 1) * tile_width),
            )
            keys = kv_ref[key_at]
            values = kv_ref[value_at]
            scores = dot_nt(keys, q2[pair])
            probs = jnp.where(allowed, jnp.exp2(scores * factor - log_rows[pair]), 0.0)
            prob_grad = dot_nt(values, g2[pair])
            score_grad = (probs * (prob_grad - delta_rows[pair])).astype(bf16)
            key_grad = dot_nn(score_grad, q2[pair]) * scale
            value_grad = dot_nn(probs.astype(bf16), g2[pair])
            if adding:
                key_grad = key_grad + dkv_ref[key_at].astype(f32)
                value_grad = value_grad + dkv_ref[value_at].astype(f32)
            dkv_ref[key_at] = key_grad.astype(bf16)
            dkv_ref[value_at] = value_grad.astype(bf16)
            dq_ref[pair] += dot_tn(keys, score_grad)
        return carry

    lax.fori_loop(first, last, step, 0)
    tiles = []
    for pair in range(PAIRS):
        both = dq_ref[pair]
        feature = lax.broadcasted_iota(jnp.int32, (tile_width, rows), 0)
        picked = jnp.where(feature < tile_width // 2, both[:, :rows], both[:, rows:])
        tiles.append(jnp.transpose(picked) * scale)
    return jnp.concatenate(tiles, axis=1)


def query_grads(
    q_block, g_block, kv_ref, low_col, high_col, log_cols, delta_cols, first, last,
    key_rows, factor, scale, acc_ref,
):
    width = q_block.shape[1]
    tile_width = width // PAIRS
    q2 = [stack_heads(tile_of(q_block, pair, tile_width)) for pair in range(PAIRS)]
    g2 = [stack_heads(tile_of(g_block, pair, tile_width)) for pair in range(PAIRS)]
    low2 = jnp.concatenate([low_col, low_col], axis=0)
    high2 = jnp.concatenate([high_col, high_col], axis=0)
    acc_ref[...] = jnp.zeros(acc_ref.shape, f32)

    def step(index, carry):
        base = pl.multiple_of(index * key_rows, key_rows)
        key_pos = base + lax.broadcasted_iota(jnp.int32, (1, key_rows), 1)
        allowed = (key_pos >= low2) & (key_pos <= high2)
        for pair in range(PAIRS):
            start = pair * tile_width
            keys = kv_ref[pl.ds(base, key_rows), start : start + tile_width]
            values = kv_ref[pl.ds(base, key_rows), width + start : width + start + tile_width]
            scores = dot_nt(q2[pair], keys)
            probs = jnp.where(allowed, jnp.exp2(scores * factor - log_cols[pair]), 0.0)
            prob_grad = dot_nt(g2[pair], values)
            score_grad = (probs * (prob_grad - delta_cols[pair])).astype(bf16)
            acc_ref[pair] += dot_nn(score_grad, keys)
        return carry

    lax.fori_loop(first, last, step, 0)
    return jnp.concatenate([merge_heads(acc_ref[p]) * scale for p in range(PAIRS)], axis=1)


def key_grads(
    k_block, v_block, q_ref, g_ref, stats_ref, low_col, high_col, first, last,
    factor, scale, dk_ref, dv_ref,
):
    width = k_block.shape[1]
    tile_width = width // PAIRS
    rows = k_block.shape[0]
    query_rows = self_block
    blocks = query_rows // rows
    k2 = [stack_heads(tile_of(k_block, pair, tile_width)) for pair in range(PAIRS)]
    v2 = [stack_heads(tile_of(v_block, pair, tile_width)) for pair in range(PAIRS)]
    low2 = jnp.concatenate([low_col, low_col], axis=0)
    high2 = jnp.concatenate([high_col, high_col], axis=0)
    dk_ref[...] = jnp.zeros(dk_ref.shape, f32)
    dv_ref[...] = jnp.zeros(dv_ref.shape, f32)

    def step(index, carry):
        base = pl.multiple_of(index * query_rows, query_rows)
        query_pos = base + lax.broadcasted_iota(jnp.int32, (1, query_rows), 1)
        allowed = (query_pos >= low2) & (query_pos <= high2)
        stats = jnp.concatenate([stats_ref[index * blocks + u] for u in range(blocks)], axis=1)

        def two_rows(first_row):
            return jnp.concatenate(
                [
                    jnp.broadcast_to(stats[first_row : first_row + 1], (rows, query_rows)),
                    jnp.broadcast_to(stats[first_row + 1 : first_row + 2], (rows, query_rows)),
                ],
                axis=0,
            )

        for pair in range(PAIRS):
            at = (pl.ds(base, query_rows), slice(pair * tile_width, (pair + 1) * tile_width))
            queries = q_ref[at]
            upstream = g_ref[at]
            scores = dot_nt(k2[pair], queries)
            probs = jnp.where(allowed, jnp.exp2(scores * factor - two_rows(2 * pair)), 0.0)
            prob_grad = dot_nt(v2[pair], upstream)
            score_grad = (probs * (prob_grad - two_rows(HEADS + 2 * pair))).astype(bf16)
            dk_ref[pair] += dot_nn(score_grad, queries)
            dv_ref[pair] += dot_nn(probs.astype(bf16), upstream)
        return carry

    lax.fori_loop(first, last, step, 0)
    key_grad = jnp.concatenate([merge_heads(dk_ref[p]) * scale for p in range(PAIRS)], axis=1)
    value_grad = jnp.concatenate([merge_heads(dv_ref[p]) for p in range(PAIRS)], axis=1)
    return key_grad, value_grad


def split_three(value):
    one = value.astype(bf16)
    rest = value - one.astype(f32)
    two = rest.astype(bf16)
    three = (rest - two.astype(f32)).astype(bf16)
    return [one, two, three]


def side_by_side(stats):
    rows = stats.shape[0] // 2
    return jnp.concatenate([stats[:rows], stats[rows:]], axis=1)


def gathered_chunks(piece_refs, planes):
    for s in range(planes):
        for dx in range(2):
            for dc in range(2):
                yield 4 * s + 2 * dx + dc, piece_refs[dc * planes + s].at[dx]


class PieceSink:
    def __init__(self, keep_ref, send_ref, scratch_ref, me, side):
        self.keep, self.send, self.scratch, self.me, self.side = keep_ref, send_ref, scratch_ref, me, side

    def emit(self, block, stride, offset):
        planes = self.keep.shape[2]
        count = 4 * planes
        piece = half_rows // count
        at = slice(block * piece, (block + 1) * piece)
        for r in range(count):
            s, dx, dc = r >> 2, (r >> 1) & 1, r & 1
            for fy in range(2):
                source = (self.side ^ fy) * stride + offset + (self.me ^ r) * piece
                rows = self.scratch[pl.ds(pl.multiple_of(source, piece), piece), :]
                target = self.send if dc else self.keep
                target[fy, dx, s, at, :] = rows.astype(bf16)

    def put(self, block, matrix):
        rows = matrix.shape[0]
        self.scratch[0:rows, :] = matrix.astype(f32)
        blocks = rows // (2 * half_rows)
        for b in range(blocks):
            self.emit(block + b, rows // 2, b * half_rows)


class PlainSink:
    def __init__(self, plain_ref):
        self.plain = plain_ref

    def put(self, block, matrix):
        size = 2 * half_rows
        for b in range(matrix.shape[0] // size):
            self.plain[block + b] = matrix[b * size : (b + 1) * size].astype(bf16)


def pair_rows(by_head, block, rows, pair):
    at = slice(block * rows, (block + 1) * rows)
    return jnp.concatenate(
        [by_head[2 * pair : 2 * pair + 1, at], by_head[2 * pair + 1 : 2 * pair + 2, at]], axis=1
    )


def norm_stats(residual):
    centre = residual - jnp.mean(residual, axis=1, keepdims=True)
    spread = jnp.mean(centre * centre, axis=1, keepdims=True)
    inverse = lax.rsqrt(spread + eps_norm)
    return centre * inverse, inverse


def norm_back(normed, inverse, gain_row, upstream):
    scaled = upstream * gain_row
    mean_one = jnp.mean(scaled, axis=1, keepdims=True)
    mean_two = jnp.mean(scaled * normed, axis=1, keepdims=True)
    return (scaled - mean_one - normed * mean_two) * inverse


def column_sum(matrix):
    return jnp.sum(matrix.astype(f32), axis=0, keepdims=True)


def self_forward_kernel(
    bounds_ref, x_ref, w_ref, bias_ref, cols_ref, *refs, factor, planes,
):
    pieces, refs = refs[: 2 * planes], refs[2 * planes :]
    q_ref, a_ref, log_ref, kv_ref, max_ref, sum_ref, acc_ref = refs
    me = bounds_ref[12]
    rows, width = x_ref.shape
    for r, chunk in gathered_chunks(pieces, planes):
        at = pl.ds(pl.multiple_of((me ^ r) * rows, rows), rows)
        block = chunk[...]
        kv_ref[at, 0:width] = dot_nn(block, w_ref[1]).astype(bf16)
        kv_ref[at, width:] = (dot_nn(block, w_ref[2]) + bias_ref[1:2, :]).astype(bf16)
    q_rows = (dot_nn(x_ref[...], w_ref[0]) + bias_ref[0:1, :]).astype(bf16)
    q_ref[...] = q_rows
    half = rows // 2
    columns = []
    for block in range(2):
        at = slice(block * half, (block + 1) * half)
        output, log_sums = attend(
            q_rows[at], kv_ref, cols_ref[at, 0:1], cols_ref[at, 1:2],
            bounds_ref[2 * block], bounds_ref[2 * block + 1], self_block, factor,
            (max_ref, sum_ref, acc_ref),
        )
        a_ref[at, :] = output
        columns += log_sums
    packed = columns_to_rows(columns)
    by_head = []
    for head in range(HEADS):
        lanes = slice((head % 2) * half, (head % 2 + 1) * half)
        by_head.append(
            jnp.concatenate(
                [packed[b * PAIRS + head // 2 : b * PAIRS + head // 2 + 1, lanes] for b in range(2)],
                axis=1,
            )
        )
    log_ref[...] = jnp.concatenate(by_head, axis=0)


def project_kernel(bounds_ref, w_ref, bias_ref, *refs, planes):
    pieces, (q_ref,) = refs[: 2 * planes], refs[2 * planes :]
    me = bounds_ref[12]
    for r, chunk in gathered_chunks(pieces, planes):
        rows = chunk.shape[0]
        at = pl.ds(pl.multiple_of((me ^ r) * rows, rows), rows)
        q_ref[at, :] = (dot_nn(chunk[...], w_ref[0]) + bias_ref[0:1, :]).astype(bf16)


def middle_kernel(
    bounds_ref, x_ref, a_ref, g_ref, log_ref, cols_ref, rows_ref, gain_ref, bias_ref,
    ffn_bias_ref, wc_ref, u_ref, v_ref, *refs, factor, scale, planes,
):
    pieces, refs = refs[: 2 * planes], refs[2 * planes :]
    (
        out_ref, a_low_ref, h1_ref, h2_ref, f_ref, e3_ref, gu_ref, e2_ref, e1_ref, ac_ref,
        dqc_ref, ga_ref, gr1_ref, delta_ref, pm_keep_ref, pm_send_ref, dwc_ref, sums_ref, csum_ref,
        max_ref, sum_ref, acc_ref, dq_ref, mem_ref, kvc_ref, dkvc_ref, dw_acc_ref, pm_block_ref,
    ) = refs
    me = bounds_ref[12]
    rows, width = x_ref.shape
    half = rows // 2
    mem_rows = pieces[0].shape[1]
    cross_block = 2 * mem_rows
    live_first = jnp.minimum(bounds_ref[4], bounds_ref[6])
    live_last = jnp.maximum(bounds_ref[5], bounds_ref[7])
    for r, chunk in gathered_chunks(pieces, planes):
        mem_ref[pl.ds(pl.multiple_of((me ^ r) * mem_rows, mem_rows), mem_rows), :] = chunk[...]

    def project(index, carry):
        at = pl.ds(pl.multiple_of(index * cross_block, cross_block), cross_block)
        block = mem_ref[at, :]
        kvc_ref[at, 0:width] = dot_nn(block, wc_ref[1]).astype(bf16)
        kvc_ref[at, width:] = (dot_nn(block, wc_ref[2]) + bias_ref[5:6, :]).astype(bf16)
        dkvc_ref[at, :] = jnp.zeros((cross_block, 2 * width), bf16)
        return carry

    lax.fori_loop(live_first, live_last, project, 0)
    attn_self = a_ref[...]
    a_low = attn_self.astype(bf16)
    a_low_ref[...] = a_low
    r1 = x_ref[...].astype(f32) + (dot_nn(a_low, wc_ref[3]) + bias_ref[2:3, :])
    n1, inv1 = norm_stats(r1)
    h1 = n1 * gain_ref[0:1, :] + bias_ref[3:4, :]
    h1_low = h1.astype(bf16)
    h1_ref[...] = h1_low
    qc = (dot_nn(h1_low, wc_ref[0]) + bias_ref[4:5, :]).astype(bf16)
    blocks, columns = [], []
    for block in range(2):
        at = slice(block * half, (block + 1) * half)
        output, log_sums = attend(
            qc[at], kvc_ref, cols_ref[at, 2:3], cols_ref[at, 3:4],
            bounds_ref[4 + 2 * block], bounds_ref[5 + 2 * block], cross_block, factor,
            (max_ref, sum_ref, acc_ref),
        )
        blocks.append(output)
        columns += log_sums
    cross_logs = columns_to_rows(columns)
    attn_cross = jnp.concatenate(blocks, axis=0)
    ac_low = attn_cross.astype(bf16)
    ac_ref[...] = ac_low
    r2 = h1 + (dot_nn(ac_low, wc_ref[4]) + bias_ref[6:7, :])
    n2, inv2 = norm_stats(r2)
    h2 = n2 * gain_ref[1:2, :] + bias_ref[7:8, :]
    h2_low = h2.astype(bf16)
    h2_ref[...] = h2_low
    u = dot_nn(h2_low, u_ref[...]) + ffn_bias_ref[...]
    sig = 1.0 / (1.0 + jnp.exp(-u))
    act = (u / (1.0 + jnp.exp(-u))).astype(bf16)
    f_ref[...] = act
    slope = sig * (1.0 + u * (1.0 - sig))
    r3 = h2 + (dot_nn(act, v_ref[...]) + bias_ref[8:9, :])
    n3, inv3 = norm_stats(r3)
    out_ref[...] = n3 * gain_ref[2:3, :] + bias_ref[9:10, :]
    upstream = g_ref[...].astype(f32)
    sums_ref[2:3, :] = column_sum(upstream * n3)
    sums_ref[12:13, :] = column_sum(upstream)
    gr3 = norm_back(n3, inv3, gain_ref[2:3, :], upstream)
    e3 = gr3.astype(bf16)
    e3_ref[...] = e3
    sums_ref[11:12, :] = column_sum(e3)
    gu = (dot_nt(e3, v_ref[...]) * slope).astype(bf16)
    gu_ref[...] = gu
    csum_ref[...] = column_sum(gu)
    gh2 = gr3 + dot_nt(gu, u_ref[...])
    sums_ref[1:2, :] = column_sum(gh2 * n2)
    sums_ref[10:11, :] = column_sum(gh2)
    gr2 = norm_back(n2, inv2, gain_ref[1:2, :], gh2)
    e2 = gr2.astype(bf16)
    e2_ref[...] = e2
    sums_ref[9:10, :] = column_sum(e2)
    gac = dot_nt(e2, wc_ref[4]).astype(bf16)
    sums_ref[8:9, :] = column_sum(gac)
    delta_cross = head_sums(gac.astype(f32) * attn_cross)
    grads = []
    for block in (1, 0):
        at = slice(block * half, (block + 1) * half)
        grads.append(
            attend_back(
                qc[at], gac[at], kvc_ref, dkvc_ref, rows_ref[2:3, at], rows_ref[3:4, at],
                [cross_logs[block * PAIRS + p : block * PAIRS + p + 1] for p in range(PAIRS)],
                [pair_rows(delta_cross, block, half, p) for p in range(PAIRS)],
                bounds_ref[4 + 2 * block], bounds_ref[5 + 2 * block], cross_block, factor, scale,
                dq_ref, True,
            )
        )
    dqc = jnp.concatenate([grads[1], grads[0]], axis=0).astype(bf16)
    dqc_ref[...] = dqc
    sums_ref[7:8, :] = column_sum(dqc)
    gh1 = gr2 + dot_nt(dqc, wc_ref[0])
    sums_ref[0:1, :] = column_sum(gh1 * n1)
    sums_ref[6:7, :] = column_sum(gh1)
    gr1 = norm_back(n1, inv1, gain_ref[0:1, :], gh1)
    gr1_ref[...] = gr1
    e1 = gr1.astype(bf16)
    e1_ref[...] = e1
    sums_ref[5:6, :] = column_sum(e1)
    ga = dot_nt(e1, wc_ref[3]).astype(bf16)
    ga_ref[0:rows, :] = ga
    sums_ref[4:5, :] = column_sum(ga)
    sums_ref[3:4, :] = jnp.zeros_like(sums_ref[3:4, :])
    sums_ref[13:16, :] = jnp.zeros_like(sums_ref[13:16, :])
    delta = head_sums(ga.astype(f32) * attn_self)
    delta_ref[...] = delta
    extra = split_three(side_by_side(log_ref[...])) + split_three(side_by_side(delta))
    extra.append(jnp.zeros((2 * HEADS // 2, width), bf16))
    ga_ref[rows:, :] = jnp.concatenate([e.astype(f32) for e in extra], axis=0).astype(bf16)
    pm_keep_ref[...] = jnp.zeros(pm_keep_ref.shape, bf16)
    pm_send_ref[...] = jnp.zeros(pm_send_ref.shape, bf16)
    dw_acc_ref[...] = jnp.zeros(dw_acc_ref.shape, f32)
    odd = me & 1

    def memory_step(index, carry):
        at = pl.ds(pl.multiple_of(index * cross_block, cross_block), cross_block)
        grads_block = dkvc_ref[at, :]
        pm_block_ref[...] = dot_nt(grads_block[:, :width], wc_ref[1]) + dot_nt(
            grads_block[:, width:], wc_ref[2]
        )
        pair = (me >> 1) ^ index
        slot = (pair & 1) * planes + (pair >> 1)
        mine = pl.ds(pl.multiple_of(odd * mem_rows, mem_rows), mem_rows)
        other = pl.ds(pl.multiple_of((1 - odd) * mem_rows, mem_rows), mem_rows)
        pm_keep_ref[slot] = pm_block_ref[mine, :].astype(bf16)
        pm_send_ref[slot] = pm_block_ref[other, :].astype(bf16)
        dw_acc_ref[...] += dot_tn(mem_ref[at, :], grads_block)
        return carry

    lax.fori_loop(live_first, live_last, memory_step, 0)
    dwc_ref[...] = dw_acc_ref[...].astype(bf16)


def self_backward_kernel(
    bounds_ref, x_ref, q_ref, ga_ref, gr1_ref, kv_ref, q_all_ref, log_ref, delta_ref, w_ref,
    cols_ref, sums_ref, csum_ref, *refs, factor, scale, planes, plain,
):
    pieces, refs = refs[: 2 * planes], refs[2 * planes :]
    tok_ref, refs = refs[0], refs[1:]
    sink_refs, refs = (refs[:1], refs[1:]) if plain else (refs[:2], refs[2:])
    acc_ref, dv_ref, g_all_ref, stats_ref, dw_ref = refs
    me, side = bounds_ref[12], bounds_ref[13]
    rows, width = x_ref.shape
    half = rows // 2
    count = 4 * planes
    heads = HEADS
    pad = jnp.zeros((128 - 2 * heads, rows), f32)
    stat_cols = jnp.transpose(jnp.concatenate([log_ref[...], delta_ref[...], pad], axis=0))

    def stat_column(at, first_head):
        return jnp.concatenate(
            [stat_cols[at, first_head : first_head + 1], stat_cols[at, first_head + 1 : first_head + 2]],
            axis=0,
        )

    dq_blocks = []
    for block in range(2):
        at = slice(block * half, (block + 1) * half)
        dq_blocks.append(
            query_grads(
                q_ref[at, :], ga_ref[at, :], kv_ref, cols_ref[at, 0:1], cols_ref[at, 1:2],
                [stat_column(at, 2 * p) for p in range(PAIRS)],
                [stat_column(at, heads + 2 * p) for p in range(PAIRS)],
                bounds_ref[2 * block], bounds_ref[2 * block + 1], self_block, factor, scale, acc_ref,
            )
        )
    dq = jnp.concatenate(dq_blocks, axis=0).astype(bf16)
    for r, chunk in gathered_chunks(pieces, planes):
        worker = me ^ r
        extra = chunk[rows : rows + 32, :].astype(f32)
        logs = extra[0:4] + extra[4:8] + extra[8:12]
        deltas = extra[12:16] + extra[16:20] + extra[20:24]
        for part in range(2):
            block = worker if part == 0 else 2 * count - 1 - worker
            lanes = slice(part * half, (part + 1) * half)
            high = slice(rows + part * half, rows + (part + 1) * half)
            g_all_ref[pl.ds(pl.multiple_of(block * half, half), half), :] = chunk[lanes, :]
            stats_ref[block] = jnp.concatenate(
                [logs[:, lanes], logs[:, high], deltas[:, lanes], deltas[:, high]], axis=0
            )
    dk_blocks, dv_blocks = [], []
    for block in range(2):
        at = slice(block * half, (block + 1) * half)
        index = me if block == 0 else 2 * count - 1 - me
        mine = pl.ds(pl.multiple_of(index * half, half), half)
        key_grad, value_grad = key_grads(
            kv_ref[mine, 0:width], kv_ref[mine, width:], q_all_ref, g_all_ref, stats_ref,
            cols_ref[at, 1:2], cols_ref[at, 4:5], bounds_ref[8 + 2 * block],
            bounds_ref[9 + 2 * block], factor, scale, acc_ref, dv_ref,
        )
        dk_blocks.append(key_grad)
        dv_blocks.append(value_grad)
    dk = jnp.concatenate(dk_blocks, axis=0).astype(bf16)
    dv = jnp.concatenate(dv_blocks, axis=0).astype(bf16)
    tok = gr1_ref[...] + dot_nt(dq, w_ref[0]) + dot_nt(dk, w_ref[1]) + dot_nt(dv, w_ref[2])
    tok_ref[...] = tok.astype(bf16)
    sink = PlainSink(*sink_refs) if plain else PieceSink(*sink_refs, dw_ref, me, side)
    x_rows = x_ref[...]
    sink.put(0, dot_tn(x_rows, dq))
    sink.put(1, dot_tn(x_rows, dk))
    sink.put(2, dot_tn(x_rows, dv))
    dw_ref[...] = jnp.zeros(dw_ref.shape, f32)
    sums = sums_ref[...]
    row = lax.broadcasted_iota(jnp.int32, sums.shape, 0)
    sums = jnp.where(row == 3, column_sum(dq), sums)
    fine = 2 * half_rows // 2
    piece = half_rows // count
    lanes = csum_ref.shape[1] // 8
    for yh in range(2):
        base = yh * half_rows
        dw_ref[base : base + 16, 0:lanes] = sums[:, yh * lanes : (yh + 1) * lanes]
        for k in range(4):
            start = yh * 4 * lanes + k * lanes
            dw_ref[base + 16 + k : base + 17 + k, 0:lanes] = csum_ref[:, start : start + lanes]
    if plain:
        sink.plain[3] = dw_ref[...].astype(bf16)
    else:
        sink.emit(3, half_rows, 0)


def feed_grads_kernel(bounds_ref, h2_ref, gu_ref, f_ref, e3_ref, *refs, plain):
    sink_refs, (dw_ref,) = (refs[:1], refs[1:]) if plain else (refs[:2], refs[2:])
    sink = (
        PlainSink(*sink_refs) if plain else PieceSink(*sink_refs, dw_ref, bounds_ref[12], bounds_ref[13])
    )
    width = h2_ref.shape[1]
    parts = gu_ref.shape[1] // width
    for k in range(parts):
        sink.put(k, dot_tn(h2_ref[...], gu_ref[:, k * width : (k + 1) * width]))
    sink.put(parts, dot_tn(f_ref[...], e3_ref[...]))


def map_grads_kernel(
    bounds_ref, a_ref, e1_ref, ac_ref, e2_ref, h1_ref, dqc_ref, dwc_ref, *refs, plain
):
    sink_refs, (dw_ref,) = (refs[:1], refs[1:]) if plain else (refs[:2], refs[2:])
    sink = (
        PlainSink(*sink_refs) if plain else PieceSink(*sink_refs, dw_ref, bounds_ref[12], bounds_ref[13])
    )
    width = a_ref.shape[1]
    sink.put(0, dot_tn(a_ref[...], e1_ref[...]))
    sink.put(1, dot_tn(ac_ref[...], e2_ref[...]))
    sink.put(2, dot_tn(h1_ref[...], dqc_ref[...]))
    sink.put(3, dwc_ref[:, :width])
    sink.put(4, dwc_ref[:, width:])


def call_kernel(kernel, inputs, outputs, scratch, name):
    vmem = pl.BlockSpec(memory_space=pltpu.VMEM)
    smem = pl.BlockSpec(memory_space=pltpu.SMEM)
    return pl.pallas_call(
        kernel,
        in_specs=[smem] + [vmem] * (len(inputs) - 1),
        out_specs=[vmem] * len(outputs),
        out_shape=[jax.ShapeDtypeStruct(*entry) for entry in outputs],
        scratch_shapes=[pltpu.VMEM(*entry) for entry in scratch],
        compiler_params=pltpu.CompilerParams(vmem_limit_bytes=vmem_bytes),
        name=name,
    )(*inputs)


def exchange(value, bits):
    count = lax.axis_size("ctx")
    return lax.ppermute(value, "ctx", [(i, i ^ bits) for i in range(count)])


def swap_side(value):
    return lax.ppermute(value, "fsdp", [(0, 1), (1, 0)])


def gather_pieces(value):
    planes = lax.axis_size("ctx") // 4
    from_planes = [value] + [exchange(value, 4 * s) for s in range(1, planes)]
    own = [jnp.stack([chunk, exchange(chunk, 2)]) for chunk in from_planes]
    return own + [exchange(pair, 1) for pair in own]


def in_order(bit, own, other, axis):
    return jnp.where(
        bit == 0,
        jnp.concatenate([own, other], axis=axis),
        jnp.concatenate([other, own], axis=axis),
    )


def gather_rows(shard, axis):
    if lax.axis_size("fsdp") != 2:
        return lax.all_gather(shard, "fsdp", axis=axis, tiled=True)
    core = lax.axis_index("ctx") % 2
    rows = shard.shape[axis] // 2
    part = lax.dynamic_slice_in_dim(shard, core * rows, rows, axis)
    fetched = swap_side(part)
    peer = in_order(core, fetched, exchange(fetched, 1), axis)
    return in_order(lax.axis_index("fsdp"), shard, peer, axis)


def reduce_chunks(keep, send):
    planes = keep.shape[1]
    part = keep.astype(f32) + exchange(send, 1).astype(f32)
    part = part[0] + exchange(part[1].astype(bf16), 2).astype(f32)
    low = part.astype(bf16)
    total = part[0]
    for s in range(1, planes):
        total = total + exchange(low[s], 4 * s).astype(f32)
    return total


def gather_sums(total):
    count = lax.axis_size("ctx")
    planes = count // 4
    me = lax.axis_index("ctx")
    low = total.astype(bf16)
    relative = [low] + [exchange(low, 4 * s) for s in range(1, planes)]
    plane = me // 4
    slots = []
    for target in range(planes):
        value = relative[0]
        for s in range(1, planes):
            value = jnp.where((plane ^ s) == target, relative[s], value)
        slots.append(value)
    by_plane = jnp.stack(slots)[:, None]
    by_chip = in_order((me // 2) % 2, by_plane, exchange(by_plane, 2), 1)[:, :, None]
    by_core = in_order(me % 2, by_chip, exchange(by_chip, 1), 2)
    return by_core.reshape((count,) + total.shape)


def reduce_pieces(keep, send):
    part = keep.astype(f32) + exchange(send, 1).astype(f32)
    part = part[0] + swap_side(part[1].astype(bf16)).astype(f32)
    part = part[0] + exchange(part[1].astype(bf16), 2).astype(f32)
    low = part.astype(bf16)
    total = part[0]
    for s in range(1, part.shape[0]):
        total = total + exchange(low[s], 4 * s).astype(f32)
    pieces = gather_sums(total)
    count, rows, width = pieces.shape
    piece = half_rows // count
    blocks = pieces.reshape(count, rows // piece, piece, width)
    return blocks.transpose(1, 0, 2, 3).reshape(rows // piece, half_rows, width).astype(f32)


def zigzag_perms(count):
    def worker(block):
        return block if block < count else 2 * count - 1 - block

    first = [(owner, worker(2 * owner)) for owner in range(count)]
    second = [(owner, worker(2 * owner + 1)) for owner in range(count)]
    return first, second


def body(
    tokens, memory, token_seg, memory_seg, out_grad,
    in_proj, out_proj, ffn_in, ffn_out, norm_gain, bias_rows, ffn_bias,
):
    count = lax.axis_size("ctx")
    sides = lax.axis_size("fsdp")
    planes = count // 4
    plain = sides != 2
    me = lax.axis_index("ctx")
    side = lax.axis_index("fsdp")
    row_count, width = tokens.shape[1], tokens.shape[2]
    mem_count = memory.shape[1]
    half = row_count // 2
    scale = 1.0 / math.sqrt(width // HEADS)
    factor = scale * math.log2(math.e)
    total = row_count * count
    mem_total = mem_count * count

    self_maps = gather_rows(in_proj[0:3].astype(bf16), 1)
    x_pieces = gather_pieces(tokens[0])
    small = jnp.concatenate(
        [norm_gain, bias_rows, ffn_bias.reshape(-1, norm_gain.shape[1])], axis=0
    ).astype(bf16)
    if sides == 2:
        small = jnp.stack([small, swap_side(small)])
        small = jnp.where(side == 0, small, small[::-1]).astype(f32)
    else:
        small = lax.all_gather(small, "fsdp").astype(f32)
    table = small[:, 0:13].transpose(1, 0, 2).reshape(13, width)
    gains, biases = table[0:3], table[3:13]
    ffn_shift = small[:, 13:].reshape(1, -1)

    block_a, block_b = me, 2 * count - 1 - me
    perm_first, perm_second = zigzag_perms(count)
    even = me % 2 == 0
    rows_in = jnp.stack([tokens[0], out_grad[0]])
    one = lax.ppermute(rows_in[:, :half], "ctx", perm_first)
    two = lax.ppermute(rows_in[:, half:], "ctx", perm_second)
    rows_in = jnp.where(
        even, jnp.concatenate([one, two], axis=1), jnp.concatenate([two, one], axis=1)
    )
    x_rows, g_rows = rows_in[0], rows_in[1]

    cross_maps = gather_rows(
        jnp.concatenate([in_proj[3:6], out_proj], axis=0).astype(bf16), 1
    )
    m_pieces = gather_pieces(memory[0])
    ffn_up = gather_rows(ffn_in.astype(bf16), 0)
    ffn_down = gather_rows(ffn_out.astype(bf16), 0)

    segs, mem_segs = token_seg[0], memory_seg[0]

    def own_blocks(vector):
        return jnp.concatenate(
            [
                lax.dynamic_slice_in_dim(vector, block_a * half, half),
                lax.dynamic_slice_in_dim(vector, block_b * half, half),
            ]
        )

    row_pos = own_blocks(jnp.arange(total, dtype=jnp.int32))
    row_seg = own_blocks(segs)

    def below(keys, closed):
        hits = keys[None, :] <= row_seg[:, None] if closed else keys[None, :] < row_seg[:, None]
        return jnp.sum(hits, axis=1, dtype=jnp.int32)

    low_self, end_self = below(segs, False), below(segs, True) - 1
    low_cross, end_cross = below(mem_segs, False), below(mem_segs, True) - 1
    spare = jnp.zeros_like(row_pos)
    rows_info = jnp.stack(
        [low_self, row_pos, low_cross, end_cross, end_self, spare, spare, spare]
    )
    cols_info = rows_info.T
    a0, a1, b0, b1 = 0, half - 1, half, row_count - 1
    cross_block = 2 * mem_count
    bounds = jnp.stack(
        [
            low_self[a0] // self_block, row_pos[a1] // self_block + 1,
            low_self[b0] // self_block, row_pos[b1] // self_block + 1,
            low_cross[a0] // cross_block, end_cross[a1] // cross_block + 1,
            low_cross[b0] // cross_block, end_cross[b1] // cross_block + 1,
            row_pos[a0] // self_block, end_self[a1] // self_block + 1,
            row_pos[b0] // self_block, end_self[b1] // self_block + 1,
            me, side, 0 * me, 0 * me,
        ]
    ).astype(jnp.int32)

    tile = width // PAIRS
    column = ((PAIRS, row_count, 1), f32)
    square = ((PAIRS, row_count, tile), f32)
    rows_low = ((row_count, width), bf16)
    rows_full = ((row_count, width), f32)
    q_rows, a_rows, log_rows, kv = call_kernel(
        lambda *refs: self_forward_kernel(*refs, factor=factor, planes=planes),
        (bounds, x_rows, self_maps, biases, cols_info, *x_pieces),
        (rows_low, rows_full, ((HEADS, row_count), f32), ((total, 2 * width), bf16)),
        [column, column, square],
        "self_forward",
    )
    ff_rows = ((row_count, ffn_up.shape[1]), bf16)
    part_shape = ((2 * planes, mem_count, width), bf16)
    (
        out_rows, a_low, h1_low, h2_low, act, e3, gu, e2, e1, ac_low, dqc, ga, gr1, delta,
        pm_keep, pm_send, dwc, sums, csum,
    ) = call_kernel(
        lambda *refs: middle_kernel(*refs, factor=factor, scale=scale, planes=planes),
        (
            bounds, x_rows, a_rows, g_rows, log_rows, cols_info, rows_info, gains, biases,
            ffn_shift, cross_maps, ffn_up, ffn_down, *m_pieces,
        ),
        (
            rows_full, rows_low, rows_low, rows_low, ff_rows, rows_low, ff_rows,
            rows_low, rows_low, rows_low, rows_low, ((row_count + 32, width), bf16), rows_full,
            ((HEADS, row_count), f32), part_shape, part_shape, ((width, 2 * width), bf16),
            ((16, width), f32), ((1, ffn_up.shape[1]), f32),
        ),
        [
            column, column, square, ((PAIRS, tile, row_count), f32),
            ((mem_total, width), bf16), ((mem_total, 2 * width), bf16),
            ((mem_total, 2 * width), bf16), ((width, 2 * width), f32), ((cross_block, width), f32),
        ],
        "middle",
    )
    ga_pieces = gather_pieces(ga)

    def sink_shapes(blocks):
        if plain:
            return [((blocks, width, width), bf16)]
        return [((2, 2, planes, blocks * (half_rows // count), width), bf16)] * 2

    feed = call_kernel(
        lambda *refs: feed_grads_kernel(*refs, plain=plain),
        (bounds, h2_low, gu, act, e3),
        sink_shapes(8),
        [((ffn_up.shape[1], width), f32)],
        "feed_grads",
    )
    maps = call_kernel(
        lambda *refs: map_grads_kernel(*refs, plain=plain),
        (bounds, a_low, e1, ac_low, e2, h1_low, dqc, dwc),
        sink_shapes(5),
        [((width, width), f32)],
        "map_grads",
    )
    (q_all,) = call_kernel(
        lambda *refs: project_kernel(*refs, planes=planes),
        (bounds, self_maps, biases, *x_pieces),
        (((total, width), bf16),),
        [],
        "project",
    )
    tok_rows, *last = call_kernel(
        lambda *refs: self_backward_kernel(*refs, factor=factor, scale=scale, planes=planes, plain=plain),
        (
            bounds, x_rows, q_rows, ga, gr1, kv, q_all, log_rows, delta, self_maps, cols_info,
            sums, csum, *ga_pieces,
        ),
        [rows_low] + sink_shapes(4),
        [
            square, square, ((total, width), bf16), ((2 * count, 2 * HEADS, half), f32),
            ((width, width), f32),
        ],
        "self_backward",
    )

    back_first = [(to, owner) for owner, to in perm_first]
    back_second = [(to, owner) for owner, to in perm_second]

    def give_back(rows):
        rows = rows.astype(bf16)
        half_one = jnp.where(even, rows[:half], rows[half:])
        half_two = jnp.where(even, rows[half:], rows[:half])
        return jnp.concatenate(
            [
                lax.ppermute(half_one, "ctx", back_first),
                lax.ppermute(half_two, "ctx", back_second),
            ],
            axis=0,
        ).astype(f32)

    layer_out = give_back(out_rows)
    tokens_grad = give_back(tok_rows)
    in_chips = (2, planes, mem_count, width)
    memory_grad = reduce_chunks(pm_keep.reshape(in_chips), pm_send.reshape(in_chips))

    if plain:

        def owned(matrix, axis):
            part = lax.psum_scatter(matrix, "fsdp", scatter_dimension=axis, tiled=True)
            return lax.psum(part, "ctx").astype(f32)

        feed, maps, last = feed[0], maps[0], last[0]
        ins = owned(jnp.concatenate([last[0:3], maps[2:5]], axis=0), 1)
        outs = owned(maps[0:2], 1)
        up = owned(jnp.concatenate([feed[k] for k in range(4)], axis=1), 0)
        down = owned(feed[4:8].reshape(-1, width), 0)
        lanes = width // 2
        rest = jnp.stack([last[3, 0:half_rows, 0:lanes], last[3, half_rows:, 0:lanes]], axis=1)
        table = owned(rest[0:13].reshape(13, width).astype(f32), 1)
        shift = owned(rest[16:20].transpose(1, 0, 2).reshape(-1).astype(f32), 0)
    else:
        feed = reduce_pieces(*feed)
        maps = reduce_pieces(*maps)
        last = reduce_pieces(*last)
        ins = jnp.concatenate([last[0:3], maps[2:5]], axis=0)
        outs = maps[0:2]
        up = jnp.concatenate([feed[k] for k in range(4)], axis=1)
        down = feed[4:8].reshape(-1, width)
        lanes = width // 2
        table = last[3, 0:13, 0:lanes]
        shift = last[3, 16:20, 0:lanes].reshape(-1)
    return (
        layer_out[None], tokens_grad[None], memory_grad[None], ins, outs, up, down,
        table[0:3], table[3:13], shift,
    )


def solution(mesh):
    rows = P("fsdp", "ctx", None)
    params = (
        P(None, "fsdp", None), P(None, "fsdp", None), P("fsdp", None), P("fsdp", None),
        P(None, "fsdp"), P(None, "fsdp"), P("fsdp"),
    )
    return jax.shard_map(
        body,
        mesh=mesh,
        in_specs=(rows, rows, P("fsdp", None), P("fsdp", None), rows) + params,
        out_specs=(rows, rows, rows) + params,
        check_vma=False,
    )
```

```python
import math

import jax
import jax.numpy as jnp
from jax import lax
from jax.experimental import pallas as pl
from jax.experimental.pallas import tpu as pltpu
from jax.sharding import PartitionSpec as P

HEADS = 8
PAIRS = HEADS // 2
neg_fill = -1e30
eps_norm = 1e-05
self_block = 512
bf16 = jnp.bfloat16
f32 = jnp.float32
vmem_bytes = 60 * 1024 * 1024
half_rows = 256
chunk_rows = 32


def dot_nn(first_op, second_op):
    return jnp.dot(first_op, second_op, preferred_element_type=f32)


def dot_nt(first_op, second_op):
    return lax.dot_general(
        first_op, second_op, (((1,), (1,)), ((), ())), preferred_element_type=f32
    )


def dot_tn(first_op, second_op):
    return lax.dot_general(
        first_op, second_op, (((0,), (0,)), ((), ())), preferred_element_type=f32
    )


def stack_heads(tile):
    lane = lax.broadcasted_iota(jnp.int32, tile.shape, 1)
    half = tile.shape[1] // 2
    zero = jnp.zeros_like(tile)
    return jnp.concatenate(
        [jnp.where(lane < half, tile, zero), jnp.where(lane >= half, tile, zero)], axis=0
    )


def merge_heads(stacked):
    rows = stacked.shape[0] // 2
    lane = lax.broadcasted_iota(jnp.int32, (rows, stacked.shape[1]), 1)
    return jnp.where(lane < stacked.shape[1] // 2, stacked[:rows], stacked[rows:])


def tile_of(value, pair, tile_width):
    return value[:, pair * tile_width : (pair + 1) * tile_width]


def head_sums(product):
    width = product.shape[1]
    head = lax.broadcasted_iota(jnp.int32, (HEADS, width), 0)
    lane = lax.broadcasted_iota(jnp.int32, (HEADS, width), 1)
    pick = (lane // (width // HEADS) == head).astype(f32)
    return lax.dot_general(
        pick,
        product,
        (((1,), (1,)), ((), ())),
        precision=lax.Precision.HIGHEST,
        preferred_element_type=f32,
    )


def over_range(first, last):
    def run(step):
        def visit(index, carry):
            step(index, index)
            return carry

        lax.fori_loop(first, last, visit, 0)

    return run


def over_planes(info, plane_first, plane_count, first, last):
    def run(step):
        def visit(stored, carry):
            index = 2 * (info.plane ^ (plane_first + (stored >> 1))) + (stored & 1)

            @pl.when((index >= first) & (index < last))
            def _():
                step(stored, index)

            return carry

        lax.fori_loop(0, 2 * plane_count, visit, 0)

    return run


class RowInfo:
    def __init__(self, info_ref):
        self.table = info_ref
        self.half = info_ref.shape[1] // 2
        self.me = info_ref[5, 0]
        self.side = info_ref[6, 0]
        self.plane = self.me >> 2

    def ends(self, block):
        return block * self.half, (block + 1) * self.half - 1

    def self_keys(self, block):
        start, stop = self.ends(block)
        return self.table[0, start] // self_block, self.table[1, stop] // self_block + 1

    def cross_keys(self, block, size):
        start, stop = self.ends(block)
        return self.table[2, start] // size, self.table[3, stop] // size + 1

    def queries(self, block):
        start, stop = self.ends(block)
        return self.table[1, start] // self_block, self.table[4, stop] // self_block + 1


def twice(column):
    return jnp.concatenate([column, column], axis=0)


def stacked_tiles(rows):
    tile_width = rows.shape[1] // PAIRS
    return [stack_heads(tile_of(rows, pair, tile_width)) for pair in range(PAIRS)]


def attend_plain(q_block, kv_ref, low_col, high_col, run, key_rows, factor, acc_ref):
    width = q_block.shape[1]
    tile_width = width // PAIRS
    stacked = stacked_tiles(q_block)
    low2, high2 = twice(low_col), twice(high_col)
    ones = jnp.ones((key_rows, tile_width), bf16)

    def step(stored, index):
        base = pl.multiple_of(stored * key_rows, key_rows)
        key_pos = index * key_rows + lax.broadcasted_iota(jnp.int32, (1, key_rows), 1)
        allowed = (key_pos >= low2) & (key_pos <= high2)
        for pair in range(PAIRS):
            start = pair * tile_width
            keys = kv_ref[pl.ds(base, key_rows), start : start + tile_width]
            values = kv_ref[pl.ds(base, key_rows), width + start : width + start + tile_width]
            scores = dot_nt(stacked[pair], keys)
            weights = jnp.where(allowed, jnp.exp2(scores * factor), 0.0).astype(bf16)
            acc_ref[pair] += dot_nn(weights, jnp.concatenate([values, ones], axis=1))

    run(step)


def weighted_rows(acc_ref):
    tile_width = acc_ref.shape[2] // 2
    tops = [merge_heads(acc_ref[pair, :, 0:tile_width]) for pair in range(PAIRS)]
    sums = [merge_heads(acc_ref[pair, :, tile_width:]) for pair in range(PAIRS)]
    return jnp.concatenate(tops, axis=1), jnp.concatenate(sums, axis=1)


def in_range(sums):
    return (jnp.min(sums) > 2.0**-100) & (jnp.max(sums) < 2.0**100)


def attend_running(q_block, parts, low_col, high_col, key_rows, factor, scratch):
    max_ref, sum_ref, acc_ref = scratch
    width = q_block.shape[1]
    tile_width = width // PAIRS
    stacked = stacked_tiles(q_block)
    low2, high2 = twice(low_col), twice(high_col)
    max_ref[...] = jnp.full(max_ref.shape, neg_fill, f32)
    sum_ref[...] = jnp.zeros(sum_ref.shape, f32)
    acc_ref[...] = jnp.zeros(acc_ref.shape, f32)
    for kv_ref, run in parts:

        def step(stored, index, kv_ref=kv_ref):
            base = pl.multiple_of(stored * key_rows, key_rows)
            key_pos = index * key_rows + lax.broadcasted_iota(jnp.int32, (1, key_rows), 1)
            allowed = (key_pos >= low2) & (key_pos <= high2)
            for pair in range(PAIRS):
                start = pair * tile_width
                keys = kv_ref[pl.ds(base, key_rows), start : start + tile_width]
                values = kv_ref[pl.ds(base, key_rows), width + start : width + start + tile_width]
                scores = jnp.where(allowed, dot_nt(stacked[pair], keys), neg_fill)
                old_max = max_ref[pair]
                new_max = jnp.maximum(old_max, jnp.max(scores, axis=1, keepdims=True))
                probs = jnp.exp2((scores - new_max) * factor)
                rescale = jnp.exp2((old_max - new_max) * factor)
                sum_ref[pair] = sum_ref[pair] * rescale + jnp.sum(probs, axis=1, keepdims=True)
                acc_ref[pair] = acc_ref[pair] * rescale + dot_nn(probs.astype(bf16), values)
                max_ref[pair] = new_max

        run(step)
    outputs, logs = [], []
    for pair in range(PAIRS):
        outputs.append(merge_heads(acc_ref[pair] / sum_ref[pair]))
        column = max_ref[pair] * factor + jnp.log2(sum_ref[pair])
        logs.append(merge_heads(jnp.broadcast_to(column, acc_ref.shape[1:])))
    return jnp.concatenate(outputs, axis=1), jnp.concatenate(logs, axis=1)


def log_rows_of(lane_logs):
    return head_sums(lane_logs) * (HEADS / lane_logs.shape[1])


def query_grads(
    q_block, g_block, kv_ref, low_col, high_col, log_ref, delta_ref, run, key_rows, factor, acc_ref
):
    width = q_block.shape[1]
    tile_width = width // PAIRS
    q2, g2 = stacked_tiles(q_block), stacked_tiles(g_block)
    low2, high2 = twice(low_col), twice(high_col)

    def step(stored, index):
        base = pl.multiple_of(stored * key_rows, key_rows)
        key_pos = index * key_rows + lax.broadcasted_iota(jnp.int32, (1, key_rows), 1)
        allowed = (key_pos >= low2) & (key_pos <= high2)
        for pair in range(PAIRS):
            start = pair * tile_width
            keys = kv_ref[pl.ds(base, key_rows), start : start + tile_width]
            values = kv_ref[pl.ds(base, key_rows), width + start : width + start + tile_width]
            scores = dot_nt(q2[pair], keys)
            repeats = key_rows // log_ref.shape[2]
            logs = jnp.concatenate([log_ref[pair]] * repeats, axis=1)
            deltas = jnp.concatenate([delta_ref[pair]] * repeats, axis=1)
            probs = jnp.where(allowed, jnp.exp2(scores * factor - logs), 0.0)
            prob_grad = dot_nt(g2[pair], values)
            score_grad = (probs * (prob_grad - deltas)).astype(bf16)
            acc_ref[pair] += dot_nn(score_grad, keys)

    run(step)


def key_grads(k_block, v_block, q_ref, g_ref, stats_ref, low_col, high_col, run, factor, dk_ref, dv_ref):
    width = k_block.shape[1]
    tile_width = width // PAIRS
    rows = k_block.shape[0]
    query_rows = self_block
    blocks = query_rows // rows
    k2, v2 = stacked_tiles(k_block), stacked_tiles(v_block)
    low2, high2 = twice(low_col), twice(high_col)

    def step(stored, index):
        base = pl.multiple_of(stored * query_rows, query_rows)
        q_base = pl.multiple_of(index * query_rows, query_rows)
        query_pos = q_base + lax.broadcasted_iota(jnp.int32, (1, query_rows), 1)
        allowed = (query_pos >= low2) & (query_pos <= high2)
        stats = jnp.concatenate([stats_ref[stored * blocks + u] for u in range(blocks)], axis=1)

        def two_rows(first_row):
            return jnp.concatenate(
                [
                    jnp.broadcast_to(stats[first_row : first_row + 1], (rows, query_rows)),
                    jnp.broadcast_to(stats[first_row + 1 : first_row + 2], (rows, query_rows)),
                ],
                axis=0,
            )

        for pair in range(PAIRS):
            lanes = slice(pair * tile_width, (pair + 1) * tile_width)
            queries = q_ref[pl.ds(q_base, query_rows), lanes]
            upstream = g_ref[pl.ds(base, query_rows), lanes]
            scores = dot_nt(k2[pair], queries)
            probs = jnp.where(allowed, jnp.exp2(scores * factor - two_rows(2 * pair)), 0.0)
            prob_grad = dot_nt(v2[pair], upstream)
            score_grad = (probs * (prob_grad - two_rows(HEADS + 2 * pair))).astype(bf16)
            dk_ref[pair] += dot_nn(score_grad, queries)
            dv_ref[pair] += dot_nn(probs.astype(bf16), upstream)

    run(step)


def merged_rows(acc_ref):
    return jnp.concatenate([merge_heads(acc_ref[pair]) for pair in range(PAIRS)], axis=1)


def chunk_views(piece_refs, planes):
    for s in range(planes):
        for dx in range(2):
            for dc in range(2):
                yield s, 2 * dx + dc, piece_refs[dc * planes + s].at[dx]


def fill_rows(target, parts, info, source=None):
    if len(parts) == 1:
        target[...] = parts[0][...]
        return
    own, fetched, other = parts
    rows = own.shape[-2]
    core = info.me & 1
    starts = (
        info.side * rows,
        (1 - info.side) * rows + core * (rows // 2),
        (1 - info.side) * rows + (1 - core) * (rows // 2),
    )
    for part, start, size in zip((own, fetched, other), starts, (rows, rows // 2, rows // 2)):
        at = pl.ds(pl.multiple_of(start, rows // 2), size)
        if len(target.shape) == 3:
            for k in range(target.shape[0]):
                target[k, at, :] = part[k]
        else:
            target[at, :] = part[...]


def attend_back(
    q_block, g_block, kv_ref, dkv_ref, low_row, high_row, log_rows, delta_rows,
    first, last, key_rows, factor, scale, dq_ref, adding,
):
    width = q_block.shape[1]
    tile_width = width // PAIRS
    rows = q_block.shape[0]
    q2 = [stack_heads(tile_of(q_block, pair, tile_width)) for pair in range(PAIRS)]
    g2 = [stack_heads(tile_of(g_block, pair, tile_width)) for pair in range(PAIRS)]
    low2 = jnp.concatenate([low_row, low_row], axis=1)
    high2 = jnp.concatenate([high_row, high_row], axis=1)
    dq_ref[...] = jnp.zeros(dq_ref.shape, f32)

    def step(index, carry):
        base = pl.multiple_of(index * key_rows, key_rows)
        key_pos = base + lax.broadcasted_iota(jnp.int32, (key_rows, 1), 0)
        allowed = (key_pos >= low2) & (key_pos <= high2)
        for pair in range(PAIRS):
            key_at = (pl.ds(base, key_rows), slice(pair * tile_width, (pair + 1) * tile_width))
            value_at = (
                pl.ds(base, key_rows),
                slice(width + pair * tile_width, width + (pair + 1) * tile_width),
            )
            keys = kv_ref[key_at]
            values = kv_ref[value_at]
            scores = dot_nt(keys, q2[pair])
            probs = jnp.where(allowed, jnp.exp2(scores * factor - log_rows[pair]), 0.0)
            prob_grad = dot_nt(values, g2[pair])
            score_grad = (probs * (prob_grad - delta_rows[pair])).astype(bf16)
            key_grad = dot_nn(score_grad, q2[pair]) * scale
            value_grad = dot_nn(probs.astype(bf16), g2[pair])
            if adding:
                key_grad = key_grad + dkv_ref[key_at].astype(f32)
                value_grad = value_grad + dkv_ref[value_at].astype(f32)
            dkv_ref[key_at] = key_grad.astype(bf16)
            dkv_ref[value_at] = value_grad.astype(bf16)
            dq_ref[pair] += dot_tn(keys, score_grad)
        return carry

    lax.fori_loop(first, last, step, 0)
    tiles = []
    for pair in range(PAIRS):
        both = dq_ref[pair]
        feature = lax.broadcasted_iota(jnp.int32, (tile_width, rows), 0)
        picked = jnp.where(feature < tile_width // 2, both[:, :rows], both[:, rows:])
        tiles.append(jnp.transpose(picked) * scale)
    return jnp.concatenate(tiles, axis=1)


def split_three(value):
    one = value.astype(bf16)
    rest = value - one.astype(f32)
    two = rest.astype(bf16)
    three = (rest - two.astype(f32)).astype(bf16)
    return [one, two, three]


def side_by_side(stats):
    rows = stats.shape[0] // 2
    return jnp.concatenate([stats[:rows], stats[rows:]], axis=1)


class PieceSink:
    def __init__(self, keep_ref, send_ref, scratch_ref, me, side):
        self.keep, self.send, self.scratch, self.me, self.side = keep_ref, send_ref, scratch_ref, me, side

    def emit(self, block, stride, offset):
        planes = self.keep.shape[2]
        count = 4 * planes
        piece = half_rows // count
        at = slice(block * piece, (block + 1) * piece)
        for r in range(count):
            s, dx, dc = r >> 2, (r >> 1) & 1, r & 1
            for fy in range(2):
                source = (self.side ^ fy) * stride + offset + (self.me ^ r) * piece
                rows = self.scratch[pl.ds(pl.multiple_of(source, piece), piece), :]
                target = self.send if dc else self.keep
                target[fy, dx, s, at, :] = rows.astype(bf16)

    def put(self, block, matrix):
        rows = matrix.shape[0]
        self.scratch[0:rows, :] = matrix.astype(f32)
        blocks = rows // (2 * half_rows)
        for b in range(blocks):
            self.emit(block + b, rows // 2, b * half_rows)


class PlainSink:
    def __init__(self, plain_ref):
        self.plain = plain_ref

    def put(self, block, matrix):
        size = 2 * half_rows
        for b in range(matrix.shape[0] // size):
            self.plain[block + b] = matrix[b * size : (b + 1) * size].astype(bf16)


def pair_rows(by_head, block, rows, pair):
    at = slice(block * rows, (block + 1) * rows)
    return jnp.concatenate(
        [by_head[2 * pair : 2 * pair + 1, at], by_head[2 * pair + 1 : 2 * pair + 2, at]], axis=1
    )


def norm_stats(residual):
    centre = residual - jnp.mean(residual, axis=1, keepdims=True)
    spread = jnp.mean(centre * centre, axis=1, keepdims=True)
    inverse = lax.rsqrt(spread + eps_norm)
    return centre * inverse, inverse


def norm_back(normed, inverse, gain_row, upstream):
    scaled = upstream * gain_row
    mean_one = jnp.mean(scaled, axis=1, keepdims=True)
    mean_two = jnp.mean(scaled * normed, axis=1, keepdims=True)
    return (scaled - mean_one - normed * mean_two) * inverse


def column_sum(matrix):
    return jnp.sum(matrix.astype(f32), axis=0, keepdims=True)


def project_chunks(pieces, planes, kv_ref, w_ref, shift, info):
    width = w_ref.shape[2]
    rows = pieces[0].shape[1]
    for s, bits, chunk in chunk_views(pieces, planes):
        start = 4 * rows * s + rows * ((info.me & 3) ^ bits)
        at = pl.ds(pl.multiple_of(start, rows), rows)
        block = chunk[...]
        kv_ref[at, 0:width] = dot_nn(block, w_ref[1]).astype(bf16)
        kv_ref[at, width:] = (dot_nn(block, w_ref[2]) + shift).astype(bf16)


def first_forward_kernel(info_ref, x_ref, bias_ref, cols_ref, *refs, factor, planes, shards):
    maps, refs = refs[:shards], refs[shards:]
    pieces, refs = refs[: 2 * planes], refs[2 * planes :]
    q_ref, kv_rows_ref, kv_ref, w_ref, top_ref, sums_ref, acc_ref = refs
    info = RowInfo(info_ref)
    width = x_ref.shape[1]
    half = info.half
    fill_rows(w_ref, maps, info)
    shift = bias_ref[1:2, :]
    project_chunks(pieces, planes, kv_ref, w_ref, shift, info)
    x_rows = x_ref[...]
    q_rows = (dot_nn(x_rows, w_ref[0]) + bias_ref[0:1, :]).astype(bf16)
    q_ref[...] = q_rows
    kv_rows_ref[:, 0:width] = dot_nn(x_rows, w_ref[1]).astype(bf16)
    kv_rows_ref[:, width:] = (dot_nn(x_rows, w_ref[2]) + shift).astype(bf16)
    for block in range(2):
        at = slice(block * half, (block + 1) * half)
        acc_ref[...] = jnp.zeros(acc_ref.shape, f32)
        run = over_planes(info, 0, planes, *info.self_keys(block))
        attend_plain(
            q_rows[at], kv_ref, cols_ref[at, 0:1], cols_ref[at, 1:2], run, self_block, factor, acc_ref
        )
        top_ref[at, :], sums_ref[at, :] = weighted_rows(acc_ref)


def second_forward_kernel(
    info_ref, kv_near_ref, q_in_ref, bias_ref, cols_ref, w_ref, top_ref, sums_ref, *refs,
    factor, planes,
):
    pieces, refs = refs[: 2 * planes], refs[2 * planes :]
    a_ref, log_ref, kv_ref, acc_ref, max_ref, sum_ref, run_ref, lane_ref, near_ref, near_sem = refs
    info = RowInfo(info_ref)
    half = info.half
    project_chunks(pieces, planes, kv_ref, w_ref, bias_ref[1:2, :], info)
    fine = None
    for block in range(2):
        at = slice(block * half, (block + 1) * half)
        acc_ref[...] = jnp.zeros(acc_ref.shape, f32)
        run = over_planes(info, planes, planes, *info.self_keys(block))
        attend_plain(
            q_in_ref[at, :], kv_ref, cols_ref[at, 0:1], cols_ref[at, 1:2], run, self_block, factor,
            acc_ref,
        )
        top, sums = weighted_rows(acc_ref)
        sums = sums + sums_ref[at, :]
        a_ref[at, :] = (top + top_ref[at, :]) / sums
        lane_ref[at, :] = jnp.log2(sums)
        fine = in_range(sums) if fine is None else fine & in_range(sums)

    @pl.when(jnp.logical_not(fine))
    def _():
        copy = pltpu.make_async_copy(kv_near_ref, near_ref, near_sem)
        copy.start()
        copy.wait()
        for block in range(2):
            at = slice(block * half, (block + 1) * half)
            keys = info.self_keys(block)
            a_ref[at, :], lane_ref[at, :] = attend_running(
                q_in_ref[at, :],
                [
                    (near_ref, over_planes(info, 0, planes, *keys)),
                    (kv_ref, over_planes(info, planes, planes, *keys)),
                ],
                cols_ref[at, 0:1], cols_ref[at, 1:2], self_block, factor, (max_ref, sum_ref, run_ref),
            )

    log_ref[...] = log_rows_of(lane_ref[...])


def project_kernel(info_ref, w_ref, bias_ref, *refs, planes):
    pieces, (q_ref,) = refs[: 2 * planes], refs[2 * planes :]
    info = RowInfo(info_ref)
    for s, bits, chunk in chunk_views(pieces, planes):
        rows = chunk.shape[0]
        at = pl.ds(pl.multiple_of((info.me ^ (4 * s + bits)) * rows, rows), rows)
        q_ref[at, :] = (dot_nn(chunk[...], w_ref[0]) + bias_ref[0:1, :]).astype(bf16)


def middle_forward_kernel(
    info_ref, x_ref, a_ref, g_ref, cols_ref, gain_ref, bias_ref, ffn_bias_ref, mem_ref, *refs,
    factor, shards, cross_rows,
):
    maps, refs = refs[:shards], refs[shards:]
    up, refs = refs[:shards], refs[shards:]
    down, refs = refs[:shards], refs[shards:]
    (
        out_ref, a_low_ref, h1_ref, h2_ref, f_ref, e3_ref, gu_ref, e2_ref, ac_ref, gr2_ref, r1_ref,
        qc_ref, cross_ref, cross_log_ref, kvc_ref, sums_ref, csum_ref, wc_ref,
        acc_ref, max_ref, sum_ref, run_ref, lane_ref, *whole_refs,
    ) = refs
    info = RowInfo(info_ref)
    fill_rows(wc_ref, maps, info)
    if shards == 1:
        u_ref, v_ref = up[0], down[0]
    else:
        u_ref, v_ref = whole_refs
        fill_rows(u_ref, up, info)
        fill_rows(v_ref, down, info)
    rows, width = x_ref.shape
    half = rows // 2
    cross_block = cross_rows
    cross_range = [info.cross_keys(block, cross_block) for block in range(2)]
    live_first = jnp.minimum(cross_range[0][0], cross_range[1][0])
    live_last = jnp.maximum(cross_range[0][1], cross_range[1][1])

    def project(index, carry):
        at = pl.ds(pl.multiple_of(index * cross_block, cross_block), cross_block)
        block = mem_ref[at, :]
        kvc_ref[at, 0:width] = dot_nn(block, wc_ref[1]).astype(bf16)
        kvc_ref[at, width:] = (dot_nn(block, wc_ref[2]) + bias_ref[5:6, :]).astype(bf16)
        return carry

    lax.fori_loop(live_first, live_last, project, 0)
    attn_self = a_ref[...]
    a_low = attn_self.astype(bf16)
    a_low_ref[...] = a_low
    r1 = x_ref[...].astype(f32) + (dot_nn(a_low, wc_ref[3]) + bias_ref[2:3, :])
    r1_ref[...] = r1
    n1, inv1 = norm_stats(r1)
    h1 = n1 * gain_ref[0:1, :] + bias_ref[3:4, :]
    h1_low = h1.astype(bf16)
    h1_ref[...] = h1_low
    qc = (dot_nn(h1_low, wc_ref[0]) + bias_ref[4:5, :]).astype(bf16)
    qc_ref[...] = qc
    fine = None
    for block in range(2):
        at = slice(block * half, (block + 1) * half)
        acc_ref[...] = jnp.zeros(acc_ref.shape, f32)
        attend_plain(
            qc[at], kvc_ref, cols_ref[at, 2:3], cols_ref[at, 3:4], over_range(*cross_range[block]),
            cross_block, factor, acc_ref,
        )
        top, weights = weighted_rows(acc_ref)
        cross_ref[at, :] = top / weights
        lane_ref[at, :] = jnp.log2(weights)
        fine = in_range(weights) if fine is None else fine & in_range(weights)

    @pl.when(jnp.logical_not(fine))
    def _():
        for block in range(2):
            at = slice(block * half, (block + 1) * half)
            cross_ref[at, :], lane_ref[at, :] = attend_running(
                qc_ref[at, :], [(kvc_ref, over_range(*cross_range[block]))],
                cols_ref[at, 2:3], cols_ref[at, 3:4], cross_block, factor, (max_ref, sum_ref, run_ref),
            )

    cross_log_ref[...] = log_rows_of(lane_ref[...])
    attn_cross = cross_ref[...]
    ac_low = attn_cross.astype(bf16)
    ac_ref[...] = ac_low
    r2 = h1 + (dot_nn(ac_low, wc_ref[4]) + bias_ref[6:7, :])
    n2, inv2 = norm_stats(r2)
    h2 = n2 * gain_ref[1:2, :] + bias_ref[7:8, :]
    h2_low = h2.astype(bf16)
    h2_ref[...] = h2_low
    u = dot_nn(h2_low, u_ref[...]) + ffn_bias_ref[...]
    sig = 1.0 / (1.0 + jnp.exp(-u))
    act = (u / (1.0 + jnp.exp(-u))).astype(bf16)
    f_ref[...] = act
    slope = sig * (1.0 + u * (1.0 - sig))
    r3 = h2 + (dot_nn(act, v_ref[...]) + bias_ref[8:9, :])
    n3, inv3 = norm_stats(r3)
    out_ref[...] = n3 * gain_ref[2:3, :] + bias_ref[9:10, :]
    sums_ref[...] = jnp.zeros_like(sums_ref)
    upstream = g_ref[...].astype(f32)
    sums_ref[2:3, :] = column_sum(upstream * n3)
    sums_ref[12:13, :] = column_sum(upstream)
    gr3 = norm_back(n3, inv3, gain_ref[2:3, :], upstream)
    e3 = gr3.astype(bf16)
    e3_ref[...] = e3
    sums_ref[11:12, :] = column_sum(e3)
    gu = (dot_nt(e3, v_ref[...]) * slope).astype(bf16)
    gu_ref[...] = gu
    csum_ref[...] = column_sum(gu)
    gh2 = gr3 + dot_nt(gu, u_ref[...])
    sums_ref[1:2, :] = column_sum(gh2 * n2)
    sums_ref[10:11, :] = column_sum(gh2)
    gr2 = norm_back(n2, inv2, gain_ref[1:2, :], gh2)
    gr2_ref[...] = gr2
    e2 = gr2.astype(bf16)
    e2_ref[...] = e2
    sums_ref[9:10, :] = column_sum(e2)


def middle_backward_kernel(
    info_ref, a_ref, log_ref, rows_ref, gain_ref, mem_ref, wc_ref, e2_ref, gr2_ref, r1_ref, qc_ref,
    cross_ref, cross_log_ref, kvc_ref, sums_in_ref,
    e1_ref, dqc_ref, ga_ref, gr1_ref, delta_ref, pm_keep_ref, pm_send_ref, dwc_ref, sums_ref,
    dq_ref, dkvc_ref, dw_acc_ref, pm_block_ref, *, factor, scale, planes,
):
    info = RowInfo(info_ref)
    me = info.me
    rows, width = a_ref.shape
    half = rows // 2
    mem_rows = pm_keep_ref.shape[1]
    cross_block = 2 * mem_rows
    cross_range = [info.cross_keys(block, cross_block) for block in range(2)]
    live_first = jnp.minimum(cross_range[0][0], cross_range[1][0])
    live_last = jnp.maximum(cross_range[0][1], cross_range[1][1])
    sums_ref[...] = sums_in_ref[...]
    n1, inv1 = norm_stats(r1_ref[...])
    attn_self, attn_cross = a_ref[...], cross_ref[...]
    gr2, e2, qc, cross_logs = gr2_ref[...], e2_ref[...], qc_ref[...], cross_log_ref[...]

    def clear(index, carry):
        at = pl.ds(pl.multiple_of(index * cross_block, cross_block), cross_block)
        dkvc_ref[at, :] = jnp.zeros((cross_block, 2 * width), bf16)
        return carry

    lax.fori_loop(live_first, live_last, clear, 0)
    gac = dot_nt(e2, wc_ref[4]).astype(bf16)
    sums_ref[8:9, :] = column_sum(gac)
    delta_cross = head_sums(gac.astype(f32) * attn_cross)
    grads = []
    for block in (1, 0):
        at = slice(block * half, (block + 1) * half)
        grads.append(
            attend_back(
                qc[at], gac[at], kvc_ref, dkvc_ref, rows_ref[2:3, at], rows_ref[3:4, at],
                [pair_rows(cross_logs, block, half, p) for p in range(PAIRS)],
                [pair_rows(delta_cross, block, half, p) for p in range(PAIRS)],
                *cross_range[block], cross_block, factor, scale,
                dq_ref, True,
            )
        )
    dqc = jnp.concatenate([grads[1], grads[0]], axis=0).astype(bf16)
    dqc_ref[...] = dqc
    sums_ref[7:8, :] = column_sum(dqc)
    gh1 = gr2 + dot_nt(dqc, wc_ref[0])
    sums_ref[0:1, :] = column_sum(gh1 * n1)
    sums_ref[6:7, :] = column_sum(gh1)
    gr1 = norm_back(n1, inv1, gain_ref[0:1, :], gh1)
    gr1_ref[...] = gr1
    e1 = gr1.astype(bf16)
    e1_ref[...] = e1
    sums_ref[5:6, :] = column_sum(e1)
    ga = dot_nt(e1, wc_ref[3]).astype(bf16)
    ga_ref[0:rows, :] = ga
    sums_ref[4:5, :] = column_sum(ga)
    delta = head_sums(ga.astype(f32) * attn_self)
    delta_ref[...] = delta
    extra = split_three(side_by_side(log_ref[...])) + split_three(side_by_side(delta))
    extra.append(jnp.zeros((2 * HEADS // 2, width), bf16))
    ga_ref[rows:, :] = jnp.concatenate([e.astype(f32) for e in extra], axis=0).astype(bf16)
    pm_keep_ref[...] = jnp.zeros(pm_keep_ref.shape, bf16)
    pm_send_ref[...] = jnp.zeros(pm_send_ref.shape, bf16)
    dw_acc_ref[...] = jnp.zeros(dw_acc_ref.shape, f32)
    odd = me & 1

    def memory_step(index, carry):
        at = pl.ds(pl.multiple_of(index * cross_block, cross_block), cross_block)
        grads_block = dkvc_ref[at, :]
        pm_block_ref[...] = dot_nt(grads_block[:, :width], wc_ref[1]) + dot_nt(
            grads_block[:, width:], wc_ref[2]
        )
        pair = (me >> 1) ^ index
        slot = (pair & 1) * planes + (pair >> 1)
        mine = pl.ds(pl.multiple_of(odd * mem_rows, mem_rows), mem_rows)
        other = pl.ds(pl.multiple_of((1 - odd) * mem_rows, mem_rows), mem_rows)
        pm_keep_ref[slot] = pm_block_ref[mine, :].astype(bf16)
        pm_send_ref[slot] = pm_block_ref[other, :].astype(bf16)
        dw_acc_ref[...] += dot_tn(mem_ref[at, :], grads_block)
        return carry

    lax.fori_loop(live_first, live_last, memory_step, 0)
    dwc_ref[...] = dw_acc_ref[...].astype(bf16)


def query_backward_kernel(
    info_ref, q_ref, ga_ref, kv_one_ref, kv_two_ref, log_ref, delta_ref, cols_ref, dq_ref, acc_ref,
    log_rep_ref, delta_rep_ref, *, factor, scale, planes,
):
    info = RowInfo(info_ref)
    rows = q_ref.shape[0]
    half = info.half
    pad = jnp.zeros((128 - 2 * HEADS, rows), f32)
    stat_cols = jnp.transpose(jnp.concatenate([log_ref[...], delta_ref[...], pad], axis=0))

    def stat_column(at, head):
        return jnp.concatenate(
            [stat_cols[at, head : head + 1], stat_cols[at, head + 1 : head + 2]], axis=0
        )

    for block in range(2):
        at = slice(block * half, (block + 1) * half)
        acc_ref[...] = jnp.zeros(acc_ref.shape, f32)
        for p in range(PAIRS):
            log_rep_ref[p] = jnp.broadcast_to(stat_column(at, 2 * p), log_rep_ref.shape[1:])
            delta_rep_ref[p] = jnp.broadcast_to(stat_column(at, HEADS + 2 * p), log_rep_ref.shape[1:])
        for part, kv_ref in enumerate((kv_one_ref, kv_two_ref)):
            query_grads(
                q_ref[at, :], ga_ref[at, :], kv_ref, cols_ref[at, 0:1], cols_ref[at, 1:2],
                log_rep_ref, delta_rep_ref,
                over_planes(info, part * planes, planes, *info.self_keys(block)),
                self_block, factor, acc_ref,
            )
        dq_ref[at, :] = (merged_rows(acc_ref) * scale).astype(bf16)


def key_backward_kernel(
    info_ref, kv_rows_ref, q_all_ref, cols_ref, *refs, factor, scale, planes, part, last,
    plain, total_planes,
):
    state_in, refs = (refs[:2], refs[2:]) if part else ((), refs)
    if last:
        (x_ref, gr1_ref, dq_ref, w_ref), refs = refs[:4], refs[4:]
    pieces, refs = refs[: 2 * planes], refs[2 * planes :]
    if last:
        tok_ref, refs = refs[0], refs[1:]
        sink_refs, refs = (refs[:1], refs[1:]) if plain else (refs[:2], refs[2:])
    if last:
        g_ref, stats_ref, dk_ref, dv_ref, dw_ref = refs
    else:
        dk_ref, dv_ref, g_ref, stats_ref = refs
    info = RowInfo(info_ref)
    half = info.half
    rows = 2 * half
    width = q_all_ref.shape[1]
    for s, bits, chunk in chunk_views(pieces, planes):
        place = (info.me & 3) ^ bits
        extra = chunk[rows : rows + chunk_rows, :].astype(f32)
        logs = extra[0:4] + extra[4:8] + extra[8:12]
        deltas = extra[12:16] + extra[16:20] + extra[20:24]
        for side in range(2):
            block = 8 * s + 4 * side + (place if side == 0 else 3 - place)
            lanes = slice(side * half, (side + 1) * half)
            high = slice(rows + side * half, rows + (side + 1) * half)
            g_ref[pl.ds(pl.multiple_of(block * half, half), half), :] = chunk[lanes, :]
            stats_ref[block] = jnp.concatenate(
                [logs[:, lanes], logs[:, high], deltas[:, lanes], deltas[:, high]], axis=0
            )

    def groups(first, stop):
        def run(step):
            def visit(stored, carry):
                plane = info.plane ^ (part * planes + (stored >> 1))
                index = jnp.where((stored & 1) == 0, plane, 2 * total_planes - 1 - plane)

                @pl.when((index >= first) & (index < stop))
                def _():
                    step(stored, index)

                return carry

            lax.fori_loop(0, 2 * planes, visit, 0)

        return run

    for block in range(2):
        at = slice(block * half, (block + 1) * half)
        if part:
            dk_ref[block] = state_in[0][block]
            dv_ref[block] = state_in[1][block]
        else:
            dk_ref[block] = jnp.zeros(dk_ref.shape[1:], f32)
            dv_ref[block] = jnp.zeros(dv_ref.shape[1:], f32)
        key_grads(
            kv_rows_ref[at, 0:width], kv_rows_ref[at, width:], q_all_ref, g_ref, stats_ref,
            cols_ref[at, 1:2], cols_ref[at, 4:5], groups(*info.queries(block)), factor,
            dk_ref.at[block], dv_ref.at[block],
        )
    if not last:
        return
    dk = jnp.concatenate([merged_rows(dk_ref.at[b]) for b in range(2)], axis=0) * scale
    dv = jnp.concatenate([merged_rows(dv_ref.at[b]) for b in range(2)], axis=0)
    dk, dv = dk.astype(bf16), dv.astype(bf16)
    tok = gr1_ref[...] + dot_nt(dq_ref[...], w_ref[0]) + dot_nt(dk, w_ref[1]) + dot_nt(dv, w_ref[2])
    tok_ref[...] = tok.astype(bf16)
    sink = PlainSink(*sink_refs) if plain else PieceSink(*sink_refs, dw_ref, info.me, info.side)
    x_rows = x_ref[...]
    sink.put(0, dot_tn(x_rows, dk))
    sink.put(1, dot_tn(x_rows, dv))


def feed_grads_kernel(info_ref, h2_ref, gu_ref, f_ref, e3_ref, *refs, plain):
    sink_refs, (dw_ref,) = (refs[:1], refs[1:]) if plain else (refs[:2], refs[2:])
    info = RowInfo(info_ref)
    sink = PlainSink(*sink_refs) if plain else PieceSink(*sink_refs, dw_ref, info.me, info.side)
    width = h2_ref.shape[1]
    parts = gu_ref.shape[1] // width
    for k in range(parts):
        sink.put(k, dot_tn(h2_ref[...], gu_ref[:, k * width : (k + 1) * width]))
    sink.put(parts, dot_tn(f_ref[...], e3_ref[...]))


def map_grads_kernel(
    info_ref, a_ref, e1_ref, ac_ref, e2_ref, h1_ref, dqc_ref, dwc_ref, x_ref, dq_ref, sums_ref,
    csum_ref, *refs, plain,
):
    sink_refs, (dw_ref,) = (refs[:1], refs[1:]) if plain else (refs[:2], refs[2:])
    info = RowInfo(info_ref)
    sink = PlainSink(*sink_refs) if plain else PieceSink(*sink_refs, dw_ref, info.me, info.side)
    width = a_ref.shape[1]
    sink.put(0, dot_tn(a_ref[...], e1_ref[...]))
    sink.put(1, dot_tn(ac_ref[...], e2_ref[...]))
    sink.put(2, dot_tn(h1_ref[...], dqc_ref[...]))
    sink.put(3, dwc_ref[:, :width])
    sink.put(4, dwc_ref[:, width:])
    sink.put(5, dot_tn(x_ref[...], dq_ref[...]))
    dw_ref[...] = jnp.zeros(dw_ref.shape, f32)
    sums = sums_ref[...]
    row = lax.broadcasted_iota(jnp.int32, sums.shape, 0)
    sums = jnp.where(row == 3, column_sum(dq_ref[...]), sums)
    lanes = csum_ref.shape[1] // 8
    for yh in range(2):
        base = yh * half_rows
        dw_ref[base : base + 16, 0:lanes] = sums[:, yh * lanes : (yh + 1) * lanes]
        for k in range(4):
            start = yh * 4 * lanes + k * lanes
            dw_ref[base + 16 + k : base + 17 + k, 0:lanes] = csum_ref[:, start : start + lanes]
    if plain:
        sink.plain[6] = dw_ref[...].astype(bf16)
    else:
        sink.emit(6, half_rows, 0)


def call_kernel(kernel, inputs, outputs, scratch, name, micros, in_place=()):
    vmem = pl.BlockSpec(memory_space=pltpu.VMEM)
    smem = pl.BlockSpec(memory_space=pltpu.SMEM)
    return pl.pallas_call(
        kernel,
        in_specs=[smem]
        + [
            pl.BlockSpec(memory_space=pl.ANY) if index in in_place else vmem
            for index in range(1, len(inputs))
        ],
        out_specs=[vmem] * len(outputs),
        out_shape=[jax.ShapeDtypeStruct(*entry) for entry in outputs],
        scratch_shapes=[pltpu.VMEM(*entry) if isinstance(entry, tuple) else entry for entry in scratch],
        compiler_params=pltpu.CompilerParams(vmem_limit_bytes=vmem_bytes),
        cost_estimate=pl.CostEstimate(
            flops=int(micros * 1e9), transcendentals=0, bytes_accessed=int(micros * 1e5)
        ),
        name=name,
    )(*inputs)


def exchange(value, bits):
    count = lax.axis_size("ctx")
    return lax.ppermute(value, "ctx", [(i, i ^ bits) for i in range(count)])


def swap_side(value):
    return lax.ppermute(value, "fsdp", [(0, 1), (1, 0)])


def after(value, *others):
    return lax.optimization_barrier((value,) + others)[0]


def fetch_planes(value):
    planes = lax.axis_size("ctx") // 4
    return [value] + [exchange(value, 4 * s) for s in range(1, planes)]


def fetch_chips(chunks):
    return [jnp.stack([chunk, exchange(chunk, 2)]) for chunk in chunks]


def fetch_cores(pairs):
    return pairs + [exchange(pair, 1) for pair in pairs]


def in_order(bit, own, other, axis):
    return jnp.where(
        bit == 0,
        jnp.concatenate([own, other], axis=axis),
        jnp.concatenate([other, own], axis=axis),
    )


def core_part(shard, axis):
    rows = shard.shape[axis] // 2
    return lax.dynamic_slice_in_dim(shard, (lax.axis_index("ctx") % 2) * rows, rows, axis)


def gather_sums(total):
    count = lax.axis_size("ctx")
    planes = count // 4
    me = lax.axis_index("ctx")
    low = total.astype(bf16)
    relative = [low] + [exchange(low, 4 * s) for s in range(1, planes)]
    plane = me // 4
    slots = []
    for target in range(planes):
        value = relative[0]
        for s in range(1, planes):
            value = jnp.where((plane ^ s) == target, relative[s], value)
        slots.append(value)
    by_plane = jnp.stack(slots)[:, None]
    by_chip = in_order((me // 2) % 2, by_plane, exchange(by_plane, 2), 1)[:, :, None]
    by_core = in_order(me % 2, by_chip, exchange(by_chip, 1), 2)
    return by_core.reshape((count,) + total.shape)


def add_cores(keep, send):
    other = exchange(send, 1)
    return keep[0].astype(f32) + other[0].astype(f32), (
        keep[1].astype(f32) + other[1].astype(f32)
    ).astype(bf16)


def add_sides(kept, sent):
    part = kept + swap_side(sent).astype(f32)
    return part[0], part[1].astype(bf16)


def add_chips(kept, sent):
    return kept + exchange(sent, 2).astype(f32)


def add_planes(part, low=None):
    low = part.astype(bf16) if low is None else low
    total = part[0]
    for s in range(1, part.shape[0]):
        total = total + exchange(low[s], 4 * s).astype(f32)
    return total


def spread(total):
    pieces = gather_sums(total)
    count, rows, width = pieces.shape
    piece = half_rows // count
    blocks = pieces.reshape(count, rows // piece, piece, width)
    return blocks.transpose(1, 0, 2, 3).reshape(rows // piece, half_rows, width).astype(f32)


def zigzag_perms(count):
    def worker(block):
        return block if block < count else 2 * count - 1 - block

    first = [(owner, worker(2 * owner)) for owner in range(count)]
    second = [(owner, worker(2 * owner + 1)) for owner in range(count)]
    return first, second


def body(
    tokens, memory, token_seg, memory_seg, out_grad,
    in_proj, out_proj, ffn_in, ffn_out, norm_gain, bias_rows, ffn_bias,
):
    count = lax.axis_size("ctx")
    sides = lax.axis_size("fsdp")
    planes = count // 4
    plain = sides != 2
    me = lax.axis_index("ctx")
    side = lax.axis_index("fsdp")
    row_count, width = tokens.shape[1], tokens.shape[2]
    mem_count = memory.shape[1]
    half = row_count // 2
    scale = 1.0 / math.sqrt(width // HEADS)
    factor = scale * math.log2(math.e)
    total = row_count * count
    mem_total = mem_count * count
    near, far = planes // 2, planes - planes // 2

    x_planes = fetch_planes(tokens[0])
    self_low = in_proj[0:3].astype(bf16)
    if plain:
        self_maps = (lax.all_gather(self_low, "fsdp", axis=1, tiled=True),)
    else:
        fetched = swap_side(core_part(self_low, 1))
        self_maps = (self_low, fetched, exchange(fetched, 1))
    x_pairs = fetch_chips(x_planes)
    x_pieces = fetch_cores(x_pairs)

    perm_first, perm_second = zigzag_perms(count)
    even = me % 2 == 0
    rows_in = jnp.stack([tokens[0], out_grad[0]])
    one = lax.ppermute(rows_in[:, :half], "ctx", perm_first)
    two = lax.ppermute(rows_in[:, half:], "ctx", perm_second)
    rows_in = jnp.where(
        even, jnp.concatenate([one, two], axis=1), jnp.concatenate([two, one], axis=1)
    )
    x_rows, g_rows = rows_in[0], rows_in[1]

    small = jnp.concatenate(
        [norm_gain, bias_rows, ffn_bias.reshape(-1, norm_gain.shape[1])], axis=0
    ).astype(bf16)
    if plain:
        small = lax.all_gather(small, "fsdp").astype(f32)
    else:
        small = jnp.stack([small, swap_side(small)])
        small = jnp.where(side == 0, small, small[::-1]).astype(f32)
    table = small[:, 0:13].transpose(1, 0, 2).reshape(13, width)
    gains, biases = table[0:3], table[3:13]
    ffn_shift = small[:, 13:].reshape(1, -1)

    up_low, down_low = ffn_in.astype(bf16), ffn_out.astype(bf16)
    cross_low = jnp.concatenate([in_proj[3:6], out_proj], axis=0).astype(bf16)
    if plain:
        late_maps = (
            lax.all_gather(cross_low, "fsdp", axis=1, tiled=True),
            lax.all_gather(up_low, "fsdp", axis=0, tiled=True),
            lax.all_gather(down_low, "fsdp", axis=0, tiled=True),
        )
    else:
        cross_part = core_part(cross_low, 1)
        sent = jnp.concatenate([cross_part.reshape(-1, width), core_part(down_low, 0)], axis=0)
        fetched_one = swap_side(after(sent, fetched))
        fetched_two = swap_side(after(core_part(up_low, 0), fetched))
        other_one, other_two = exchange(fetched_one, 1), exchange(fetched_two, 1)
        cut = cross_part.shape[0] * cross_part.shape[1]

        def as_maps(matrix):
            return matrix[:cut].reshape(cross_part.shape)

        late_maps = (
            cross_low, as_maps(fetched_one), as_maps(other_one), up_low, fetched_two, other_two,
            down_low, fetched_one[cut:], other_one[cut:],
        )
    m_all = lax.all_gather(after(memory[0], *x_planes[1:]), "ctx", axis=0, tiled=True)

    segs, mem_segs = token_seg[0], memory_seg[0]
    step = jnp.arange(half, dtype=jnp.int32)
    row_pos = jnp.concatenate([me * half + step, (2 * count - 1 - me) * half + step])
    row_seg = jnp.concatenate(
        [
            lax.dynamic_slice_in_dim(segs, me * half, half),
            lax.dynamic_slice_in_dim(segs, (2 * count - 1 - me) * half, half),
        ]
    )

    def below(keys, closed):
        hits = keys[None, :] <= row_seg[:, None] if closed else keys[None, :] < row_seg[:, None]
        return jnp.sum(hits, axis=1, dtype=jnp.int32)

    ones = jnp.ones_like(row_pos)
    info = jnp.stack(
        [
            below(segs, False), row_pos, below(mem_segs, False), below(mem_segs, True) - 1,
            below(segs, True) - 1, me * ones, side * ones, ones,
        ]
    )
    cols = info.T

    tile = width // PAIRS
    column = ((PAIRS, row_count, 1), f32)
    square = ((PAIRS, row_count, tile), f32)
    two_squares = ((2, PAIRS, row_count, tile), f32)
    rows_low = ((row_count, width), bf16)
    rows_full = ((row_count, width), f32)
    kv_rows_shape = ((row_count, 2 * width), bf16)

    def halves(pieces):
        own, other = pieces[:planes], pieces[planes:]
        return own[:near] + other[:near], own[near:] + other[near:]

    x_near, x_far = halves(x_pieces)
    wide = ((PAIRS, row_count, 2 * tile), f32)
    q_rows, kv_rows, kv_near, w_self, top, weights = call_kernel(
        lambda *refs: first_forward_kernel(
            *refs, factor=factor, planes=near, shards=len(self_maps)
        ),
        (info, x_rows, biases, cols, *self_maps, *x_near),
        (
            rows_low, kv_rows_shape, ((4 * near * row_count, 2 * width), bf16),
            ((3, width, width), bf16), rows_full, rows_full,
        ),
        [wide],
        "first_forward",
        10,
    )
    a_rows, log_rows, kv_far = call_kernel(
        lambda *refs: second_forward_kernel(*refs, factor=factor, planes=far),
        (info, kv_near, q_rows, biases, cols, w_self, top, weights, *x_far),
        (rows_full, ((HEADS, row_count), f32), ((4 * far * row_count, 2 * width), bf16)),
        [
            wide, column, column, square, rows_full, ((4 * near * row_count, 2 * width), bf16),
            pltpu.SemaphoreType.DMA,
        ],
        "second_forward",
        10,
        (1,),
    )
    ff_width = ffn_in.shape[1]
    ff_rows = ((row_count, ff_width), bf16)
    part_shape = ((2 * planes, mem_count, width), bf16)
    by_head = ((HEADS, row_count), f32)
    kvc_shape = ((mem_total, 2 * width), bf16)
    sums_shape = ((16, width), f32)
    whole_maps = [] if plain else [((width, ff_width), bf16), ((ff_width, width), bf16)]
    (
        out_rows, a_low, h1_low, h2_low, act, e3, gu, e2, ac_low, gr2, r1, qc, cross, cross_log,
        kvc, sums, csum, w_cross,
    ) = call_kernel(
        lambda *refs: middle_forward_kernel(
            *refs, factor=factor, shards=len(self_maps), cross_rows=2 * mem_count
        ),
        (info, x_rows, a_rows, g_rows, cols, gains, biases, ffn_shift, m_all, *late_maps),
        (
            rows_full, rows_low, rows_low, rows_low, ff_rows, rows_low, ff_rows, rows_low, rows_low,
            rows_full, rows_full, rows_low, rows_full, by_head, kvc_shape, sums_shape,
            ((1, ff_width), f32), ((5, width, width), bf16),
        ),
        [wide, column, column, square, rows_full, *whole_maps],
        "middle_forward",
        25,
    )

    def sink_shapes(blocks):
        if plain:
            return [((blocks, width, width), bf16)]
        return [((2, 2, planes, blocks * (half_rows // count), width), bf16)] * 2

    feed = call_kernel(
        lambda *refs: feed_grads_kernel(*refs, plain=plain),
        (info, h2_low, gu, act, e3),
        sink_shapes(8),
        [((ff_width, width), f32)],
        "feed_grads",
        5,
    )
    gr2 = after(gr2, *feed)
    e1, dqc, ga, gr1, delta, pm_keep, pm_send, dwc, sums = call_kernel(
        lambda *refs: middle_backward_kernel(*refs, factor=factor, scale=scale, planes=planes),
        (
            info, a_rows, log_rows, info, gains, m_all, w_cross, e2, gr2, r1, qc, cross, cross_log,
            kvc, sums,
        ),
        (
            rows_low, rows_low, ((row_count + chunk_rows, width), bf16), rows_full, by_head,
            part_shape, part_shape, ((width, 2 * width), bf16), sums_shape,
        ),
        [
            ((PAIRS, tile, row_count), f32), kvc_shape, ((width, 2 * width), f32),
            ((2 * mem_count, width), f32),
        ],
        "middle_backward",
        16,
    )
    g_planes = fetch_planes(ga)
    g_pairs = fetch_chips(g_planes)
    g_pieces = fetch_cores(g_pairs)
    if not plain:
        feed = add_cores(*feed)
        q_rows = after(q_rows, feed[1])
    (dq,) = call_kernel(
        lambda *refs: query_backward_kernel(*refs, factor=factor, scale=scale, planes=near),
        (info, q_rows, ga, kv_near, kv_far, log_rows, delta, cols),
        (rows_low,),
        [square, square, square],
        "query_backward",
        15,
    )
    h1_low = after(h1_low, *g_planes[1:])
    maps = call_kernel(
        lambda *refs: map_grads_kernel(*refs, plain=plain),
        (info, a_low, e1, ac_low, e2, h1_low, dqc, dwc, x_rows, dq, sums, csum),
        sink_shapes(7),
        [((width, width), f32)],
        "map_grads",
        5,
    )
    (q_all,) = call_kernel(
        lambda *refs: project_kernel(*refs, planes=planes),
        (info, w_self, biases, *x_pieces),
        (((total, width), bf16),),
        [],
        "project",
        7,
    )
    in_chips = (2, planes, mem_count, width)
    mem_part = pm_keep.reshape(in_chips).astype(f32) + exchange(pm_send, 1).reshape(in_chips).astype(f32)
    if plain:
        chips = (mem_part[0], mem_part[1].astype(bf16))
    else:
        maps = add_cores(*maps)
        feed = add_sides(*feed)
        chips = (
            jnp.concatenate([feed[0], mem_part[0]], axis=1),
            jnp.concatenate([feed[1], mem_part[1].astype(bf16)], axis=1),
        )
        kv_rows = after(kv_rows, chips[1], maps[1])
    g_near, g_far = halves(g_pieces)
    dk_part, dv_part = call_kernel(
        lambda *refs: key_backward_kernel(
            *refs, factor=factor, scale=scale, planes=near, part=0, last=False, plain=plain,
            total_planes=planes,
        ),
        (info, kv_rows, q_all, cols, *g_near),
        [two_squares, two_squares],
        [
            ((4 * near * row_count, width), bf16), ((8 * near, 2 * HEADS, half), f32),
        ],
        "key_backward",
        8,
    )
    chips = add_chips(*chips)
    low_chips = chips.astype(bf16)
    dk_part = after(dk_part, low_chips)
    if not plain:
        maps = add_sides(*maps)
        dk_part = after(dk_part, maps[1])
    tok_rows, *last = call_kernel(
        lambda *refs: key_backward_kernel(
            *refs, factor=factor, scale=scale, planes=far, part=1, last=True, plain=plain,
            total_planes=planes,
        ),
        (info, kv_rows, q_all, cols, dk_part, dv_part, x_rows, gr1, dq, w_self, *g_far),
        [rows_low] + sink_shapes(2),
        [
            ((4 * far * row_count, width), bf16), ((8 * far, 2 * HEADS, half), f32),
            two_squares, two_squares, ((width, width), f32),
        ],
        "key_backward_last",
        10,
    )

    back_first = [(to, owner) for owner, to in perm_first]
    back_second = [(to, owner) for owner, to in perm_second]

    rows_out = jnp.stack([out_rows.astype(bf16), tok_rows])
    half_one = jnp.where(even, rows_out[:, :half], rows_out[:, half:])
    half_two = jnp.where(even, rows_out[:, half:], rows_out[:, :half])
    rows_out = jnp.concatenate(
        [lax.ppermute(half_one, "ctx", back_first), lax.ppermute(half_two, "ctx", back_second)],
        axis=1,
    ).astype(f32)
    layer_out, tokens_grad = rows_out[0], rows_out[1]
    chips = add_planes(chips, low_chips)
    memory_grad = chips[-mem_count:]

    lanes = width // 2
    if plain:

        def owned(matrix, axis):
            part = lax.psum_scatter(matrix, "fsdp", scatter_dimension=axis, tiled=True)
            return lax.psum(part, "ctx").astype(f32)

        feed, maps, last = feed[0], maps[0], last[0]
        ins = owned(jnp.concatenate([maps[5:6], last, maps[2:5]], axis=0), 1)
        outs = owned(maps[0:2], 1)
        up = owned(jnp.concatenate([feed[k] for k in range(4)], axis=1), 0)
        down = owned(feed[4:8].reshape(-1, width), 0)
        rest = jnp.stack([maps[6, 0:half_rows, 0:lanes], maps[6, half_rows:, 0:lanes]], axis=1)
        table = owned(rest[0:13].reshape(13, width).astype(f32), 1)
        shift = owned(rest[16:20].transpose(1, 0, 2).reshape(-1).astype(f32), 0)
    else:
        feed = spread(chips[:-mem_count])
        maps = add_planes(add_chips(*maps))
        last = add_planes(add_chips(*add_sides(*add_cores(*last))))
        rest = spread(jnp.concatenate([maps, last], axis=0))
        maps, last = rest[0:7], rest[7:9]
        ins = jnp.concatenate([maps[5:6], last, maps[2:5]], axis=0)
        outs = maps[0:2]
        up = jnp.concatenate([feed[k] for k in range(4)], axis=1)
        down = feed[4:8].reshape(-1, width)
        table = maps[6, 0:13, 0:lanes]
        shift = maps[6, 16:20, 0:lanes].reshape(-1)
    return (
        layer_out[None], tokens_grad[None], memory_grad[None], ins, outs, up, down,
        table[0:3], table[3:13], shift,
    )


def solution(mesh):
    rows = P("fsdp", "ctx", None)
    params = (
        P(None, "fsdp", None), P(None, "fsdp", None), P("fsdp", None), P("fsdp", None),
        P(None, "fsdp"), P(None, "fsdp"), P("fsdp"),
    )
    return jax.shard_map(
        body,
        mesh=mesh,
        in_specs=(rows, rows, P("fsdp", None), P("fsdp", None), rows) + params,
        out_specs=(rows, rows, rows) + params,
        check_vma=False,
    )
```

```python
import math

import jax
import jax.numpy as jnp
from jax import lax
from jax.experimental import pallas as pl
from jax.experimental.pallas import tpu as pltpu
from jax.sharding import PartitionSpec as P

HEADS = 8
PAIRS = HEADS // 2
neg_fill = -1e30
eps_norm = 1e-05
self_block = 512
bf16 = jnp.bfloat16
f32 = jnp.float32
vmem_bytes = 60 * 1024 * 1024
half_rows = 256
chunk_rows = 32


def dot_nn(first_op, second_op):
    return jnp.dot(first_op, second_op, preferred_element_type=f32)


def dot_nt(first_op, second_op):
    return lax.dot_general(
        first_op, second_op, (((1,), (1,)), ((), ())), preferred_element_type=f32
    )


def dot_tn(first_op, second_op):
    return lax.dot_general(
        first_op, second_op, (((0,), (0,)), ((), ())), preferred_element_type=f32
    )


def stack_heads(tile):
    lane = lax.broadcasted_iota(jnp.int32, tile.shape, 1)
    half = tile.shape[1] // 2
    zero = jnp.zeros_like(tile)
    return jnp.concatenate(
        [jnp.where(lane < half, tile, zero), jnp.where(lane >= half, tile, zero)], axis=0
    )


def merge_heads(stacked):
    rows = stacked.shape[0] // 2
    lane = lax.broadcasted_iota(jnp.int32, (rows, stacked.shape[1]), 1)
    return jnp.where(lane < stacked.shape[1] // 2, stacked[:rows], stacked[rows:])


def tile_of(value, pair, tile_width):
    return value[:, pair * tile_width : (pair + 1) * tile_width]


def head_sums(product):
    width = product.shape[1]
    head = lax.broadcasted_iota(jnp.int32, (HEADS, width), 0)
    lane = lax.broadcasted_iota(jnp.int32, (HEADS, width), 1)
    pick = (lane // (width // HEADS) == head).astype(f32)
    return lax.dot_general(
        pick,
        product,
        (((1,), (1,)), ((), ())),
        precision=lax.Precision.HIGHEST,
        preferred_element_type=f32,
    )


def over_range(first, last):
    def run(step):
        def visit(index, carry):
            step(index, index)
            return carry

        lax.fori_loop(first, last, visit, 0)

    return run


def over_planes(info, plane_first, plane_count, first, last):
    def run(step):
        def visit(stored, carry):
            index = 2 * (info.plane ^ (plane_first + (stored >> 1))) + (stored & 1)

            @pl.when((index >= first) & (index < last))
            def _():
                step(stored, index)

            return carry

        lax.fori_loop(0, 2 * plane_count, visit, 0)

    return run


class RowInfo:
    def __init__(self, info_ref):
        self.table = info_ref
        self.half = info_ref.shape[1] // 2
        self.me = info_ref[5, 0]
        self.side = info_ref[6, 0]
        self.plane = self.me >> 2

    def ends(self, block):
        return block * self.half, (block + 1) * self.half - 1

    def self_keys(self, block):
        start, stop = self.ends(block)
        return self.table[0, start] // self_block, self.table[1, stop] // self_block + 1

    def cross_keys(self, block, size):
        start, stop = self.ends(block)
        return self.table[2, start] // size, self.table[3, stop] // size + 1

    def queries(self, block):
        start, stop = self.ends(block)
        return self.table[1, start] // self_block, self.table[4, stop] // self_block + 1


def twice(column):
    return jnp.concatenate([column, column], axis=0)


def stacked_tiles(rows):
    tile_width = rows.shape[1] // PAIRS
    return [stack_heads(tile_of(rows, pair, tile_width)) for pair in range(PAIRS)]


def attend_plain(q_block, kv_ref, low_col, high_col, run, key_rows, factor, acc_ref):
    width = q_block.shape[1]
    tile_width = width // PAIRS
    stacked = stacked_tiles(q_block)
    low2, high2 = twice(low_col), twice(high_col)
    ones = jnp.ones((key_rows, tile_width), bf16)

    def step(stored, index):
        base = pl.multiple_of(stored * key_rows, key_rows)
        key_pos = index * key_rows + lax.broadcasted_iota(jnp.int32, (1, key_rows), 1)
        allowed = (key_pos >= low2) & (key_pos <= high2)
        for pair in range(PAIRS):
            start = pair * tile_width
            keys = kv_ref[pl.ds(base, key_rows), start : start + tile_width]
            values = kv_ref[pl.ds(base, key_rows), width + start : width + start + tile_width]
            scores = dot_nt(stacked[pair], keys)
            weights = jnp.where(allowed, jnp.exp2(scores * factor), 0.0).astype(bf16)
            acc_ref[pair] += dot_nn(weights, jnp.concatenate([values, ones], axis=1))

    run(step)


def weighted_rows(acc_ref):
    tile_width = acc_ref.shape[2] // 2
    tops = [merge_heads(acc_ref[pair, :, 0:tile_width]) for pair in range(PAIRS)]
    sums = [merge_heads(acc_ref[pair, :, tile_width:]) for pair in range(PAIRS)]
    return jnp.concatenate(tops, axis=1), jnp.concatenate(sums, axis=1)


def in_range(sums):
    return (jnp.min(sums) > 2.0**-100) & (jnp.max(sums) < 2.0**100)


def attend_running(q_block, parts, low_col, high_col, key_rows, factor, scratch):
    max_ref, sum_ref, acc_ref = scratch
    width = q_block.shape[1]
    tile_width = width // PAIRS
    stacked = stacked_tiles(q_block)
    low2, high2 = twice(low_col), twice(high_col)
    max_ref[...] = jnp.full(max_ref.shape, neg_fill, f32)
    sum_ref[...] = jnp.zeros(sum_ref.shape, f32)
    acc_ref[...] = jnp.zeros(acc_ref.shape, f32)
    for kv_ref, run in parts:

        def step(stored, index, kv_ref=kv_ref):
            base = pl.multiple_of(stored * key_rows, key_rows)
            key_pos = index * key_rows + lax.broadcasted_iota(jnp.int32, (1, key_rows), 1)
            allowed = (key_pos >= low2) & (key_pos <= high2)
            for pair in range(PAIRS):
                start = pair * tile_width
                keys = kv_ref[pl.ds(base, key_rows), start : start + tile_width]
                values = kv_ref[pl.ds(base, key_rows), width + start : width + start + tile_width]
                scores = jnp.where(allowed, dot_nt(stacked[pair], keys), neg_fill)
                old_max = max_ref[pair]
                new_max = jnp.maximum(old_max, jnp.max(scores, axis=1, keepdims=True))
                probs = jnp.exp2((scores - new_max) * factor)
                rescale = jnp.exp2((old_max - new_max) * factor)
                sum_ref[pair] = sum_ref[pair] * rescale + jnp.sum(probs, axis=1, keepdims=True)
                acc_ref[pair] = acc_ref[pair] * rescale + dot_nn(probs.astype(bf16), values)
                max_ref[pair] = new_max

        run(step)
    outputs, logs = [], []
    for pair in range(PAIRS):
        outputs.append(merge_heads(acc_ref[pair] / sum_ref[pair]))
        column = max_ref[pair] * factor + jnp.log2(sum_ref[pair])
        logs.append(merge_heads(jnp.broadcast_to(column, acc_ref.shape[1:])))
    return jnp.concatenate(outputs, axis=1), jnp.concatenate(logs, axis=1)


def log_rows_of(lane_logs):
    return head_sums(lane_logs) * (HEADS / lane_logs.shape[1])


def query_grads(
    q_block, g_block, kv_ref, low_col, high_col, log_ref, delta_ref, run, key_rows, factor, acc_ref
):
    width = q_block.shape[1]
    tile_width = width // PAIRS
    q2, g2 = stacked_tiles(q_block), stacked_tiles(g_block)
    low2, high2 = twice(low_col), twice(high_col)

    def step(stored, index):
        base = pl.multiple_of(stored * key_rows, key_rows)
        key_pos = index * key_rows + lax.broadcasted_iota(jnp.int32, (1, key_rows), 1)
        allowed = (key_pos >= low2) & (key_pos <= high2)
        for pair in range(PAIRS):
            start = pair * tile_width
            keys = kv_ref[pl.ds(base, key_rows), start : start + tile_width]
            values = kv_ref[pl.ds(base, key_rows), width + start : width + start + tile_width]
            scores = dot_nt(q2[pair], keys)
            repeats = key_rows // log_ref.shape[2]
            logs = jnp.concatenate([log_ref[pair]] * repeats, axis=1)
            deltas = jnp.concatenate([delta_ref[pair]] * repeats, axis=1)
            probs = jnp.where(allowed, jnp.exp2(scores * factor - logs), 0.0)
            prob_grad = dot_nt(g2[pair], values)
            score_grad = (probs * (prob_grad - deltas)).astype(bf16)
            acc_ref[pair] += dot_nn(score_grad, keys)

    run(step)


def key_grads(k_block, v_block, q_ref, g_ref, stats_ref, low_col, high_col, run, factor, dk_ref, dv_ref):
    width = k_block.shape[1]
    tile_width = width // PAIRS
    rows = k_block.shape[0]
    query_rows = self_block
    blocks = query_rows // rows
    k2, v2 = stacked_tiles(k_block), stacked_tiles(v_block)
    low2, high2 = twice(low_col), twice(high_col)

    def step(stored, index):
        base = pl.multiple_of(stored * query_rows, query_rows)
        q_base = pl.multiple_of(index * query_rows, query_rows)
        query_pos = q_base + lax.broadcasted_iota(jnp.int32, (1, query_rows), 1)
        allowed = (query_pos >= low2) & (query_pos <= high2)
        stats = jnp.concatenate([stats_ref[stored * blocks + u] for u in range(blocks)], axis=1)

        def two_rows(first_row):
            return jnp.concatenate(
                [
                    jnp.broadcast_to(stats[first_row : first_row + 1], (rows, query_rows)),
                    jnp.broadcast_to(stats[first_row + 1 : first_row + 2], (rows, query_rows)),
                ],
                axis=0,
            )

        for pair in range(PAIRS):
            lanes = slice(pair * tile_width, (pair + 1) * tile_width)
            queries = q_ref[pl.ds(q_base, query_rows), lanes]
            upstream = g_ref[pl.ds(base, query_rows), lanes]
            scores = dot_nt(k2[pair], queries)
            probs = jnp.where(allowed, jnp.exp2(scores * factor - two_rows(2 * pair)), 0.0)
            prob_grad = dot_nt(v2[pair], upstream)
            score_grad = (probs * (prob_grad - two_rows(HEADS + 2 * pair))).astype(bf16)
            dk_ref[pair] += dot_nn(score_grad, queries)
            dv_ref[pair] += dot_nn(probs.astype(bf16), upstream)

    run(step)


def merged_rows(acc_ref):
    return jnp.concatenate([merge_heads(acc_ref[pair]) for pair in range(PAIRS)], axis=1)


def chunk_views(piece_refs, planes):
    for s in range(planes):
        for bits in range(4):
            yield s, bits, piece_refs[(bits >> 1) + 2 * (bits & 1)].at[s]


def fill_rows(target, parts, info, skip=0, lead=0):
    own, fetched, other = parts
    rows = own.shape[-2]
    core = info.me & 1
    starts = (
        info.side * rows,
        (1 - info.side) * rows + core * (rows // 2),
        (1 - info.side) * rows + (1 - core) * (rows // 2),
    )
    for number, (part, start) in enumerate(zip((own, fetched, other), starts)):
        size = rows // 2 if number else rows
        at = pl.ds(pl.multiple_of(start, rows // 2), size)
        if len(target.shape) == 3:
            for k in range(target.shape[0]):
                first = skip + k * size
                window = part[first : first + size] if number else part[lead + k]
                target[k, at, :] = window.astype(bf16)
        elif target.shape[1] == part.shape[1]:
            target[at, :] = (part[skip : skip + size] if number else part[...]).astype(bf16)
        elif not number:
            target[at, :] = part[...].astype(bf16)
        else:
            width = part.shape[1]
            for k in range(target.shape[1] // width):
                first = skip + k * size
                target[at, k * width : (k + 1) * width] = part[first : first + size]


def attend_back(
    q_block, g_block, kv_ref, dkv_ref, low_row, high_row, log_rows, delta_rows,
    first, last, key_rows, factor, scale, dq_ref, adding,
):
    width = q_block.shape[1]
    tile_width = width // PAIRS
    rows = q_block.shape[0]
    q2 = [stack_heads(tile_of(q_block, pair, tile_width)) for pair in range(PAIRS)]
    g2 = [stack_heads(tile_of(g_block, pair, tile_width)) for pair in range(PAIRS)]
    low2 = jnp.concatenate([low_row, low_row], axis=1)
    high2 = jnp.concatenate([high_row, high_row], axis=1)
    dq_ref[...] = jnp.zeros(dq_ref.shape, f32)

    def step(index, carry):
        base = pl.multiple_of(index * key_rows, key_rows)
        key_pos = base + lax.broadcasted_iota(jnp.int32, (key_rows, 1), 0)
        allowed = (key_pos >= low2) & (key_pos <= high2)
        for pair in range(PAIRS):
            key_at = (pl.ds(base, key_rows), slice(pair * tile_width, (pair + 1) * tile_width))
            value_at = (
                pl.ds(base, key_rows),
                slice(width + pair * tile_width, width + (pair + 1) * tile_width),
            )
            keys = kv_ref[key_at]
            values = kv_ref[value_at]
            scores = dot_nt(keys, q2[pair])
            probs = jnp.where(allowed, jnp.exp2(scores * factor - log_rows[pair]), 0.0)
            prob_grad = dot_nt(values, g2[pair])
            score_grad = (probs * (prob_grad - delta_rows[pair])).astype(bf16)
            key_grad = dot_nn(score_grad, q2[pair]) * scale
            value_grad = dot_nn(probs.astype(bf16), g2[pair])
            if adding:
                key_grad = key_grad + dkv_ref[key_at].astype(f32)
                value_grad = value_grad + dkv_ref[value_at].astype(f32)
            dkv_ref[key_at] = key_grad.astype(bf16)
            dkv_ref[value_at] = value_grad.astype(bf16)
            dq_ref[pair] += dot_tn(keys, score_grad)
        return carry

    lax.fori_loop(first, last, step, 0)
    tiles = []
    for pair in range(PAIRS):
        both = dq_ref[pair]
        feature = lax.broadcasted_iota(jnp.int32, (tile_width, rows), 0)
        picked = jnp.where(feature < tile_width // 2, both[:, :rows], both[:, rows:])
        tiles.append(jnp.transpose(picked) * scale)
    return jnp.concatenate(tiles, axis=1)


def split_three(value):
    one = value.astype(bf16)
    rest = value - one.astype(f32)
    two = rest.astype(bf16)
    three = (rest - two.astype(f32)).astype(bf16)
    return [one, two, three]


def side_by_side(stats):
    rows = stats.shape[0] // 2
    return jnp.concatenate([stats[:rows], stats[rows:]], axis=1)


class PieceSink:
    def __init__(self, keep_ref, send_ref, scratch_ref, me, side):
        self.keep, self.send, self.scratch, self.me, self.side = keep_ref, send_ref, scratch_ref, me, side

    def emit(self, block, stride, offset):
        planes = self.keep.shape[2]
        piece = half_rows // (4 * planes)
        at = slice(block * piece, (block + 1) * piece)
        for s in range(planes):
            for bits in range(4):
                dc, dx = bits & 1, bits >> 1
                owner = self.me ^ (4 * s + bits)
                for fy in range(2):
                    source = (self.side ^ fy) * stride + offset + owner * piece
                    rows = self.scratch[pl.ds(pl.multiple_of(source, piece), piece), :]
                    target = self.send if dc else self.keep
                    target[fy, dx, s, at, :] = rows.astype(bf16)

    def put(self, block, matrix):
        rows = matrix.shape[0]
        self.scratch[0:rows, :] = matrix.astype(f32)
        blocks = rows // (2 * half_rows)
        for b in range(blocks):
            self.emit(block + b, rows // 2, b * half_rows)


class PlainSink:
    def __init__(self, plain_ref):
        self.plain = plain_ref

    def put(self, block, matrix):
        size = 2 * half_rows
        for b in range(matrix.shape[0] // size):
            self.plain[block + b] = matrix[b * size : (b + 1) * size].astype(bf16)


def pair_rows(by_head, block, rows, pair):
    at = slice(block * rows, (block + 1) * rows)
    return jnp.concatenate(
        [by_head[2 * pair : 2 * pair + 1, at], by_head[2 * pair + 1 : 2 * pair + 2, at]], axis=1
    )


def norm_stats(residual):
    centre = residual - jnp.mean(residual, axis=1, keepdims=True)
    spread = jnp.mean(centre * centre, axis=1, keepdims=True)
    inverse = lax.rsqrt(spread + eps_norm)
    return centre * inverse, inverse


def norm_back(normed, inverse, gain_row, upstream):
    scaled = upstream * gain_row
    mean_one = jnp.mean(scaled, axis=1, keepdims=True)
    mean_two = jnp.mean(scaled * normed, axis=1, keepdims=True)
    return (scaled - mean_one - normed * mean_two) * inverse


def column_sum(matrix):
    return jnp.sum(matrix.astype(f32), axis=0, keepdims=True)


def project_chunks(pieces, planes, kv_ref, w_ref, shift, info):
    width = w_ref.shape[2]
    rows = pieces[0].shape[1]
    for s, bits, chunk in chunk_views(pieces, planes):
        start = 4 * rows * s + rows * ((info.me & 3) ^ bits)
        at = pl.ds(pl.multiple_of(start, rows), rows)
        block = chunk[...]
        kv_ref[at, 0:width] = dot_nn(block, w_ref[1]).astype(bf16)
        kv_ref[at, width:] = (dot_nn(block, w_ref[2]) + shift).astype(bf16)


def first_forward_kernel(info_ref, x_ref, bias_ref, cols_ref, *refs, factor, planes, shards):
    maps, refs = refs[:shards], refs[shards:]
    pieces, refs = refs[:4], refs[4:]
    q_ref, kv_rows_ref, kv_ref, w_ref, top_ref, sums_ref, acc_ref = refs
    info = RowInfo(info_ref)
    width = x_ref.shape[1]
    half = info.half
    if shards == 1:
        w_ref[...] = maps[0][0:3]
    else:
        fill_rows(w_ref, maps, info)
    shift = bias_ref[1:2, :]
    project_chunks(pieces, planes, kv_ref, w_ref, shift, info)
    x_rows = x_ref[...]
    q_rows = (dot_nn(x_rows, w_ref[0]) + bias_ref[0:1, :]).astype(bf16)
    q_ref[...] = q_rows
    kv_rows_ref[:, 0:width] = dot_nn(x_rows, w_ref[1]).astype(bf16)
    kv_rows_ref[:, width:] = (dot_nn(x_rows, w_ref[2]) + shift).astype(bf16)
    for block in range(2):
        at = slice(block * half, (block + 1) * half)
        acc_ref[...] = jnp.zeros(acc_ref.shape, f32)
        run = over_planes(info, 0, planes, *info.self_keys(block))
        attend_plain(
            q_rows[at], kv_ref, cols_ref[at, 0:1], cols_ref[at, 1:2], run, self_block, factor, acc_ref
        )
        top_ref[at, :], sums_ref[at, :] = weighted_rows(acc_ref)


def second_forward_kernel(
    info_ref, kv_near_ref, q_in_ref, bias_ref, cols_ref, w_ref, top_ref, sums_ref, *refs,
    factor, planes,
):
    pieces, refs = refs[:4], refs[4:]
    a_ref, log_ref, kv_ref, acc_ref, max_ref, sum_ref, run_ref, lane_ref, near_ref, near_sem = refs
    info = RowInfo(info_ref)
    half = info.half
    project_chunks(pieces, planes, kv_ref, w_ref, bias_ref[1:2, :], info)
    fine = None
    for block in range(2):
        at = slice(block * half, (block + 1) * half)
        acc_ref[...] = jnp.zeros(acc_ref.shape, f32)
        run = over_planes(info, planes, planes, *info.self_keys(block))
        attend_plain(
            q_in_ref[at, :], kv_ref, cols_ref[at, 0:1], cols_ref[at, 1:2], run, self_block, factor,
            acc_ref,
        )
        top, sums = weighted_rows(acc_ref)
        sums = sums + sums_ref[at, :]
        a_ref[at, :] = (top + top_ref[at, :]) / sums
        lane_ref[at, :] = jnp.log2(sums)
        fine = in_range(sums) if fine is None else fine & in_range(sums)

    @pl.when(jnp.logical_not(fine))
    def _():
        copy = pltpu.make_async_copy(kv_near_ref, near_ref, near_sem)
        copy.start()
        copy.wait()
        for block in range(2):
            at = slice(block * half, (block + 1) * half)
            keys = info.self_keys(block)
            a_ref[at, :], lane_ref[at, :] = attend_running(
                q_in_ref[at, :],
                [
                    (near_ref, over_planes(info, 0, planes, *keys)),
                    (kv_ref, over_planes(info, planes, planes, *keys)),
                ],
                cols_ref[at, 0:1], cols_ref[at, 1:2], self_block, factor, (max_ref, sum_ref, run_ref),
            )

    log_ref[...] = log_rows_of(lane_ref[...])


def project_kernel(info_ref, w_ref, bias_ref, *refs, planes):
    pieces, (q_ref,) = refs[:8], refs[8:]
    info = RowInfo(info_ref)
    for part in range(2):
        for s, bits, chunk in chunk_views(pieces[4 * part : 4 * part + 4], planes):
            rows = chunk.shape[0]
            place = info.me ^ (4 * (part * planes + s) + bits)
            at = pl.ds(pl.multiple_of(place * rows, rows), rows)
            q_ref[at, :] = (dot_nn(chunk[...], w_ref[0]) + bias_ref[0:1, :]).astype(bf16)


def middle_forward_kernel(
    info_ref, x_ref, a_ref, g_ref, cols_ref, gain_ref, bias_ref, ffn_bias_ref, mem_ref, *refs,
    factor, shards, cross_rows,
):
    late, refs = (refs[:3], refs[3:]) if shards == 1 else (refs[:5], refs[5:])
    (
        out_ref, a_low_ref, h1_ref, h2_ref, f_ref, e3_ref, gu_ref, e2_ref, ac_ref, gr2_ref, r1_ref,
        qc_ref, cross_ref, cross_log_ref, kvc_ref, sums_ref, csum_ref, wc_ref,
        acc_ref, max_ref, sum_ref, run_ref, lane_ref, *whole_refs,
    ) = refs
    info = RowInfo(info_ref)
    if shards == 1:
        maps_ref, u_ref, v_ref = late
        wc_ref[...] = maps_ref[3:8]
    else:
        maps_ref, up_ref, down_ref, one, two = late
        u_ref, v_ref = whole_refs
        size = maps_ref.shape[1] // 2
        fill_rows(wc_ref, (maps_ref, one, two), info, 0, 3)
        fill_rows(v_ref, (down_ref, one, two), info, 5 * size)
        fill_rows(u_ref, (up_ref, one, two), info, 5 * size + down_ref.shape[0] // 2)
    rows, width = x_ref.shape
    half = rows // 2
    cross_block = cross_rows
    cross_range = [info.cross_keys(block, cross_block) for block in range(2)]
    live_first = jnp.minimum(cross_range[0][0], cross_range[1][0])
    live_last = jnp.maximum(cross_range[0][1], cross_range[1][1])

    def project(index, carry):
        at = pl.ds(pl.multiple_of(index * cross_block, cross_block), cross_block)
        block = mem_ref[at, :]
        kvc_ref[at, 0:width] = dot_nn(block, wc_ref[1]).astype(bf16)
        kvc_ref[at, width:] = (dot_nn(block, wc_ref[2]) + bias_ref[5:6, :]).astype(bf16)
        return carry

    lax.fori_loop(live_first, live_last, project, 0)
    attn_self = a_ref[...]
    a_low = attn_self.astype(bf16)
    a_low_ref[...] = a_low
    r1 = x_ref[...].astype(f32) + (dot_nn(a_low, wc_ref[3]) + bias_ref[2:3, :])
    r1_ref[...] = r1
    n1, inv1 = norm_stats(r1)
    h1 = n1 * gain_ref[0:1, :] + bias_ref[3:4, :]
    h1_low = h1.astype(bf16)
    h1_ref[...] = h1_low
    qc = (dot_nn(h1_low, wc_ref[0]) + bias_ref[4:5, :]).astype(bf16)
    qc_ref[...] = qc
    fine = None
    for block in range(2):
        at = slice(block * half, (block + 1) * half)
        acc_ref[...] = jnp.zeros(acc_ref.shape, f32)
        attend_plain(
            qc[at], kvc_ref, cols_ref[at, 2:3], cols_ref[at, 3:4], over_range(*cross_range[block]),
            cross_block, factor, acc_ref,
        )
        top, weights = weighted_rows(acc_ref)
        cross_ref[at, :] = top / weights
        lane_ref[at, :] = jnp.log2(weights)
        fine = in_range(weights) if fine is None else fine & in_range(weights)

    @pl.when(jnp.logical_not(fine))
    def _():
        for block in range(2):
            at = slice(block * half, (block + 1) * half)
            cross_ref[at, :], lane_ref[at, :] = attend_running(
                qc_ref[at, :], [(kvc_ref, over_range(*cross_range[block]))],
                cols_ref[at, 2:3], cols_ref[at, 3:4], cross_block, factor, (max_ref, sum_ref, run_ref),
            )

    cross_log_ref[...] = log_rows_of(lane_ref[...])
    attn_cross = cross_ref[...]
    ac_low = attn_cross.astype(bf16)
    ac_ref[...] = ac_low
    r2 = h1 + (dot_nn(ac_low, wc_ref[4]) + bias_ref[6:7, :])
    n2, inv2 = norm_stats(r2)
    h2 = n2 * gain_ref[1:2, :] + bias_ref[7:8, :]
    h2_low = h2.astype(bf16)
    h2_ref[...] = h2_low
    u = dot_nn(h2_low, u_ref[...]) + ffn_bias_ref[...]
    sig = 1.0 / (1.0 + jnp.exp(-u))
    act = (u / (1.0 + jnp.exp(-u))).astype(bf16)
    f_ref[...] = act
    slope = sig * (1.0 + u * (1.0 - sig))
    r3 = h2 + (dot_nn(act, v_ref[...]) + bias_ref[8:9, :])
    n3, inv3 = norm_stats(r3)
    out_ref[...] = n3 * gain_ref[2:3, :] + bias_ref[9:10, :]
    sums_ref[...] = jnp.zeros_like(sums_ref)
    upstream = g_ref[...].astype(f32)
    sums_ref[2:3, :] = column_sum(upstream * n3)
    sums_ref[12:13, :] = column_sum(upstream)
    gr3 = norm_back(n3, inv3, gain_ref[2:3, :], upstream)
    e3 = gr3.astype(bf16)
    e3_ref[...] = e3
    sums_ref[11:12, :] = column_sum(e3)
    gu = (dot_nt(e3, v_ref[...]) * slope).astype(bf16)
    gu_ref[...] = gu
    csum_ref[...] = column_sum(gu)
    gh2 = gr3 + dot_nt(gu, u_ref[...])
    sums_ref[1:2, :] = column_sum(gh2 * n2)
    sums_ref[10:11, :] = column_sum(gh2)
    gr2 = norm_back(n2, inv2, gain_ref[1:2, :], gh2)
    gr2_ref[...] = gr2
    e2 = gr2.astype(bf16)
    e2_ref[...] = e2
    sums_ref[9:10, :] = column_sum(e2)


def middle_backward_kernel(
    info_ref, a_ref, log_ref, rows_ref, gain_ref, wc_ref, e2_ref, gr2_ref, r1_ref, qc_ref,
    cross_ref, cross_log_ref, kvc_ref, sums_in_ref,
    e1_ref, dqc_ref, ga_ref, gr1_ref, delta_ref, dkvc_ref, sums_ref, dq_ref,
    *, factor, scale, cross_rows,
):
    info = RowInfo(info_ref)
    rows, width = a_ref.shape
    half = rows // 2
    cross_block = cross_rows
    cross_range = [info.cross_keys(block, cross_block) for block in range(2)]
    live_first = jnp.minimum(cross_range[0][0], cross_range[1][0])
    live_last = jnp.maximum(cross_range[0][1], cross_range[1][1])
    sums_ref[...] = sums_in_ref[...]
    n1, inv1 = norm_stats(r1_ref[...])
    attn_self, attn_cross = a_ref[...], cross_ref[...]
    gr2, e2, qc, cross_logs = gr2_ref[...], e2_ref[...], qc_ref[...], cross_log_ref[...]

    def clear(index, carry):
        at = pl.ds(pl.multiple_of(index * cross_block, cross_block), cross_block)
        dkvc_ref[at, :] = jnp.zeros((cross_block, 2 * width), bf16)
        return carry

    lax.fori_loop(live_first, live_last, clear, 0)
    gac = dot_nt(e2, wc_ref[4]).astype(bf16)
    sums_ref[8:9, :] = column_sum(gac)
    delta_cross = head_sums(gac.astype(f32) * attn_cross)
    grads = []
    for block in (1, 0):
        at = slice(block * half, (block + 1) * half)
        grads.append(
            attend_back(
                qc[at], gac[at], kvc_ref, dkvc_ref, rows_ref[2:3, at], rows_ref[3:4, at],
                [pair_rows(cross_logs, block, half, p) for p in range(PAIRS)],
                [pair_rows(delta_cross, block, half, p) for p in range(PAIRS)],
                *cross_range[block], cross_block, factor, scale,
                dq_ref, True,
            )
        )
    dqc = jnp.concatenate([grads[1], grads[0]], axis=0).astype(bf16)
    dqc_ref[...] = dqc
    sums_ref[7:8, :] = column_sum(dqc)
    gh1 = gr2 + dot_nt(dqc, wc_ref[0])
    sums_ref[0:1, :] = column_sum(gh1 * n1)
    sums_ref[6:7, :] = column_sum(gh1)
    gr1 = norm_back(n1, inv1, gain_ref[0:1, :], gh1)
    gr1_ref[...] = gr1
    e1 = gr1.astype(bf16)
    e1_ref[...] = e1
    sums_ref[5:6, :] = column_sum(e1)
    ga = dot_nt(e1, wc_ref[3]).astype(bf16)
    ga_ref[0:rows, :] = ga
    sums_ref[4:5, :] = column_sum(ga)
    delta = head_sums(ga.astype(f32) * attn_self)
    delta_ref[...] = delta
    extra = split_three(side_by_side(log_ref[...])) + split_three(side_by_side(delta))
    extra.append(jnp.zeros((2 * HEADS // 2, width), bf16))
    ga_ref[rows:, :] = jnp.concatenate([e.astype(f32) for e in extra], axis=0).astype(bf16)


def memory_grads_kernel(
    info_ref, mem_ref, wc_ref, dkvc_ref, pm_ref, dwc_ref, dw_acc_ref, *, cross_block
):
    info = RowInfo(info_ref)
    width = mem_ref.shape[1]
    cross_range = [info.cross_keys(block, cross_block) for block in range(2)]
    live_first = jnp.minimum(cross_range[0][0], cross_range[1][0])
    live_last = jnp.maximum(cross_range[0][1], cross_range[1][1])
    pm_ref[...] = jnp.zeros(pm_ref.shape, bf16)
    dw_acc_ref[...] = jnp.zeros(dw_acc_ref.shape, f32)

    def memory_step(index, carry):
        at = pl.ds(pl.multiple_of(index * cross_block, cross_block), cross_block)
        grads_block = dkvc_ref[at, :]
        block = dot_nt(grads_block[:, :width], wc_ref[1]) + dot_nt(grads_block[:, width:], wc_ref[2])
        pm_ref[at, :] = block.astype(bf16)
        dw_acc_ref[...] += dot_tn(mem_ref[at, :], grads_block)
        return carry

    lax.fori_loop(live_first, live_last, memory_step, 0)
    dwc_ref[...] = dw_acc_ref[...].astype(bf16)


def query_backward_kernel(
    info_ref, q_ref, ga_ref, kv_near_ref, kv_far_ref, log_ref, delta_ref, cols_ref, dq_ref, acc_ref,
    log_rep_ref, delta_rep_ref, *, factor, scale, planes,
):
    info = RowInfo(info_ref)
    rows = q_ref.shape[0]
    half = info.half
    pad = jnp.zeros((128 - 2 * HEADS, rows), f32)
    stat_cols = jnp.transpose(jnp.concatenate([log_ref[...], delta_ref[...], pad], axis=0))

    def stat_column(at, head):
        return jnp.concatenate(
            [stat_cols[at, head : head + 1], stat_cols[at, head + 1 : head + 2]], axis=0
        )

    for block in range(2):
        at = slice(block * half, (block + 1) * half)
        acc_ref[...] = jnp.zeros(acc_ref.shape, f32)
        for p in range(PAIRS):
            log_rep_ref[p] = jnp.broadcast_to(stat_column(at, 2 * p), log_rep_ref.shape[1:])
            delta_rep_ref[p] = jnp.broadcast_to(stat_column(at, HEADS + 2 * p), log_rep_ref.shape[1:])
        for part, kv_ref in enumerate((kv_near_ref, kv_far_ref)):
            query_grads(
                q_ref[at, :], ga_ref[at, :], kv_ref, cols_ref[at, 0:1], cols_ref[at, 1:2],
                log_rep_ref, delta_rep_ref,
                over_planes(info, part * planes, planes, *info.self_keys(block)),
                self_block, factor, acc_ref,
            )
        dq_ref[at, :] = (merged_rows(acc_ref) * scale).astype(bf16)


def key_backward_kernel(
    info_ref, kv_rows_ref, q_all_ref, cols_ref, *refs, factor, scale, planes, part, last,
    total_planes,
):
    state_in, refs = (refs[:2], refs[2:]) if part else ((), refs)
    pieces, refs = refs[:4], refs[4:]
    if last:
        dk_out_ref, dv_out_ref, g_ref, stats_ref, dk_ref, dv_ref = refs
    else:
        dk_ref, dv_ref, g_ref, stats_ref = refs
    info = RowInfo(info_ref)
    half = info.half
    rows = 2 * half
    width = q_all_ref.shape[1]
    for s, bits, chunk in chunk_views(pieces, planes):
        place = (info.me & 3) ^ bits
        extra = chunk[rows : rows + chunk_rows, :].astype(f32)
        logs = extra[0:4] + extra[4:8] + extra[8:12]
        deltas = extra[12:16] + extra[16:20] + extra[20:24]
        for side in range(2):
            block = 8 * s + 4 * side + (place if side == 0 else 3 - place)
            lanes = slice(side * half, (side + 1) * half)
            high = slice(rows + side * half, rows + (side + 1) * half)
            g_ref[pl.ds(pl.multiple_of(block * half, half), half), :] = chunk[lanes, :]
            stats_ref[block] = jnp.concatenate(
                [logs[:, lanes], logs[:, high], deltas[:, lanes], deltas[:, high]], axis=0
            )

    def groups(first, stop):
        def run(step):
            def visit(stored, carry):
                plane = info.plane ^ (part * planes + (stored >> 1))
                index = jnp.where((stored & 1) == 0, plane, 2 * total_planes - 1 - plane)

                @pl.when((index >= first) & (index < stop))
                def _():
                    step(stored, index)

                return carry

            lax.fori_loop(0, 2 * planes, visit, 0)

        return run

    for block in range(2):
        at = slice(block * half, (block + 1) * half)
        if part:
            dk_ref[block] = state_in[0][block]
            dv_ref[block] = state_in[1][block]
        else:
            dk_ref[block] = jnp.zeros(dk_ref.shape[1:], f32)
            dv_ref[block] = jnp.zeros(dv_ref.shape[1:], f32)
        key_grads(
            kv_rows_ref[at, 0:width], kv_rows_ref[at, width:], q_all_ref, g_ref, stats_ref,
            cols_ref[at, 1:2], cols_ref[at, 4:5], groups(*info.queries(block)), factor,
            dk_ref.at[block], dv_ref.at[block],
        )
    if not last:
        return
    dk = jnp.concatenate([merged_rows(dk_ref.at[b]) for b in range(2)], axis=0) * scale
    dv = jnp.concatenate([merged_rows(dv_ref.at[b]) for b in range(2)], axis=0)
    dk_out_ref[...] = dk.astype(bf16)
    dv_out_ref[...] = dv.astype(bf16)


def self_grads_kernel(
    info_ref, x_ref, gr1_ref, dq_ref, dk_ref, dv_ref, w_ref, tok_ref, *refs, plain
):
    sink_refs, (dw_ref,) = (refs[:1], refs[1:]) if plain else (refs[:2], refs[2:])
    info = RowInfo(info_ref)
    dk, dv = dk_ref[...], dv_ref[...]
    tok = gr1_ref[...] + dot_nt(dq_ref[...], w_ref[0]) + dot_nt(dk, w_ref[1]) + dot_nt(dv, w_ref[2])
    tok_ref[...] = tok.astype(bf16)
    sink = PlainSink(*sink_refs) if plain else PieceSink(*sink_refs, dw_ref, info.me, info.side)
    x_rows = x_ref[...]
    sink.put(0, dot_tn(x_rows, dk))
    sink.put(1, dot_tn(x_rows, dv))


def feed_grads_kernel(info_ref, h2_ref, gu_ref, f_ref, e3_ref, *refs, plain):
    sink_refs, (dw_ref,) = (refs[:1], refs[1:]) if plain else (refs[:2], refs[2:])
    info = RowInfo(info_ref)
    sink = PlainSink(*sink_refs) if plain else PieceSink(*sink_refs, dw_ref, info.me, info.side)
    width = h2_ref.shape[1]
    parts = gu_ref.shape[1] // width
    for k in range(parts):
        sink.put(k, dot_tn(h2_ref[...], gu_ref[:, k * width : (k + 1) * width]))
    sink.put(parts, dot_tn(f_ref[...], e3_ref[...]))


def map_grads_kernel(
    info_ref, a_ref, e1_ref, ac_ref, e2_ref, h1_ref, dqc_ref, dwc_ref, x_ref, dq_ref, sums_ref,
    csum_ref, *refs, plain,
):
    sink_refs, (dw_ref,) = (refs[:1], refs[1:]) if plain else (refs[:2], refs[2:])
    info = RowInfo(info_ref)
    sink = PlainSink(*sink_refs) if plain else PieceSink(*sink_refs, dw_ref, info.me, info.side)
    width = a_ref.shape[1]
    sink.put(0, dot_tn(a_ref[...], e1_ref[...]))
    sink.put(1, dot_tn(ac_ref[...], e2_ref[...]))
    sink.put(2, dot_tn(h1_ref[...], dqc_ref[...]))
    sink.put(3, dwc_ref[:, :width])
    sink.put(4, dwc_ref[:, width:])
    sink.put(5, dot_tn(x_ref[...], dq_ref[...]))
    put_small(sink, 6, dw_ref, sums_ref[...], csum_ref, dq_ref[...])


def put_small(sink, block, dw_ref, sums, csum_ref, dq):
    dw_ref[...] = jnp.zeros(dw_ref.shape, f32)
    row = lax.broadcasted_iota(jnp.int32, sums.shape, 0)
    sums = jnp.where(row == 3, column_sum(dq), sums)
    lanes = csum_ref.shape[1] // 8
    for yh in range(2):
        base = yh * half_rows
        dw_ref[base : base + 16, 0:lanes] = sums[:, yh * lanes : (yh + 1) * lanes]
        for k in range(4):
            start = yh * 4 * lanes + k * lanes
            dw_ref[base + 16 + k : base + 17 + k, 0:lanes] = csum_ref[:, start : start + lanes]
    if isinstance(sink, PlainSink):
        sink.plain[block] = dw_ref[...].astype(bf16)
    else:
        sink.emit(block, half_rows, 0)


def place_kernel(info_ref, *refs, places):
    sources, outs = refs[:4], refs[4:]
    info = RowInfo(info_ref)
    planes = sources[0].shape[0]
    piece = half_rows // (4 * planes)
    for s in range(planes):
        for bits in range(4):
            owner = info.me ^ (4 * s + bits)
            source = sources[(bits >> 1) + 2 * (bits & 1)]
            for block, (number, kind, k) in enumerate(places):
                rows = source[s, block * piece : (block + 1) * piece, :].astype(f32)
                width = rows.shape[1]
                base = k * half_rows if kind == "rows" else 0
                at = pl.ds(pl.multiple_of(base + owner * piece, piece), piece)
                if kind == "lead":
                    outs[number][k, at, :] = rows
                elif kind == "cols":
                    outs[number][at, k * width : (k + 1) * width] = rows
                else:
                    outs[number][at, :] = rows


def place_maps_kernel(
    info_ref, own_ref, other_ref, own_core_ref, other_core_ref, ins_ref, outs_ref, gain_ref, bias_ref,
    shift_ref, rest_ref,
):
    place_kernel(
        info_ref, own_ref, other_ref, own_core_ref, other_core_ref, ins_ref, outs_ref, rest_ref,
        places=[(1, "lead", 0), (1, "lead", 1)]
        + [(0, "lead", k) for k in (3, 4, 5, 0)]
        + [(2, "rows", 0), (0, "lead", 1), (0, "lead", 2)],
    )
    lanes = gain_ref.shape[1]
    gain_ref[...] = rest_ref[0:3, 0:lanes]
    bias_ref[...] = rest_ref[3:13, 0:lanes]
    shift_ref[...] = rest_ref[16:20, 0:lanes]


def call_kernel(kernel, inputs, outputs, scratch, name, micros, in_place=()):
    vmem = pl.BlockSpec(memory_space=pltpu.VMEM)
    smem = pl.BlockSpec(memory_space=pltpu.SMEM)
    return pl.pallas_call(
        kernel,
        in_specs=[smem]
        + [
            pl.BlockSpec(memory_space=pl.ANY) if index in in_place else vmem
            for index in range(1, len(inputs))
        ],
        out_specs=[vmem] * len(outputs),
        out_shape=[jax.ShapeDtypeStruct(*entry) for entry in outputs],
        scratch_shapes=[pltpu.VMEM(*entry) if isinstance(entry, tuple) else entry for entry in scratch],
        compiler_params=pltpu.CompilerParams(vmem_limit_bytes=vmem_bytes),
        cost_estimate=pl.CostEstimate(
            flops=int(micros * 1e9), transcendentals=0, bytes_accessed=int(micros * 1e4)
        ),
        name=name,
    )(*inputs)


def exchange(value, bits):
    count = lax.axis_size("ctx")
    return lax.ppermute(value, "ctx", [(i, i ^ bits) for i in range(count)])


def swap_side(value):
    return lax.ppermute(value, "fsdp", [(0, 1), (1, 0)])


def after(value, *others):
    return lax.optimization_barrier((value,) + others)[0]


def fetch_planes(value):
    planes = lax.axis_size("ctx") // 4
    return [value] + [exchange(value, 4 * s) for s in range(1, planes)]


def fetch_chips(chunks):
    return [chunks, exchange(chunks, 2)]


def fetch_cores(pair):
    return pair + [exchange(chunks, 1) for chunks in pair]


def core_part(shard, axis):
    rows = shard.shape[axis] // 2
    return lax.dynamic_slice_in_dim(shard, (lax.axis_index("ctx") % 2) * rows, rows, axis)


def add_cores(keep, send):
    other = exchange(send, 1)
    return keep[0].astype(f32) + other[0].astype(f32), (
        keep[1].astype(f32) + other[1].astype(f32)
    ).astype(bf16)


def add_sides(kept, sent):
    return kept + swap_side(sent).astype(f32)


def add_chips(part, low):
    return part[0] + exchange(low, 2).astype(f32)


def low_planes(part):
    return [part[s].astype(bf16) for s in range(1, part.shape[0])]


def add_planes(part, low):
    total = part[0]
    for s, sent in enumerate(low):
        total = total + exchange(sent, 4 * (s + 1)).astype(f32)
    return total


def spread_planes(low):
    planes = lax.axis_size("ctx") // 4
    return [low] + [exchange(low, 4 * s) for s in range(1, planes)]


def spread_chips(chunks, before=None):
    own = jnp.stack(chunks)
    other = exchange(own, 2)
    sent = [own, other] if before is None else [after(own, before), after(other, before)]
    return [own, other] + [exchange(chunk, 1) for chunk in sent]


def zigzag_perms(count):
    def worker(block):
        return block if block < count else 2 * count - 1 - block

    first = [(owner, worker(2 * owner)) for owner in range(count)]
    second = [(owner, worker(2 * owner + 1)) for owner in range(count)]
    return first, second


def body(
    tokens, memory, token_seg, memory_seg, out_grad,
    in_proj, out_proj, ffn_in, ffn_out, norm_gain, bias_rows, ffn_bias,
):
    count = lax.axis_size("ctx")
    sides = lax.axis_size("fsdp")
    planes = count // 4
    plain = sides != 2
    me = lax.axis_index("ctx")
    side = lax.axis_index("fsdp")
    row_count, width = tokens.shape[1], tokens.shape[2]
    mem_count = memory.shape[1]
    half = row_count // 2
    scale = 1.0 / math.sqrt(width // HEADS)
    factor = scale * math.log2(math.e)
    total = row_count * count
    mem_total = mem_count * count
    near, far = planes // 2, planes - planes // 2

    x_planes = fetch_planes(tokens[0])
    small = jnp.concatenate(
        [norm_gain, bias_rows, ffn_bias.reshape(-1, norm_gain.shape[1])], axis=0
    ).astype(bf16)
    maps_low = jnp.concatenate([in_proj, out_proj], axis=0).astype(bf16)
    up_low, down_low = ffn_in.astype(bf16), ffn_out.astype(bf16)
    if plain:
        small = lax.all_gather(small, "fsdp").astype(f32)
        whole = lax.all_gather(maps_low, "fsdp", axis=1, tiled=True)
        self_maps = (whole,)
        late_maps = (
            whole, lax.all_gather(up_low, "fsdp", axis=0, tiled=True),
            lax.all_gather(down_low, "fsdp", axis=0, tiled=True),
        )
    else:
        small_rows = small.shape[0]
        pad = jnp.zeros((32 - small_rows, small.shape[1]), bf16)
        sent = jnp.concatenate(
            [
                core_part(in_proj[0:3], 1).astype(bf16).reshape(-1, width),
                jnp.concatenate([small, pad], axis=0).reshape(-1, width),
            ],
            axis=0,
        )
        fetched = swap_side(sent)
    x_near = fetch_chips(jnp.stack(x_planes[:near]))
    if not plain:
        ready = after(fetched, x_near[1])
        table_rows = ready[-pad.shape[1] * 32 // width :].reshape(32, -1)[:small_rows]
        small = jnp.stack([small, table_rows])
        small = jnp.where(side == 0, small, small[::-1]).astype(f32)
        self_maps = (maps_low, ready, exchange(ready, 1))
        up_part = core_part(after(ffn_in, sent), 0).astype(bf16)
        late_parts = [
            core_part(in_proj[3:6], 1).astype(bf16).reshape(-1, width),
            core_part(after(out_proj, sent), 1).astype(bf16).reshape(-1, width),
            core_part(after(ffn_out, sent), 0).astype(bf16),
        ]
        late_parts += [
            up_part[:, k * width : (k + 1) * width] for k in range(up_part.shape[1] // width)
        ]
        late_sent = jnp.concatenate(late_parts, axis=0)
        late = swap_side(after(late_sent, fetched))
    started = x_near[0] if plain else fetched
    x_far = fetch_chips(jnp.stack([after(chunk, started) for chunk in x_planes[near:]]))

    perm_first, perm_second = zigzag_perms(count)
    even = me % 2 == 0
    first_sent = small if plain else sent
    rows_in = jnp.stack([after(tokens[0], first_sent, x_near[0]), out_grad[0]])
    one = lax.ppermute(rows_in[:, :half], "ctx", perm_first)
    two = lax.ppermute(rows_in[:, half:], "ctx", perm_second)
    rows_in = jnp.where(
        even, jnp.concatenate([one, two], axis=1), jnp.concatenate([two, one], axis=1)
    )
    x_rows, g_rows = rows_in[0], rows_in[1]

    table = small[:, 0:13].transpose(1, 0, 2).reshape(13, width)
    gains, biases = table[0:3], table[3:13]
    ffn_shift = small[:, 13:].reshape(1, -1)

    m_all = lax.all_gather(memory[0], "ctx", axis=0, tiled=True)

    segs, mem_segs = after(token_seg[0], first_sent), after(memory_seg[0], first_sent)
    step = jnp.arange(half, dtype=jnp.int32)
    row_pos = jnp.concatenate([me * half + step, (2 * count - 1 - me) * half + step])
    row_seg = jnp.concatenate(
        [
            lax.dynamic_slice_in_dim(segs, me * half, half),
            lax.dynamic_slice_in_dim(segs, (2 * count - 1 - me) * half, half),
        ]
    )

    def below(keys, closed):
        hits = keys[None, :] <= row_seg[:, None] if closed else keys[None, :] < row_seg[:, None]
        return jnp.sum(hits, axis=1, dtype=jnp.int32)

    ones = jnp.ones_like(row_pos)
    info = jnp.stack(
        [
            below(segs, False), row_pos, below(mem_segs, False), below(mem_segs, True) - 1,
            below(segs, True) - 1, me * ones, side * ones, ones,
        ]
    )
    cols = info.T

    tile = width // PAIRS
    column = ((PAIRS, row_count, 1), f32)
    square = ((PAIRS, row_count, tile), f32)
    two_squares = ((2, PAIRS, row_count, tile), f32)
    rows_low = ((row_count, width), bf16)
    rows_full = ((row_count, width), f32)
    kv_rows_shape = ((row_count, 2 * width), bf16)

    x_near = fetch_cores(x_near)
    x_near[0] = after(x_near[0], x_far[0], up_low, down_low)
    wide = ((PAIRS, row_count, 2 * tile), f32)
    q_rows, kv_rows, kv_near, w_self, top, weights = call_kernel(
        lambda *refs: first_forward_kernel(
            *refs, factor=factor, planes=near, shards=len(self_maps)
        ),
        (info, x_rows, biases, cols, *self_maps, *x_near),
        (
            rows_low, kv_rows_shape, ((4 * near * row_count, 2 * width), bf16),
            ((3, width, width), bf16), rows_full, rows_full,
        ),
        [wide],
        "first_forward",
        10,
    )
    x_far = fetch_cores([after(chunks, top) for chunks in x_far])
    a_rows, log_rows, kv_far = call_kernel(
        lambda *refs: second_forward_kernel(*refs, factor=factor, planes=far),
        (info, kv_near, q_rows, biases, cols, w_self, top, weights, *x_far),
        (rows_full, ((HEADS, row_count), f32), ((4 * far * row_count, 2 * width), bf16)),
        [
            wide, column, column, square, rows_full, ((4 * near * row_count, 2 * width), bf16),
            pltpu.SemaphoreType.DMA,
        ],
        "second_forward",
        10,
        (1,),
    )
    if not plain:
        late = after(late, a_rows)
        late_maps = (maps_low, up_low, down_low, late, exchange(late, 1))
    ff_width = ffn_in.shape[1]
    ff_rows = ((row_count, ff_width), bf16)
    by_head = ((HEADS, row_count), f32)
    kvc_shape = ((mem_total, 2 * width), bf16)
    sums_shape = ((16, width), f32)
    whole_maps = [] if plain else [((width, ff_width), bf16), ((ff_width, width), bf16)]
    (
        out_rows, a_low, h1_low, h2_low, act, e3, gu, e2, ac_low, gr2, r1, qc, cross, cross_log,
        kvc, sums, csum, w_cross,
    ) = call_kernel(
        lambda *refs: middle_forward_kernel(
            *refs, factor=factor, shards=len(self_maps), cross_rows=2 * mem_count
        ),
        (info, x_rows, a_rows, g_rows, cols, gains, biases, ffn_shift, m_all, *late_maps),
        (
            rows_full, rows_low, rows_low, rows_low, ff_rows, rows_low, ff_rows, rows_low, rows_low,
            rows_full, rows_full, rows_low, rows_full, by_head, kvc_shape, sums_shape,
            ((1, ff_width), f32), ((5, width, width), bf16),
        ),
        [wide, column, column, square, rows_full, *whole_maps],
        "middle_forward",
        25,
    )

    def sink_shapes(blocks):
        if plain:
            return [((blocks, width, width), bf16)]
        return [((2, 2, planes, blocks * (half_rows // count), width), bf16)] * 2

    feed = call_kernel(
        lambda *refs: feed_grads_kernel(*refs, plain=plain),
        (info, h2_low, gu, act, e3),
        sink_shapes(8),
        [((ff_width, width), f32)],
        "feed_grads",
        5,
    )
    gr2 = after(gr2, *feed)
    e1, dqc, ga, gr1, delta, dkvc, sums = call_kernel(
        lambda *refs: middle_backward_kernel(
            *refs, factor=factor, scale=scale, cross_rows=2 * mem_count
        ),
        (
            info, a_rows, log_rows, info, gains, w_cross, e2, gr2, r1, qc, cross, cross_log, kvc,
            sums,
        ),
        (
            rows_low, rows_low, ((row_count + chunk_rows, width), bf16), rows_full, by_head,
            kvc_shape, sums_shape,
        ),
        [((PAIRS, tile, row_count), f32)],
        "middle_backward",
        14,
    )
    g_planes = fetch_planes(ga)
    if not plain:
        feed = add_cores(*feed)
        dkvc = after(dkvc, feed[1])
    mem_part, dwc = call_kernel(
        lambda *refs: memory_grads_kernel(*refs, cross_block=2 * mem_count),
        (info, m_all, w_cross, dkvc),
        (((mem_total, width), bf16), ((width, 2 * width), bf16)),
        [((width, 2 * width), f32)],
        "memory_grads",
        5,
    )
    g_near = fetch_chips(jnp.stack([after(chunk, mem_part) for chunk in g_planes[:near]]))
    (dq,) = call_kernel(
        lambda *refs: query_backward_kernel(*refs, factor=factor, scale=scale, planes=near),
        (info, after(q_rows, g_near[0]), ga, kv_near, kv_far, log_rows, delta, cols),
        (rows_low,),
        [square, square, square],
        "query_backward",
        20,
    )
    g_far = fetch_chips(jnp.stack([after(chunk, dq) for chunk in g_planes[near:]]))
    g_near = fetch_cores([after(chunks, dq) for chunks in g_near])
    maps = call_kernel(
        lambda *refs: map_grads_kernel(*refs, plain=plain),
        (info, a_low, e1, ac_low, e2, after(h1_low, g_far[0], g_near[1]), dqc, dwc, x_rows, dq, sums, csum),
        sink_shapes(7),
        [((width, width), f32)],
        "map_grads",
        6,
    )
    (q_all,) = call_kernel(
        lambda *refs: project_kernel(*refs, planes=near),
        (info, after(w_self, maps[0]), biases, *x_near, *x_far),
        (((total, width), bf16),),
        [],
        "project",
        7,
    )
    if not plain:
        maps = add_cores(*maps)
        feed = add_sides(*feed)
        feed_low = feed[1].astype(bf16)
        kv_rows = after(kv_rows, maps[1], feed_low)
    mem_part = after(mem_part, g_far[1])
    memory_grad = lax.psum_scatter(mem_part, "ctx", scatter_dimension=0, tiled=True).astype(f32)
    g_far = fetch_cores([after(chunks, q_all) for chunks in g_far])
    dk_part, dv_part = call_kernel(
        lambda *refs: key_backward_kernel(
            *refs, factor=factor, scale=scale, planes=near, part=0, last=False,
            total_planes=planes,
        ),
        (info, kv_rows, q_all, cols, *g_near),
        [two_squares, two_squares],
        [
            ((4 * near * row_count, width), bf16), ((8 * near, 2 * HEADS, half), f32),
        ],
        "key_backward",
        8,
    )
    if not plain:
        feed = add_chips(feed, feed_low)
        feed_low = low_planes(feed)
        dk_part = after(dk_part, *feed_low)
    dk, dv = call_kernel(
        lambda *refs: key_backward_kernel(
            *refs, factor=factor, scale=scale, planes=far, part=1, last=True, total_planes=planes
        ),
        (info, kv_rows, q_all, cols, dk_part, dv_part, *g_far),
        [rows_low, rows_low],
        [
            ((4 * far * row_count, width), bf16), ((8 * far, 2 * HEADS, half), f32),
            two_squares, two_squares,
        ],
        "key_backward_last",
        12,
    )
    if not plain:
        feed = add_planes(feed, feed_low).astype(bf16)
        maps = add_sides(*maps)
        maps_low = maps[1].astype(bf16)
        dk = after(dk, feed, maps_low)
    tok_rows, *last = call_kernel(
        lambda *refs: self_grads_kernel(*refs, plain=plain),
        (info, x_rows, gr1, dq, dk, dv, w_self),
        [rows_low] + sink_shapes(2),
        [((width, width), f32)],
        "self_grads",
        4,
    )

    back_first = [(to, owner) for owner, to in perm_first]
    back_second = [(to, owner) for owner, to in perm_second]

    rows_out = jnp.stack([out_rows.astype(bf16), tok_rows])
    half_one = jnp.where(even, rows_out[:, :half], rows_out[:, half:])
    half_two = jnp.where(even, rows_out[:, half:], rows_out[:, :half])
    rows_out = jnp.concatenate(
        [lax.ppermute(half_one, "ctx", back_first), lax.ppermute(half_two, "ctx", back_second)],
        axis=1,
    ).astype(f32)
    layer_out, tokens_grad = rows_out[0], rows_out[1]
    lanes = width // 2
    if plain:

        def owned(matrix, axis):
            part = lax.psum_scatter(matrix, "fsdp", scatter_dimension=axis, tiled=True)
            return lax.psum(part, "ctx").astype(f32)

        feed, maps, last = feed[0], maps[0], last[0]
        ins = owned(jnp.concatenate([maps[5:6], last, maps[2:5]], axis=0), 1)
        outs = owned(maps[0:2], 1)
        up = owned(jnp.concatenate([feed[k] for k in range(4)], axis=1), 0)
        down = owned(feed[4:8].reshape(-1, width), 0)
        rest = jnp.stack([maps[6, 0:half_rows, 0:lanes], maps[6, half_rows:, 0:lanes]], axis=1)
        table = owned(rest[0:13].reshape(13, width).astype(f32), 1)
        shift = owned(rest[16:20].transpose(1, 0, 2).reshape(-1).astype(f32), 0)
        gain_sums, bias_sums = table[0:3], table[3:13]
    else:
        feed_planes = spread_planes(feed)
        last = add_sides(*add_cores(*last))
        last_low = after(last[1].astype(bf16), *feed_planes[1:])
        feed_own = jnp.stack(feed_planes)
        feed_other = exchange(feed_own, 2)
        last = add_chips(last, last_low)
        maps = add_chips(maps, maps_low)
        maps = add_planes(maps, low_planes(maps)).astype(bf16)
        last = add_planes(last, [after(low, maps) for low in low_planes(last)]).astype(bf16)
        up, down = call_kernel(
            lambda *refs: place_kernel(
                *refs,
                places=[(0, "cols", k) for k in range(4)] + [(1, "rows", k) for k in range(4)],
            ),
            (info, feed_own, feed_other, exchange(feed_own, 1), exchange(feed_other, 1)),
            ((ffn_in.shape, f32), (ffn_out.shape, f32)),
            [],
            "place_feed",
            4,
        )
        maps = jnp.concatenate([maps, after(last, feed_other)], axis=0)
        ins, outs, gain_sums, bias_sums, shift = call_kernel(
            place_maps_kernel,
            (info, *spread_chips(spread_planes(maps), up)),
            (
                (in_proj.shape, f32), (out_proj.shape, f32), ((3, lanes), f32), ((10, lanes), f32),
                ((4, lanes), f32),
            ),
            [((half_rows, width), f32)],
            "place_maps",
            4,
        )
        shift = shift.reshape(-1)
    return (
        layer_out[None], tokens_grad[None], memory_grad[None], ins, outs, up, down,
        gain_sums, bias_sums, shift,
    )


def solution(mesh):
    rows = P("fsdp", "ctx", None)
    params = (
        P(None, "fsdp", None), P(None, "fsdp", None), P("fsdp", None), P("fsdp", None),
        P(None, "fsdp"), P(None, "fsdp"), P("fsdp"),
    )
    return jax.shard_map(
        body,
        mesh=mesh,
        in_specs=(rows, rows, P("fsdp", None), P("fsdp", None), rows) + params,
        out_specs=(rows, rows, rows) + params,
        check_vma=False,
    )
```

```python
import math

import jax
import jax.numpy as jnp
from jax import lax
from jax.experimental import pallas as pl
from jax.experimental.pallas import tpu as pltpu
from jax.sharding import PartitionSpec as P

HEADS = 8
PAIRS = HEADS // 2
neg_fill = -1e30
eps_norm = 1e-05
self_block = 512
bf16 = jnp.bfloat16
f32 = jnp.float32
vmem_bytes = 60 * 1024 * 1024
half_rows = 256
chunk_rows = 32


def dot_nn(first_op, second_op):
    return jnp.dot(first_op, second_op, preferred_element_type=f32)


def dot_nt(first_op, second_op):
    return lax.dot_general(
        first_op, second_op, (((1,), (1,)), ((), ())), preferred_element_type=f32
    )


def dot_tn(first_op, second_op):
    return lax.dot_general(
        first_op, second_op, (((0,), (0,)), ((), ())), preferred_element_type=f32
    )


def stack_heads(tile):
    lane = lax.broadcasted_iota(jnp.int32, tile.shape, 1)
    half = tile.shape[1] // 2
    zero = jnp.zeros_like(tile)
    return jnp.concatenate(
        [jnp.where(lane < half, tile, zero), jnp.where(lane >= half, tile, zero)], axis=0
    )


def merge_heads(stacked):
    rows = stacked.shape[0] // 2
    lane = lax.broadcasted_iota(jnp.int32, (rows, stacked.shape[1]), 1)
    return jnp.where(lane < stacked.shape[1] // 2, stacked[:rows], stacked[rows:])


def tile_of(value, pair, tile_width):
    return value[:, pair * tile_width : (pair + 1) * tile_width]


def head_sums(product):
    width = product.shape[1]
    head = lax.broadcasted_iota(jnp.int32, (HEADS, width), 0)
    lane = lax.broadcasted_iota(jnp.int32, (HEADS, width), 1)
    pick = (lane // (width // HEADS) == head).astype(f32)
    return lax.dot_general(
        pick,
        product,
        (((1,), (1,)), ((), ())),
        precision=lax.Precision.HIGHEST,
        preferred_element_type=f32,
    )


def over_range(first, last):
    def run(step):
        def visit(index, carry):
            step(index, index)
            return carry

        lax.fori_loop(first, last, visit, 0)

    return run


def over_planes(info, plane_first, plane_count, first, last):
    def run(step):
        def visit(stored, carry):
            index = 2 * (info.plane ^ (plane_first + (stored >> 1))) + (stored & 1)

            @pl.when((index >= first) & (index < last))
            def _():
                step(stored, index)

            return carry

        lax.fori_loop(0, 2 * plane_count, visit, 0)

    return run


class RowInfo:
    def __init__(self, info_ref):
        self.table = info_ref
        self.half = info_ref.shape[1] // 2
        self.me = info_ref[5, 0]
        self.side = info_ref[6, 0]
        self.plane = self.me >> 2

    def ends(self, block):
        return block * self.half, (block + 1) * self.half - 1

    def self_keys(self, block):
        start, stop = self.ends(block)
        return self.table[0, start] // self_block, self.table[1, stop] // self_block + 1

    def cross_keys(self, block, size):
        start, stop = self.ends(block)
        return self.table[2, start] // size, self.table[3, stop] // size + 1

    def queries(self, block):
        start, stop = self.ends(block)
        return self.table[1, start] // self_block, self.table[4, stop] // self_block + 1


def twice(column):
    return jnp.concatenate([column, column], axis=0)


def stacked_tiles(rows):
    tile_width = rows.shape[1] // PAIRS
    return [stack_heads(tile_of(rows, pair, tile_width)) for pair in range(PAIRS)]


def attend_plain(q_block, kv_ref, low_col, high_col, run, key_rows, factor, acc_ref):
    width = q_block.shape[1]
    tile_width = width // PAIRS
    stacked = stacked_tiles(q_block)
    low2, high2 = twice(low_col), twice(high_col)
    ones = jnp.ones((key_rows, tile_width), bf16)

    def step(stored, index):
        base = pl.multiple_of(stored * key_rows, key_rows)
        key_pos = index * key_rows + lax.broadcasted_iota(jnp.int32, (1, key_rows), 1)
        allowed = (key_pos >= low2) & (key_pos <= high2)
        def read(pair, offset):
            start = offset + pair * tile_width
            return kv_ref[pl.ds(base, key_rows), start : start + tile_width]

        scores = [dot_nt(stacked[0], read(0, 0))]
        for pair in range(PAIRS):
            if pair + 1 < PAIRS:
                scores.append(dot_nt(stacked[pair + 1], read(pair + 1, 0)))
            weights = jnp.where(allowed, jnp.exp2(scores[pair] * factor), 0.0).astype(bf16)
            acc_ref[pair] += dot_nn(weights, jnp.concatenate([read(pair, width), ones], axis=1))

    run(step)


def weighted_rows(acc_ref):
    tile_width = acc_ref.shape[2] // 2
    tops = [merge_heads(acc_ref[pair, :, 0:tile_width]) for pair in range(PAIRS)]
    sums = [merge_heads(acc_ref[pair, :, tile_width:]) for pair in range(PAIRS)]
    return jnp.concatenate(tops, axis=1), jnp.concatenate(sums, axis=1)


def in_range(sums):
    return (jnp.min(sums) > 2.0**-100) & (jnp.max(sums) < 2.0**100)


def attend_running(q_block, parts, low_col, high_col, key_rows, factor, scratch):
    max_ref, sum_ref, acc_ref = scratch
    width = q_block.shape[1]
    tile_width = width // PAIRS
    stacked = stacked_tiles(q_block)
    low2, high2 = twice(low_col), twice(high_col)
    max_ref[...] = jnp.full(max_ref.shape, neg_fill, f32)
    sum_ref[...] = jnp.zeros(sum_ref.shape, f32)
    acc_ref[...] = jnp.zeros(acc_ref.shape, f32)
    for kv_ref, run in parts:

        def step(stored, index, kv_ref=kv_ref):
            base = pl.multiple_of(stored * key_rows, key_rows)
            key_pos = index * key_rows + lax.broadcasted_iota(jnp.int32, (1, key_rows), 1)
            allowed = (key_pos >= low2) & (key_pos <= high2)
            for pair in range(PAIRS):
                start = pair * tile_width
                keys = kv_ref[pl.ds(base, key_rows), start : start + tile_width]
                values = kv_ref[pl.ds(base, key_rows), width + start : width + start + tile_width]
                scores = jnp.where(allowed, dot_nt(stacked[pair], keys), neg_fill)
                old_max = max_ref[pair]
                new_max = jnp.maximum(old_max, jnp.max(scores, axis=1, keepdims=True))
                probs = jnp.exp2((scores - new_max) * factor)
                rescale = jnp.exp2((old_max - new_max) * factor)
                sum_ref[pair] = sum_ref[pair] * rescale + jnp.sum(probs, axis=1, keepdims=True)
                acc_ref[pair] = acc_ref[pair] * rescale + dot_nn(probs.astype(bf16), values)
                max_ref[pair] = new_max

        run(step)
    outputs, logs = [], []
    for pair in range(PAIRS):
        outputs.append(merge_heads(acc_ref[pair] / sum_ref[pair]))
        column = max_ref[pair] * factor + jnp.log2(sum_ref[pair])
        logs.append(merge_heads(jnp.broadcast_to(column, acc_ref.shape[1:])))
    return jnp.concatenate(outputs, axis=1), jnp.concatenate(logs, axis=1)


def log_rows_of(lane_logs):
    return head_sums(lane_logs) * (HEADS / lane_logs.shape[1])


def query_grads(
    q_block, g_block, kv_ref, low_col, high_col, log_ref, delta_ref, run, key_rows, factor, acc_ref
):
    width = q_block.shape[1]
    tile_width = width // PAIRS
    q2, g2 = stacked_tiles(q_block), stacked_tiles(g_block)
    low2, high2 = twice(low_col), twice(high_col)

    def step(stored, index):
        base = pl.multiple_of(stored * key_rows, key_rows)
        key_pos = index * key_rows + lax.broadcasted_iota(jnp.int32, (1, key_rows), 1)
        allowed = (key_pos >= low2) & (key_pos <= high2)
        def read(pair, offset):
            start = offset + pair * tile_width
            return kv_ref[pl.ds(base, key_rows), start : start + tile_width]

        def products(pair):
            return dot_nt(q2[pair], read(pair, 0)), dot_nt(g2[pair], read(pair, width))

        ahead = products(0)
        repeats = key_rows // log_ref.shape[2]
        for pair in range(PAIRS):
            scores, prob_grad = ahead
            if pair + 1 < PAIRS:
                ahead = products(pair + 1)
            logs = jnp.concatenate([log_ref[pair]] * repeats, axis=1)
            deltas = jnp.concatenate([delta_ref[pair]] * repeats, axis=1)
            probs = jnp.where(allowed, jnp.exp2(scores * factor - logs), 0.0)
            score_grad = (probs * (prob_grad - deltas)).astype(bf16)
            acc_ref[pair] += dot_nn(score_grad, read(pair, 0))

    run(step)


def key_grads(k_block, v_block, q_ref, g_ref, stats_ref, low_col, high_col, run, factor, dk_ref, dv_ref):
    width = k_block.shape[1]
    tile_width = width // PAIRS
    rows = k_block.shape[0]
    query_rows = self_block
    blocks = query_rows // rows
    k2, v2 = stacked_tiles(k_block), stacked_tiles(v_block)
    low2, high2 = twice(low_col), twice(high_col)

    def step(stored, index):
        base = pl.multiple_of(stored * query_rows, query_rows)
        q_base = pl.multiple_of(index * query_rows, query_rows)
        query_pos = q_base + lax.broadcasted_iota(jnp.int32, (1, query_rows), 1)
        allowed = (query_pos >= low2) & (query_pos <= high2)
        stats = jnp.concatenate([stats_ref[stored * blocks + u] for u in range(blocks)], axis=1)

        def two_rows(first_row):
            return jnp.concatenate(
                [
                    jnp.broadcast_to(stats[first_row : first_row + 1], (rows, query_rows)),
                    jnp.broadcast_to(stats[first_row + 1 : first_row + 2], (rows, query_rows)),
                ],
                axis=0,
            )

        def read(ref, start, pair):
            return ref[pl.ds(start, query_rows), pair * tile_width : (pair + 1) * tile_width]

        def products(pair):
            return dot_nt(k2[pair], read(q_ref, q_base, pair)), dot_nt(v2[pair], read(g_ref, base, pair))

        ahead = products(0)
        for pair in range(PAIRS):
            scores, prob_grad = ahead
            if pair + 1 < PAIRS:
                ahead = products(pair + 1)
            probs = jnp.where(allowed, jnp.exp2(scores * factor - two_rows(2 * pair)), 0.0)
            score_grad = (probs * (prob_grad - two_rows(HEADS + 2 * pair))).astype(bf16)
            dk_ref[pair] += dot_nn(score_grad, read(q_ref, q_base, pair))
            dv_ref[pair] += dot_nn(probs.astype(bf16), read(g_ref, base, pair))

    run(step)


def merged_rows(acc_ref):
    return jnp.concatenate([merge_heads(acc_ref[pair]) for pair in range(PAIRS)], axis=1)


def chunk_views(piece_refs, planes):
    for s in range(planes):
        for bits in range(4):
            yield s, bits, piece_refs[(bits >> 1) + 2 * (bits & 1)].at[s]


def fill_rows(target, parts, info, skip=0, lead=0):
    own, fetched, other = parts
    rows = own.shape[-2]
    core = info.me & 1
    starts = (
        info.side * rows,
        (1 - info.side) * rows + core * (rows // 2),
        (1 - info.side) * rows + (1 - core) * (rows // 2),
    )
    for number, (part, start) in enumerate(zip((own, fetched, other), starts)):
        size = rows // 2 if number else rows
        at = pl.ds(pl.multiple_of(start, rows // 2), size)
        if len(target.shape) == 3:
            for k in range(target.shape[0]):
                first = skip + k * size
                window = part[first : first + size] if number else part[lead + k]
                target[k, at, :] = window.astype(bf16)
        elif target.shape[1] == part.shape[1]:
            target[at, :] = (part[skip : skip + size] if number else part[...]).astype(bf16)
        elif not number:
            target[at, :] = part[...].astype(bf16)
        else:
            width = part.shape[1]
            for k in range(target.shape[1] // width):
                first = skip + k * size
                target[at, k * width : (k + 1) * width] = part[first : first + size]


def attend_back(
    q_block, g_block, kv_ref, dkv_ref, low_row, high_row, log_rows, delta_rows,
    first, last, key_rows, factor, scale, dq_ref, adding,
):
    width = q_block.shape[1]
    tile_width = width // PAIRS
    rows = q_block.shape[0]
    q2 = [stack_heads(tile_of(q_block, pair, tile_width)) for pair in range(PAIRS)]
    g2 = [stack_heads(tile_of(g_block, pair, tile_width)) for pair in range(PAIRS)]
    low2 = jnp.concatenate([low_row, low_row], axis=1)
    high2 = jnp.concatenate([high_row, high_row], axis=1)
    dq_ref[...] = jnp.zeros(dq_ref.shape, f32)

    def step(index, carry):
        base = pl.multiple_of(index * key_rows, key_rows)
        key_pos = base + lax.broadcasted_iota(jnp.int32, (key_rows, 1), 0)
        allowed = (key_pos >= low2) & (key_pos <= high2)
        for pair in range(PAIRS):
            key_at = (pl.ds(base, key_rows), slice(pair * tile_width, (pair + 1) * tile_width))
            value_at = (
                pl.ds(base, key_rows),
                slice(width + pair * tile_width, width + (pair + 1) * tile_width),
            )
            keys = kv_ref[key_at]
            values = kv_ref[value_at]
            scores = dot_nt(keys, q2[pair])
            probs = jnp.where(allowed, jnp.exp2(scores * factor - log_rows[pair]), 0.0)
            prob_grad = dot_nt(values, g2[pair])
            score_grad = (probs * (prob_grad - delta_rows[pair])).astype(bf16)
            key_grad = dot_nn(score_grad, q2[pair]) * scale
            value_grad = dot_nn(probs.astype(bf16), g2[pair])
            if adding:
                key_grad = key_grad + dkv_ref[key_at].astype(f32)
                value_grad = value_grad + dkv_ref[value_at].astype(f32)
            dkv_ref[key_at] = key_grad.astype(bf16)
            dkv_ref[value_at] = value_grad.astype(bf16)
            dq_ref[pair] += dot_tn(keys, score_grad)
        return carry

    lax.fori_loop(first, last, step, 0)
    tiles = []
    for pair in range(PAIRS):
        both = dq_ref[pair]
        feature = lax.broadcasted_iota(jnp.int32, (tile_width, rows), 0)
        picked = jnp.where(feature < tile_width // 2, both[:, :rows], both[:, rows:])
        tiles.append(jnp.transpose(picked) * scale)
    return jnp.concatenate(tiles, axis=1)


def split_three(value):
    one = value.astype(bf16)
    rest = value - one.astype(f32)
    two = rest.astype(bf16)
    three = (rest - two.astype(f32)).astype(bf16)
    return [one, two, three]


def side_by_side(stats):
    rows = stats.shape[0] // 2
    return jnp.concatenate([stats[:rows], stats[rows:]], axis=1)


class PieceSink:
    def __init__(self, keep_ref, send_ref, scratch_ref, me, side):
        self.keep, self.send, self.scratch, self.me, self.side = keep_ref, send_ref, scratch_ref, me, side

    def emit(self, block, stride, offset):
        planes = self.keep.shape[2]
        piece = half_rows // (4 * planes)
        at = slice(block * piece, (block + 1) * piece)
        for s in range(planes):
            for bits in range(4):
                dc, dx = bits & 1, bits >> 1
                owner = self.me ^ (4 * s + bits)
                for fy in range(2):
                    source = (self.side ^ fy) * stride + offset + owner * piece
                    rows = self.scratch[pl.ds(pl.multiple_of(source, piece), piece), :]
                    target = self.send if dc else self.keep
                    target[fy, dx, s, at, :] = rows.astype(bf16)

    def put(self, block, matrix):
        rows = matrix.shape[0]
        self.scratch[0:rows, :] = matrix.astype(f32)
        blocks = rows // (2 * half_rows)
        for b in range(blocks):
            self.emit(block + b, rows // 2, b * half_rows)


class PlainSink:
    def __init__(self, plain_ref):
        self.plain = plain_ref

    def put(self, block, matrix):
        size = 2 * half_rows
        for b in range(matrix.shape[0] // size):
            self.plain[block + b] = matrix[b * size : (b + 1) * size].astype(bf16)


def pair_rows(by_head, block, rows, pair):
    at = slice(block * rows, (block + 1) * rows)
    return jnp.concatenate(
        [by_head[2 * pair : 2 * pair + 1, at], by_head[2 * pair + 1 : 2 * pair + 2, at]], axis=1
    )


def norm_stats(residual):
    centre = residual - jnp.mean(residual, axis=1, keepdims=True)
    spread = jnp.mean(centre * centre, axis=1, keepdims=True)
    inverse = lax.rsqrt(spread + eps_norm)
    return centre * inverse, inverse


def norm_back(normed, inverse, gain_row, upstream):
    scaled = upstream * gain_row
    mean_one = jnp.mean(scaled, axis=1, keepdims=True)
    mean_two = jnp.mean(scaled * normed, axis=1, keepdims=True)
    return (scaled - mean_one - normed * mean_two) * inverse


def column_sum(matrix):
    return jnp.sum(matrix.astype(f32), axis=0, keepdims=True)


def piece_rows(pieces):
    for bits in range(4):
        ref = pieces[(bits >> 1) + 2 * (bits & 1)]
        yield bits, ref[...].reshape(ref.shape[0] * ref.shape[1], ref.shape[2])


def project_chunks(pieces, planes, kv_ref, w_ref, shift, info):
    width = w_ref.shape[2]
    rows = pieces[0].shape[1]
    for bits, block in piece_rows(pieces):
        keys = dot_nn(block, w_ref[1]).astype(bf16)
        values = (dot_nn(block, w_ref[2]) + shift).astype(bf16)
        for s in range(planes):
            start = 4 * rows * s + rows * ((info.me & 3) ^ bits)
            at = pl.ds(pl.multiple_of(start, rows), rows)
            kv_ref[at, 0:width] = keys[s * rows : (s + 1) * rows]
            kv_ref[at, width:] = values[s * rows : (s + 1) * rows]


def first_forward_kernel(info_ref, x_ref, bias_ref, cols_ref, *refs, factor, planes, shards):
    maps, refs = refs[:shards], refs[shards:]
    pieces, refs = refs[:4], refs[4:]
    q_ref, kv_rows_ref, kv_ref, w_ref, top_ref, sums_ref, acc_ref = refs
    info = RowInfo(info_ref)
    width = x_ref.shape[1]
    half = info.half
    if shards == 1:
        w_ref[...] = maps[0][0:3]
    else:
        fill_rows(w_ref, maps, info)
    shift = bias_ref[1:2, :]
    project_chunks(pieces, planes, kv_ref, w_ref, shift, info)
    x_rows = x_ref[...]
    q_rows = (dot_nn(x_rows, w_ref[0]) + bias_ref[0:1, :]).astype(bf16)
    q_ref[...] = q_rows
    kv_rows_ref[:, 0:width] = dot_nn(x_rows, w_ref[1]).astype(bf16)
    kv_rows_ref[:, width:] = (dot_nn(x_rows, w_ref[2]) + shift).astype(bf16)
    for block in range(2):
        at = slice(block * half, (block + 1) * half)
        acc_ref[...] = jnp.zeros(acc_ref.shape, f32)
        run = over_planes(info, 0, planes, *info.self_keys(block))
        attend_plain(
            q_rows[at], kv_ref, cols_ref[at, 0:1], cols_ref[at, 1:2], run, self_block, factor, acc_ref
        )
        top_ref[at, :], sums_ref[at, :] = weighted_rows(acc_ref)


def second_forward_kernel(
    info_ref, kv_near_ref, q_in_ref, bias_ref, cols_ref, w_ref, top_ref, sums_ref, *refs,
    factor, planes,
):
    pieces, refs = refs[:4], refs[4:]
    a_ref, log_ref, kv_ref, acc_ref, max_ref, sum_ref, run_ref, lane_ref, near_ref, near_sem = refs
    info = RowInfo(info_ref)
    half = info.half
    project_chunks(pieces, planes, kv_ref, w_ref, bias_ref[1:2, :], info)
    fine = None
    for block in range(2):
        at = slice(block * half, (block + 1) * half)
        acc_ref[...] = jnp.zeros(acc_ref.shape, f32)
        run = over_planes(info, planes, planes, *info.self_keys(block))
        attend_plain(
            q_in_ref[at, :], kv_ref, cols_ref[at, 0:1], cols_ref[at, 1:2], run, self_block, factor,
            acc_ref,
        )
        top, sums = weighted_rows(acc_ref)
        sums = sums + sums_ref[at, :]
        a_ref[at, :] = (top + top_ref[at, :]) / sums
        lane_ref[at, :] = jnp.log2(sums)
        fine = in_range(sums) if fine is None else fine & in_range(sums)

    @pl.when(jnp.logical_not(fine))
    def _():
        copy = pltpu.make_async_copy(kv_near_ref, near_ref, near_sem)
        copy.start()
        copy.wait()
        for block in range(2):
            at = slice(block * half, (block + 1) * half)
            keys = info.self_keys(block)
            a_ref[at, :], lane_ref[at, :] = attend_running(
                q_in_ref[at, :],
                [
                    (near_ref, over_planes(info, 0, planes, *keys)),
                    (kv_ref, over_planes(info, planes, planes, *keys)),
                ],
                cols_ref[at, 0:1], cols_ref[at, 1:2], self_block, factor, (max_ref, sum_ref, run_ref),
            )

    log_ref[...] = log_rows_of(lane_ref[...])


def project_kernel(info_ref, w_ref, bias_ref, *refs, planes):
    pieces, (q_ref,) = refs[:8], refs[8:]
    info = RowInfo(info_ref)
    for part in range(2):
        for bits, block in piece_rows(pieces[4 * part : 4 * part + 4]):
            queries = (dot_nn(block, w_ref[0]) + bias_ref[0:1, :]).astype(bf16)
            rows = pieces[0].shape[1]
            for s in range(planes):
                place = info.me ^ (4 * (part * planes + s) + bits)
                at = pl.ds(pl.multiple_of(place * rows, rows), rows)
                q_ref[at, :] = queries[s * rows : (s + 1) * rows]


def middle_forward_kernel(
    info_ref, x_ref, a_ref, g_ref, cols_ref, gain_ref, bias_ref, ffn_bias_ref, mem_ref, *refs,
    factor, shards, cross_rows,
):
    late, refs = (refs[:3], refs[3:]) if shards == 1 else (refs[:5], refs[5:])
    (
        out_ref, a_low_ref, h1_ref, h2_ref, f_ref, e3_ref, gu_ref, e2_ref, ac_ref, gr2_ref, r1_ref,
        qc_ref, cross_ref, cross_log_ref, kvc_ref, sums_ref, csum_ref, wc_ref,
        acc_ref, max_ref, sum_ref, run_ref, lane_ref, *whole_refs,
    ) = refs
    info = RowInfo(info_ref)
    if shards == 1:
        maps_ref, u_ref, v_ref = late
        wc_ref[...] = maps_ref[3:8]
    else:
        maps_ref, up_ref, down_ref, one, two = late
        u_ref, v_ref = whole_refs
        size = maps_ref.shape[1] // 2
        fill_rows(wc_ref, (maps_ref, one, two), info, 0, 3)
        fill_rows(v_ref, (down_ref, one, two), info, 5 * size)
        fill_rows(u_ref, (up_ref, one, two), info, 5 * size + down_ref.shape[0] // 2)
    rows, width = x_ref.shape
    half = rows // 2
    cross_block = cross_rows
    cross_range = [info.cross_keys(block, cross_block) for block in range(2)]
    live_first = jnp.minimum(cross_range[0][0], cross_range[1][0])
    live_last = jnp.maximum(cross_range[0][1], cross_range[1][1])

    def project(index, carry):
        at = pl.ds(pl.multiple_of(index * cross_block, cross_block), cross_block)
        block = mem_ref[at, :]
        kvc_ref[at, 0:width] = dot_nn(block, wc_ref[1]).astype(bf16)
        kvc_ref[at, width:] = (dot_nn(block, wc_ref[2]) + bias_ref[5:6, :]).astype(bf16)
        return carry

    lax.fori_loop(live_first, live_last, project, 0)
    attn_self = a_ref[...]
    a_low = attn_self.astype(bf16)
    a_low_ref[...] = a_low
    r1 = x_ref[...].astype(f32) + (dot_nn(a_low, wc_ref[3]) + bias_ref[2:3, :])
    r1_ref[...] = r1
    n1, inv1 = norm_stats(r1)
    h1 = n1 * gain_ref[0:1, :] + bias_ref[3:4, :]
    h1_low = h1.astype(bf16)
    h1_ref[...] = h1_low
    qc = (dot_nn(h1_low, wc_ref[0]) + bias_ref[4:5, :]).astype(bf16)
    qc_ref[...] = qc
    fine = None
    for block in range(2):
        at = slice(block * half, (block + 1) * half)
        acc_ref[...] = jnp.zeros(acc_ref.shape, f32)
        attend_plain(
            qc[at], kvc_ref, cols_ref[at, 2:3], cols_ref[at, 3:4], over_range(*cross_range[block]),
            cross_block, factor, acc_ref,
        )
        top, weights = weighted_rows(acc_ref)
        cross_ref[at, :] = top / weights
        lane_ref[at, :] = jnp.log2(weights)
        fine = in_range(weights) if fine is None else fine & in_range(weights)

    @pl.when(jnp.logical_not(fine))
    def _():
        for block in range(2):
            at = slice(block * half, (block + 1) * half)
            cross_ref[at, :], lane_ref[at, :] = attend_running(
                qc_ref[at, :], [(kvc_ref, over_range(*cross_range[block]))],
                cols_ref[at, 2:3], cols_ref[at, 3:4], cross_block, factor, (max_ref, sum_ref, run_ref),
            )

    cross_log_ref[...] = log_rows_of(lane_ref[...])
    attn_cross = cross_ref[...]
    ac_low = attn_cross.astype(bf16)
    ac_ref[...] = ac_low
    r2 = h1 + (dot_nn(ac_low, wc_ref[4]) + bias_ref[6:7, :])
    n2, inv2 = norm_stats(r2)
    h2 = n2 * gain_ref[1:2, :] + bias_ref[7:8, :]
    h2_low = h2.astype(bf16)
    h2_ref[...] = h2_low
    u = dot_nn(h2_low, u_ref[...]) + ffn_bias_ref[...]
    sig = 1.0 / (1.0 + jnp.exp(-u))
    act = (u / (1.0 + jnp.exp(-u))).astype(bf16)
    f_ref[...] = act
    slope = sig * (1.0 + u * (1.0 - sig))
    r3 = h2 + (dot_nn(act, v_ref[...]) + bias_ref[8:9, :])
    n3, inv3 = norm_stats(r3)
    out_ref[...] = n3 * gain_ref[2:3, :] + bias_ref[9:10, :]
    sums_ref[...] = jnp.zeros_like(sums_ref)
    upstream = g_ref[...].astype(f32)
    sums_ref[2:3, :] = column_sum(upstream * n3)
    sums_ref[12:13, :] = column_sum(upstream)
    gr3 = norm_back(n3, inv3, gain_ref[2:3, :], upstream)
    e3 = gr3.astype(bf16)
    e3_ref[...] = e3
    sums_ref[11:12, :] = column_sum(e3)
    gu = (dot_nt(e3, v_ref[...]) * slope).astype(bf16)
    gu_ref[...] = gu
    csum_ref[...] = column_sum(gu)
    gh2 = gr3 + dot_nt(gu, u_ref[...])
    sums_ref[1:2, :] = column_sum(gh2 * n2)
    sums_ref[10:11, :] = column_sum(gh2)
    gr2 = norm_back(n2, inv2, gain_ref[1:2, :], gh2)
    gr2_ref[...] = gr2
    e2 = gr2.astype(bf16)
    e2_ref[...] = e2
    sums_ref[9:10, :] = column_sum(e2)


def middle_backward_kernel(
    info_ref, a_ref, log_ref, rows_ref, gain_ref, wc_ref, e2_ref, gr2_ref, r1_ref, qc_ref,
    cross_ref, cross_log_ref, kvc_ref, sums_in_ref,
    e1_ref, dqc_ref, ga_ref, gr1_ref, delta_ref, dkvc_ref, sums_ref, dq_ref,
    *, factor, scale, cross_rows,
):
    info = RowInfo(info_ref)
    rows, width = a_ref.shape
    half = rows // 2
    cross_block = cross_rows
    cross_range = [info.cross_keys(block, cross_block) for block in range(2)]
    live_first = jnp.minimum(cross_range[0][0], cross_range[1][0])
    live_last = jnp.maximum(cross_range[0][1], cross_range[1][1])
    sums_ref[...] = sums_in_ref[...]
    n1, inv1 = norm_stats(r1_ref[...])
    attn_self, attn_cross = a_ref[...], cross_ref[...]
    gr2, e2, qc, cross_logs = gr2_ref[...], e2_ref[...], qc_ref[...], cross_log_ref[...]

    def clear(index, carry):
        at = pl.ds(pl.multiple_of(index * cross_block, cross_block), cross_block)
        dkvc_ref[at, :] = jnp.zeros((cross_block, 2 * width), bf16)
        return carry

    lax.fori_loop(live_first, live_last, clear, 0)
    gac = dot_nt(e2, wc_ref[4]).astype(bf16)
    sums_ref[8:9, :] = column_sum(gac)
    delta_cross = head_sums(gac.astype(f32) * attn_cross)
    grads = []
    for block in (1, 0):
        at = slice(block * half, (block + 1) * half)
        grads.append(
            attend_back(
                qc[at], gac[at], kvc_ref, dkvc_ref, rows_ref[2:3, at], rows_ref[3:4, at],
                [pair_rows(cross_logs, block, half, p) for p in range(PAIRS)],
                [pair_rows(delta_cross, block, half, p) for p in range(PAIRS)],
                *cross_range[block], cross_block, factor, scale,
                dq_ref, True,
            )
        )
    dqc = jnp.concatenate([grads[1], grads[0]], axis=0).astype(bf16)
    dqc_ref[...] = dqc
    sums_ref[7:8, :] = column_sum(dqc)
    gh1 = gr2 + dot_nt(dqc, wc_ref[0])
    sums_ref[0:1, :] = column_sum(gh1 * n1)
    sums_ref[6:7, :] = column_sum(gh1)
    gr1 = norm_back(n1, inv1, gain_ref[0:1, :], gh1)
    gr1_ref[...] = gr1
    e1 = gr1.astype(bf16)
    e1_ref[...] = e1
    sums_ref[5:6, :] = column_sum(e1)
    ga = dot_nt(e1, wc_ref[3]).astype(bf16)
    ga_ref[0:rows, :] = ga
    sums_ref[4:5, :] = column_sum(ga)
    delta = head_sums(ga.astype(f32) * attn_self)
    delta_ref[...] = delta
    extra = split_three(side_by_side(log_ref[...])) + split_three(side_by_side(delta))
    extra.append(jnp.zeros((2 * HEADS // 2, width), bf16))
    ga_ref[rows:, :] = jnp.concatenate([e.astype(f32) for e in extra], axis=0).astype(bf16)


def memory_grads_kernel(
    info_ref, mem_ref, wc_ref, dkvc_ref, pm_ref, dwc_ref, dw_acc_ref, *, cross_block
):
    info = RowInfo(info_ref)
    width = mem_ref.shape[1]
    cross_range = [info.cross_keys(block, cross_block) for block in range(2)]
    live_first = jnp.minimum(cross_range[0][0], cross_range[1][0])
    live_last = jnp.maximum(cross_range[0][1], cross_range[1][1])
    pm_ref[...] = jnp.zeros(pm_ref.shape, bf16)
    dw_acc_ref[...] = jnp.zeros(dw_acc_ref.shape, f32)

    def memory_step(index, carry):
        at = pl.ds(pl.multiple_of(index * cross_block, cross_block), cross_block)
        grads_block = dkvc_ref[at, :]
        block = dot_nt(grads_block[:, :width], wc_ref[1]) + dot_nt(grads_block[:, width:], wc_ref[2])
        pm_ref[at, :] = block.astype(bf16)
        dw_acc_ref[...] += dot_tn(mem_ref[at, :], grads_block)
        return carry

    lax.fori_loop(live_first, live_last, memory_step, 0)
    dwc_ref[...] = dw_acc_ref[...].astype(bf16)


def query_backward_kernel(
    info_ref, q_ref, ga_ref, kv_near_ref, kv_far_ref, log_ref, delta_ref, cols_ref, dq_ref, acc_ref,
    log_rep_ref, delta_rep_ref, *, factor, scale, planes,
):
    info = RowInfo(info_ref)
    rows = q_ref.shape[0]
    half = info.half
    pad = jnp.zeros((128 - 2 * HEADS, rows), f32)
    stat_cols = jnp.transpose(jnp.concatenate([log_ref[...], delta_ref[...], pad], axis=0))

    def stat_column(at, head):
        return jnp.concatenate(
            [stat_cols[at, head : head + 1], stat_cols[at, head + 1 : head + 2]], axis=0
        )

    for block in range(2):
        at = slice(block * half, (block + 1) * half)
        acc_ref[...] = jnp.zeros(acc_ref.shape, f32)
        for p in range(PAIRS):
            log_rep_ref[p] = jnp.broadcast_to(stat_column(at, 2 * p), log_rep_ref.shape[1:])
            delta_rep_ref[p] = jnp.broadcast_to(stat_column(at, HEADS + 2 * p), log_rep_ref.shape[1:])
        for part, kv_ref in enumerate((kv_near_ref, kv_far_ref)):
            query_grads(
                q_ref[at, :], ga_ref[at, :], kv_ref, cols_ref[at, 0:1], cols_ref[at, 1:2],
                log_rep_ref, delta_rep_ref,
                over_planes(info, part * planes, planes, *info.self_keys(block)),
                self_block, factor, acc_ref,
            )
        dq_ref[at, :] = (merged_rows(acc_ref) * scale).astype(bf16)


def key_backward_kernel(
    info_ref, kv_rows_ref, q_all_ref, cols_ref, *refs, factor, scale, planes, part, last,
    total_planes,
):
    state_in, refs = (refs[:2], refs[2:]) if part else ((), refs)
    pieces, refs = refs[:4], refs[4:]
    if last:
        dk_out_ref, dv_out_ref, g_ref, stats_ref, dk_ref, dv_ref = refs
    else:
        dk_ref, dv_ref, g_ref, stats_ref = refs
    info = RowInfo(info_ref)
    half = info.half
    rows = 2 * half
    width = q_all_ref.shape[1]
    for s, bits, chunk in chunk_views(pieces, planes):
        place = (info.me & 3) ^ bits
        extra = chunk[rows : rows + chunk_rows, :].astype(f32)
        logs = extra[0:4] + extra[4:8] + extra[8:12]
        deltas = extra[12:16] + extra[16:20] + extra[20:24]
        for side in range(2):
            block = 8 * s + 4 * side + (place if side == 0 else 3 - place)
            lanes = slice(side * half, (side + 1) * half)
            high = slice(rows + side * half, rows + (side + 1) * half)
            g_ref[pl.ds(pl.multiple_of(block * half, half), half), :] = chunk[lanes, :]
            stats_ref[block] = jnp.concatenate(
                [logs[:, lanes], logs[:, high], deltas[:, lanes], deltas[:, high]], axis=0
            )

    def groups(first, stop):
        def run(step):
            def visit(stored, carry):
                plane = info.plane ^ (part * planes + (stored >> 1))
                index = jnp.where((stored & 1) == 0, plane, 2 * total_planes - 1 - plane)

                @pl.when((index >= first) & (index < stop))
                def _():
                    step(stored, index)

                return carry

            lax.fori_loop(0, 2 * planes, visit, 0)

        return run

    for block in range(2):
        at = slice(block * half, (block + 1) * half)
        if part:
            dk_ref[block] = state_in[0][block]
            dv_ref[block] = state_in[1][block]
        else:
            dk_ref[block] = jnp.zeros(dk_ref.shape[1:], f32)
            dv_ref[block] = jnp.zeros(dv_ref.shape[1:], f32)
        key_grads(
            kv_rows_ref[at, 0:width], kv_rows_ref[at, width:], q_all_ref, g_ref, stats_ref,
            cols_ref[at, 1:2], cols_ref[at, 4:5], groups(*info.queries(block)), factor,
            dk_ref.at[block], dv_ref.at[block],
        )
    if not last:
        return
    dk = jnp.concatenate([merged_rows(dk_ref.at[b]) for b in range(2)], axis=0) * scale
    dv = jnp.concatenate([merged_rows(dv_ref.at[b]) for b in range(2)], axis=0)
    dk_out_ref[...] = dk.astype(bf16)
    dv_out_ref[...] = dv.astype(bf16)


def self_grads_kernel(
    info_ref, x_ref, gr1_ref, dq_ref, dk_ref, dv_ref, w_ref, tok_ref, *refs, plain
):
    sink_refs, (dw_ref,) = (refs[:1], refs[1:]) if plain else (refs[:2], refs[2:])
    info = RowInfo(info_ref)
    dk, dv = dk_ref[...], dv_ref[...]
    tok = gr1_ref[...] + dot_nt(dq_ref[...], w_ref[0]) + dot_nt(dk, w_ref[1]) + dot_nt(dv, w_ref[2])
    tok_ref[...] = tok.astype(bf16)
    sink = PlainSink(*sink_refs) if plain else PieceSink(*sink_refs, dw_ref, info.me, info.side)
    x_rows = x_ref[...]
    sink.put(0, dot_tn(x_rows, dk))
    sink.put(1, dot_tn(x_rows, dv))


def feed_grads_kernel(info_ref, h2_ref, gu_ref, f_ref, e3_ref, *refs, plain):
    sink_refs, (dw_ref,) = (refs[:1], refs[1:]) if plain else (refs[:2], refs[2:])
    info = RowInfo(info_ref)
    sink = PlainSink(*sink_refs) if plain else PieceSink(*sink_refs, dw_ref, info.me, info.side)
    width = h2_ref.shape[1]
    parts = gu_ref.shape[1] // width
    for k in range(parts):
        sink.put(k, dot_tn(h2_ref[...], gu_ref[:, k * width : (k + 1) * width]))
    sink.put(parts, dot_tn(f_ref[...], e3_ref[...]))


def map_grads_kernel(
    info_ref, a_ref, e1_ref, ac_ref, e2_ref, h1_ref, dqc_ref, dwc_ref, x_ref, dq_ref, sums_ref,
    csum_ref, *refs, plain,
):
    sink_refs, (dw_ref,) = (refs[:1], refs[1:]) if plain else (refs[:2], refs[2:])
    info = RowInfo(info_ref)
    sink = PlainSink(*sink_refs) if plain else PieceSink(*sink_refs, dw_ref, info.me, info.side)
    width = a_ref.shape[1]
    sink.put(0, dot_tn(a_ref[...], e1_ref[...]))
    sink.put(1, dot_tn(ac_ref[...], e2_ref[...]))
    sink.put(2, dot_tn(h1_ref[...], dqc_ref[...]))
    sink.put(3, dwc_ref[:, :width])
    sink.put(4, dwc_ref[:, width:])
    sink.put(5, dot_tn(x_ref[...], dq_ref[...]))
    put_small(sink, 6, dw_ref, sums_ref[...], csum_ref, dq_ref[...])


def grads_project_kernel(info_ref, w_ref, bias_ref, *refs, planes, plain):
    pieces, refs = refs[:8], refs[8:]
    inputs, refs = refs[:11], refs[11:]
    q_ref, outs = refs[0], refs[1:]
    map_grads_kernel(info_ref, *inputs, *outs, plain=plain)
    project_kernel(info_ref, w_ref, bias_ref, *pieces, q_ref, planes=planes)


def put_small(sink, block, dw_ref, sums, csum_ref, dq):
    dw_ref[...] = jnp.zeros(dw_ref.shape, f32)
    row = lax.broadcasted_iota(jnp.int32, sums.shape, 0)
    sums = jnp.where(row == 3, column_sum(dq), sums)
    lanes = csum_ref.shape[1] // 8
    for yh in range(2):
        base = yh * half_rows
        dw_ref[base : base + 16, 0:lanes] = sums[:, yh * lanes : (yh + 1) * lanes]
        for k in range(4):
            start = yh * 4 * lanes + k * lanes
            dw_ref[base + 16 + k : base + 17 + k, 0:lanes] = csum_ref[:, start : start + lanes]
    if isinstance(sink, PlainSink):
        sink.plain[block] = dw_ref[...].astype(bf16)
    else:
        sink.emit(block, half_rows, 0)


def place_kernel(info_ref, *refs, places):
    sources, outs = refs[:4], refs[4:]
    info = RowInfo(info_ref)
    planes = sources[0].shape[0]
    piece = half_rows // (4 * planes)
    for s in range(planes):
        for bits in range(4):
            owner = info.me ^ (4 * s + bits)
            source = sources[(bits >> 1) + 2 * (bits & 1)]
            for block, (number, kind, k) in enumerate(places):
                rows = source[s, block * piece : (block + 1) * piece, :].astype(f32)
                width = rows.shape[1]
                base = k * half_rows if kind == "rows" else 0
                at = pl.ds(pl.multiple_of(base + owner * piece, piece), piece)
                if kind == "lead":
                    outs[number][k, at, :] = rows
                elif kind == "cols":
                    outs[number][at, k * width : (k + 1) * width] = rows
                else:
                    outs[number][at, :] = rows


def place_maps_kernel(
    info_ref, own_ref, other_ref, own_core_ref, other_core_ref, ins_ref, outs_ref, gain_ref, bias_ref,
    shift_ref, rest_ref,
):
    place_kernel(
        info_ref, own_ref, other_ref, own_core_ref, other_core_ref, ins_ref, outs_ref, rest_ref,
        places=[(1, "lead", 0), (1, "lead", 1)]
        + [(0, "lead", k) for k in (3, 4, 5, 0)]
        + [(2, "rows", 0), (0, "lead", 1), (0, "lead", 2)],
    )
    lanes = gain_ref.shape[1]
    gain_ref[...] = rest_ref[0:3, 0:lanes]
    bias_ref[...] = rest_ref[3:13, 0:lanes]
    shift_ref[...] = rest_ref[16:20, 0:lanes]


def call_kernel(kernel, inputs, outputs, scratch, name, micros, in_place=()):
    vmem = pl.BlockSpec(memory_space=pltpu.VMEM)
    smem = pl.BlockSpec(memory_space=pltpu.SMEM)
    return pl.pallas_call(
        kernel,
        in_specs=[smem]
        + [
            pl.BlockSpec(memory_space=pl.ANY) if index in in_place else vmem
            for index in range(1, len(inputs))
        ],
        out_specs=[vmem] * len(outputs),
        out_shape=[jax.ShapeDtypeStruct(*entry) for entry in outputs],
        scratch_shapes=[pltpu.VMEM(*entry) if isinstance(entry, tuple) else entry for entry in scratch],
        compiler_params=pltpu.CompilerParams(vmem_limit_bytes=vmem_bytes),
        cost_estimate=pl.CostEstimate(
            flops=int(micros * 1e9), transcendentals=0, bytes_accessed=int(micros * 1e4)
        ),
        name=name,
    )(*inputs)


def exchange(value, bits):
    count = lax.axis_size("ctx")
    return lax.ppermute(value, "ctx", [(i, i ^ bits) for i in range(count)])


def swap_side(value):
    return lax.ppermute(value, "fsdp", [(0, 1), (1, 0)])


def after(value, *others):
    return lax.optimization_barrier((value,) + others)[0]


def fetch_planes(value, first, last):
    return [exchange(value, 4 * s) if s else value for s in range(first, last)]


def fetch_chips(chunks):
    return [chunks, exchange(chunks, 2)]


def fetch_cores(pair):
    return pair + [exchange(chunks, 1) for chunks in pair]


def core_part(shard, axis):
    rows = shard.shape[axis] // 2
    return lax.dynamic_slice_in_dim(shard, (lax.axis_index("ctx") % 2) * rows, rows, axis)


def add_cores(keep, send):
    other = exchange(send, 1)
    return keep[0].astype(f32) + other[0].astype(f32), (
        keep[1].astype(f32) + other[1].astype(f32)
    ).astype(bf16)


def add_sides(kept, sent):
    return kept + swap_side(sent).astype(f32)


def add_chips(part, low):
    return part[0] + exchange(low, 2).astype(f32)


def low_planes(part):
    return [part[s].astype(bf16) for s in range(1, part.shape[0])]


def add_planes(part, low):
    total = part[0]
    for s, sent in enumerate(low):
        total = total + exchange(sent, 4 * (s + 1)).astype(f32)
    return total


def spread_planes(low):
    planes = lax.axis_size("ctx") // 4
    return [low] + [exchange(low, 4 * s) for s in range(1, planes)]


def spread_chips(chunks, before=None):
    own = jnp.stack(chunks)
    other = exchange(own, 2)
    sent = [own, other] if before is None else [after(own, before), after(other, before)]
    return [own, other] + [exchange(chunk, 1) for chunk in sent]


def zigzag_perms(count):
    def worker(block):
        return block if block < count else 2 * count - 1 - block

    first = [(owner, worker(2 * owner)) for owner in range(count)]
    second = [(owner, worker(2 * owner + 1)) for owner in range(count)]
    return first, second


def body(
    tokens, memory, token_seg, memory_seg, out_grad,
    in_proj, out_proj, ffn_in, ffn_out, norm_gain, bias_rows, ffn_bias,
):
    count = lax.axis_size("ctx")
    sides = lax.axis_size("fsdp")
    planes = count // 4
    plain = sides != 2
    me = lax.axis_index("ctx")
    side = lax.axis_index("fsdp")
    row_count, width = tokens.shape[1], tokens.shape[2]
    mem_count = memory.shape[1]
    half = row_count // 2
    scale = 1.0 / math.sqrt(width // HEADS)
    factor = scale * math.log2(math.e)
    total = row_count * count
    mem_total = mem_count * count
    near, far = planes // 2, planes - planes // 2

    x_planes = fetch_planes(tokens[0], 0, planes)
    small = jnp.concatenate(
        [norm_gain, bias_rows, ffn_bias.reshape(-1, norm_gain.shape[1])], axis=0
    ).astype(bf16)
    maps_low = jnp.concatenate([in_proj, out_proj], axis=0).astype(bf16)
    up_low, down_low = ffn_in.astype(bf16), ffn_out.astype(bf16)
    if plain:
        small = lax.all_gather(small, "fsdp").astype(f32)
        whole = lax.all_gather(maps_low, "fsdp", axis=1, tiled=True)
        self_maps = (whole,)
        late_maps = (
            whole, lax.all_gather(up_low, "fsdp", axis=0, tiled=True),
            lax.all_gather(down_low, "fsdp", axis=0, tiled=True),
        )
    else:
        small_rows = small.shape[0]
        pad = jnp.zeros((32 - small_rows, small.shape[1]), bf16)
        sent = jnp.concatenate(
            [
                core_part(in_proj[0:3], 1).astype(bf16).reshape(-1, width),
                jnp.concatenate([small, pad], axis=0).reshape(-1, width),
            ],
            axis=0,
        )
        fetched = swap_side(sent)
    x_near = fetch_chips(jnp.stack(x_planes[:near]))
    if not plain:
        ready = after(fetched, x_near[1])
        table_rows = ready[-pad.shape[1] * 32 // width :].reshape(32, -1)[:small_rows]
        small = jnp.stack([small, table_rows])
        small = jnp.where(side == 0, small, small[::-1]).astype(f32)
        self_maps = (maps_low, ready, exchange(ready, 1))
        up_part = core_part(after(ffn_in, sent), 0).astype(bf16)
        late_parts = [
            core_part(in_proj[3:6], 1).astype(bf16).reshape(-1, width),
            core_part(after(out_proj, sent), 1).astype(bf16).reshape(-1, width),
            core_part(after(ffn_out, sent), 0).astype(bf16),
        ]
        late_parts += [
            up_part[:, k * width : (k + 1) * width] for k in range(up_part.shape[1] // width)
        ]
        late_sent = jnp.concatenate(late_parts, axis=0)
        late = swap_side(after(late_sent, fetched))
    started = x_near[0] if plain else fetched
    x_far = fetch_chips(jnp.stack([after(chunk, started) for chunk in x_planes[near:]]))

    perm_first, perm_second = zigzag_perms(count)
    even = me % 2 == 0
    first_sent = small if plain else sent
    rows_in = jnp.stack([after(tokens[0], first_sent, x_near[0]), out_grad[0]])
    one = lax.ppermute(rows_in[:, :half], "ctx", perm_first)
    two = lax.ppermute(rows_in[:, half:], "ctx", perm_second)
    rows_in = jnp.where(
        even, jnp.concatenate([one, two], axis=1), jnp.concatenate([two, one], axis=1)
    )
    x_rows, g_rows = rows_in[0], rows_in[1]

    table = small[:, 0:13].transpose(1, 0, 2).reshape(13, width)
    gains, biases = table[0:3], table[3:13]
    ffn_shift = small[:, 13:].reshape(1, -1)

    m_all = lax.all_gather(memory[0], "ctx", axis=0, tiled=True)

    segs, mem_segs = after(token_seg[0], first_sent), after(memory_seg[0], first_sent)
    step = jnp.arange(half, dtype=jnp.int32)
    row_pos = jnp.concatenate([me * half + step, (2 * count - 1 - me) * half + step])
    row_seg = jnp.concatenate(
        [
            lax.dynamic_slice_in_dim(segs, me * half, half),
            lax.dynamic_slice_in_dim(segs, (2 * count - 1 - me) * half, half),
        ]
    )

    def below(keys, closed):
        hits = keys[None, :] <= row_seg[:, None] if closed else keys[None, :] < row_seg[:, None]
        return jnp.sum(hits, axis=1, dtype=jnp.int32)

    ones = jnp.ones_like(row_pos)
    info = jnp.stack(
        [
            below(segs, False), row_pos, below(mem_segs, False), below(mem_segs, True) - 1,
            below(segs, True) - 1, me * ones, side * ones, ones,
        ]
    )
    cols = info.T

    tile = width // PAIRS
    column = ((PAIRS, row_count, 1), f32)
    square = ((PAIRS, row_count, tile), f32)
    two_squares = ((2, PAIRS, row_count, tile), f32)
    rows_low = ((row_count, width), bf16)
    rows_full = ((row_count, width), f32)
    kv_rows_shape = ((row_count, 2 * width), bf16)

    x_near = fetch_cores(x_near)
    x_near[0] = after(x_near[0], x_far[0], up_low, down_low)
    wide = ((PAIRS, row_count, 2 * tile), f32)
    q_rows, kv_rows, kv_near, w_self, top, weights = call_kernel(
        lambda *refs: first_forward_kernel(
            *refs, factor=factor, planes=near, shards=len(self_maps)
        ),
        (info, x_rows, biases, cols, *self_maps, *x_near),
        (
            rows_low, kv_rows_shape, ((4 * near * row_count, 2 * width), bf16),
            ((3, width, width), bf16), rows_full, rows_full,
        ),
        [wide],
        "first_forward",
        10,
    )
    x_far = fetch_cores([after(chunks, top) for chunks in x_far])
    a_rows, log_rows, kv_far = call_kernel(
        lambda *refs: second_forward_kernel(*refs, factor=factor, planes=far),
        (info, kv_near, q_rows, biases, cols, w_self, top, weights, *x_far),
        (rows_full, ((HEADS, row_count), f32), ((4 * far * row_count, 2 * width), bf16)),
        [
            wide, column, column, square, rows_full, ((4 * near * row_count, 2 * width), bf16),
            pltpu.SemaphoreType.DMA,
        ],
        "second_forward",
        10,
        (1,),
    )
    if not plain:
        late = after(late, a_rows)
        late_maps = (maps_low, up_low, down_low, late, exchange(late, 1))
    ff_width = ffn_in.shape[1]
    ff_rows = ((row_count, ff_width), bf16)
    by_head = ((HEADS, row_count), f32)
    kvc_shape = ((mem_total, 2 * width), bf16)
    sums_shape = ((16, width), f32)
    whole_maps = [] if plain else [((width, ff_width), bf16), ((ff_width, width), bf16)]
    (
        out_rows, a_low, h1_low, h2_low, act, e3, gu, e2, ac_low, gr2, r1, qc, cross, cross_log,
        kvc, sums, csum, w_cross,
    ) = call_kernel(
        lambda *refs: middle_forward_kernel(
            *refs, factor=factor, shards=len(self_maps), cross_rows=2 * mem_count
        ),
        (info, x_rows, a_rows, g_rows, cols, gains, biases, ffn_shift, m_all, *late_maps),
        (
            rows_full, rows_low, rows_low, rows_low, ff_rows, rows_low, ff_rows, rows_low, rows_low,
            rows_full, rows_full, rows_low, rows_full, by_head, kvc_shape, sums_shape,
            ((1, ff_width), f32), ((5, width, width), bf16),
        ),
        [wide, column, column, square, rows_full, *whole_maps],
        "middle_forward",
        25,
    )

    def sink_shapes(blocks):
        if plain:
            return [((blocks, width, width), bf16)]
        return [((2, 2, planes, blocks * (half_rows // count), width), bf16)] * 2

    feed = call_kernel(
        lambda *refs: feed_grads_kernel(*refs, plain=plain),
        (info, h2_low, gu, act, e3),
        sink_shapes(8),
        [((ff_width, width), f32)],
        "feed_grads",
        5,
    )
    gr2 = after(gr2, *feed)
    e1, dqc, ga, gr1, delta, dkvc, sums = call_kernel(
        lambda *refs: middle_backward_kernel(
            *refs, factor=factor, scale=scale, cross_rows=2 * mem_count
        ),
        (
            info, a_rows, log_rows, info, gains, w_cross, e2, gr2, r1, qc, cross, cross_log, kvc,
            sums,
        ),
        (
            rows_low, rows_low, ((row_count + chunk_rows, width), bf16), rows_full, by_head,
            kvc_shape, sums_shape,
        ),
        [((PAIRS, tile, row_count), f32)],
        "middle_backward",
        14,
    )
    g_planes = fetch_planes(ga, 0, near)
    if not plain:
        feed = add_cores(*feed)
        dkvc = after(dkvc, feed[1])
    mem_part, dwc = call_kernel(
        lambda *refs: memory_grads_kernel(*refs, cross_block=2 * mem_count),
        (info, m_all, w_cross, dkvc),
        (((mem_total, width), bf16), ((width, 2 * width), bf16)),
        [((width, 2 * width), f32)],
        "memory_grads",
        5,
    )
    g_near = fetch_chips(jnp.stack([after(chunk, mem_part) for chunk in g_planes]))
    g_planes = fetch_planes(after(ga, mem_part), near, planes)
    (dq,) = call_kernel(
        lambda *refs: query_backward_kernel(*refs, factor=factor, scale=scale, planes=near),
        (info, after(q_rows, g_near[0]), ga, kv_near, kv_far, log_rows, delta, cols),
        (rows_low,),
        [square, square, square],
        "query_backward",
        20,
    )
    g_far = fetch_chips(jnp.stack([after(chunk, dq) for chunk in g_planes]))
    g_near = fetch_cores([after(chunks, dq) for chunks in g_near])
    if not plain:
        feed = add_sides(*feed)
        feed_low = feed[1].astype(bf16)
        h1_low = after(h1_low, feed_low)
    q_all, *maps = call_kernel(
        lambda *refs: grads_project_kernel(*refs, planes=near, plain=plain),
        (
            info, w_self, biases, *x_near, *x_far, a_low, e1, ac_low, e2,
            after(h1_low, g_far[0], g_near[1]), dqc, dwc, x_rows, dq, sums, csum,
        ),
        [((total, width), bf16)] + sink_shapes(7),
        [((width, width), f32)],
        "grads_project",
        12,
    )
    if not plain:
        maps = add_cores(*maps)
        feed_low = after(feed_low, q_all)
        kv_rows = after(kv_rows, maps[1], feed_low)
    mem_part = after(mem_part, g_far[1])
    memory_grad = lax.psum_scatter(mem_part, "ctx", scatter_dimension=0, tiled=True).astype(f32)
    g_far = fetch_cores([after(chunks, q_all) for chunks in g_far])
    dk_part, dv_part = call_kernel(
        lambda *refs: key_backward_kernel(
            *refs, factor=factor, scale=scale, planes=near, part=0, last=False,
            total_planes=planes,
        ),
        (info, kv_rows, q_all, cols, *g_near),
        [two_squares, two_squares],
        [
            ((4 * near * row_count, width), bf16), ((8 * near, 2 * HEADS, half), f32),
        ],
        "key_backward",
        8,
    )
    if not plain:
        feed = feed[0] + after(exchange(feed_low, 2), dk_part).astype(f32)
        feed_low = low_planes(feed)
        dk_part = after(dk_part, *feed_low)
    dk, dv = call_kernel(
        lambda *refs: key_backward_kernel(
            *refs, factor=factor, scale=scale, planes=far, part=1, last=True, total_planes=planes
        ),
        (info, kv_rows, q_all, cols, dk_part, dv_part, *g_far),
        [rows_low, rows_low],
        [
            ((4 * far * row_count, width), bf16), ((8 * far, 2 * HEADS, half), f32),
            two_squares, two_squares,
        ],
        "key_backward_last",
        3,
    )
    if not plain:
        feed = add_planes(feed, feed_low).astype(bf16)
        maps = add_sides(*maps)
        maps_low = maps[1].astype(bf16)
        dk = after(dk, feed, maps_low)
    tok_rows, *last = call_kernel(
        lambda *refs: self_grads_kernel(*refs, plain=plain),
        (info, x_rows, gr1, dq, dk, dv, w_self),
        [rows_low] + sink_shapes(2),
        [((width, width), f32)],
        "self_grads",
        4,
    )

    back_first = [(to, owner) for owner, to in perm_first]
    back_second = [(to, owner) for owner, to in perm_second]

    rows_out = jnp.stack([out_rows.astype(bf16), tok_rows])
    half_one = jnp.where(even, rows_out[:, :half], rows_out[:, half:])
    half_two = jnp.where(even, rows_out[:, half:], rows_out[:, :half])
    rows_out = jnp.concatenate(
        [lax.ppermute(half_one, "ctx", back_first), lax.ppermute(half_two, "ctx", back_second)],
        axis=1,
    ).astype(f32)
    layer_out, tokens_grad = rows_out[0], rows_out[1]
    lanes = width // 2
    if plain:

        def owned(matrix, axis):
            part = lax.psum_scatter(matrix, "fsdp", scatter_dimension=axis, tiled=True)
            return lax.psum(part, "ctx").astype(f32)

        feed, maps, last = feed[0], maps[0], last[0]
        ins = owned(jnp.concatenate([maps[5:6], last, maps[2:5]], axis=0), 1)
        outs = owned(maps[0:2], 1)
        up = owned(jnp.concatenate([feed[k] for k in range(4)], axis=1), 0)
        down = owned(feed[4:8].reshape(-1, width), 0)
        rest = jnp.stack([maps[6, 0:half_rows, 0:lanes], maps[6, half_rows:, 0:lanes]], axis=1)
        table = owned(rest[0:13].reshape(13, width).astype(f32), 1)
        shift = owned(rest[16:20].transpose(1, 0, 2).reshape(-1).astype(f32), 0)
        gain_sums, bias_sums = table[0:3], table[3:13]
    else:
        feed_planes = spread_planes(feed)
        last = add_sides(*add_cores(*last))
        last_low = after(last[1].astype(bf16), *feed_planes[1:])
        feed_own = jnp.stack(feed_planes)
        feed_other = exchange(feed_own, 2)
        last = add_chips(last, last_low)
        maps = add_chips(maps, maps_low)
        maps = add_planes(maps, low_planes(maps)).astype(bf16)
        last = add_planes(last, [after(low, maps) for low in low_planes(last)]).astype(bf16)
        up, down = call_kernel(
            lambda *refs: place_kernel(
                *refs,
                places=[(0, "cols", k) for k in range(4)] + [(1, "rows", k) for k in range(4)],
            ),
            (info, feed_own, feed_other, exchange(feed_own, 1), exchange(feed_other, 1)),
            ((ffn_in.shape, f32), (ffn_out.shape, f32)),
            [],
            "place_feed",
            4,
        )
        maps = jnp.concatenate([maps, after(last, feed_other)], axis=0)
        ins, outs, gain_sums, bias_sums, shift = call_kernel(
            place_maps_kernel,
            (info, *spread_chips(spread_planes(maps), up)),
            (
                (in_proj.shape, f32), (out_proj.shape, f32), ((3, lanes), f32), ((10, lanes), f32),
                ((4, lanes), f32),
            ),
            [((half_rows, width), f32)],
            "place_maps",
            4,
        )
        shift = shift.reshape(-1)
    return (
        layer_out[None], tokens_grad[None], memory_grad[None], ins, outs, up, down,
        gain_sums, bias_sums, shift,
    )


def solution(mesh):
    rows = P("fsdp", "ctx", None)
    params = (
        P(None, "fsdp", None), P(None, "fsdp", None), P("fsdp", None), P("fsdp", None),
        P(None, "fsdp"), P(None, "fsdp"), P("fsdp"),
    )
    return jax.shard_map(
        body,
        mesh=mesh,
        in_specs=(rows, rows, P("fsdp", None), P("fsdp", None), rows) + params,
        out_specs=(rows, rows, rows) + params,
        check_vma=False,
    )
```

```python
import math

import jax
import jax.numpy as jnp
from jax import lax
from jax.experimental import pallas as pl
from jax.experimental.pallas import tpu as pltpu
from jax.sharding import PartitionSpec as P

HEADS = 8
PAIRS = HEADS // 2
neg_fill = -1e30
eps_norm = 1e-05
self_block = 512
bf16 = jnp.bfloat16
f32 = jnp.float32
vmem_bytes = 60 * 1024 * 1024
half_rows = 256
chunk_rows = 32


def dot_nn(first_op, second_op):
    return jnp.dot(first_op, second_op, preferred_element_type=f32)


def dot_nt(first_op, second_op):
    return lax.dot_general(
        first_op, second_op, (((1,), (1,)), ((), ())), preferred_element_type=f32
    )


def dot_tn(first_op, second_op):
    return lax.dot_general(
        first_op, second_op, (((0,), (0,)), ((), ())), preferred_element_type=f32
    )


def stack_heads(tile):
    lane = lax.broadcasted_iota(jnp.int32, tile.shape, 1)
    half = tile.shape[1] // 2
    zero = jnp.zeros_like(tile)
    return jnp.concatenate(
        [jnp.where(lane < half, tile, zero), jnp.where(lane >= half, tile, zero)], axis=0
    )


def merge_heads(stacked):
    rows = stacked.shape[0] // 2
    lane = lax.broadcasted_iota(jnp.int32, (rows, stacked.shape[1]), 1)
    return jnp.where(lane < stacked.shape[1] // 2, stacked[:rows], stacked[rows:])


def tile_of(value, pair, tile_width):
    return value[:, pair * tile_width : (pair + 1) * tile_width]


def head_sums(product):
    width = product.shape[1]
    head = lax.broadcasted_iota(jnp.int32, (HEADS, width), 0)
    lane = lax.broadcasted_iota(jnp.int32, (HEADS, width), 1)
    pick = (lane // (width // HEADS) == head).astype(f32)
    return lax.dot_general(
        pick,
        product,
        (((1,), (1,)), ((), ())),
        precision=lax.Precision.HIGHEST,
        preferred_element_type=f32,
    )


def over_range(first, last):
    def run(step):
        def visit(index, carry):
            step(index, index)
            return carry

        lax.fori_loop(first, last, visit, 0)

    return run


def over_planes(info, plane_first, plane_count, first, last):
    def run(step):
        def visit(stored, carry):
            index = 2 * (info.plane ^ (plane_first + (stored >> 1))) + (stored & 1)

            @pl.when((index >= first) & (index < last))
            def _():
                step(stored, index)

            return carry

        lax.fori_loop(0, 2 * plane_count, visit, 0)

    return run


class RowInfo:
    def __init__(self, info_ref):
        self.table = info_ref
        self.half = info_ref.shape[1] // 2
        self.me = info_ref[5, 0]
        self.side = info_ref[6, 0]
        self.plane = self.me >> 2

    def ends(self, block):
        return block * self.half, (block + 1) * self.half - 1

    def self_keys(self, block):
        start, stop = self.ends(block)
        return self.table[0, start] // self_block, self.table[1, stop] // self_block + 1

    def cross_keys(self, block, size):
        start, stop = self.ends(block)
        return self.table[2, start] // size, self.table[3, stop] // size + 1

    def queries(self, block):
        start, stop = self.ends(block)
        return self.table[1, start] // self_block, self.table[4, stop] // self_block + 1


def twice(column):
    return jnp.concatenate([column, column], axis=0)


def stacked_tiles(rows):
    tile_width = rows.shape[1] // PAIRS
    return [stack_heads(tile_of(rows, pair, tile_width)) for pair in range(PAIRS)]


def attend_plain(q_block, kv_ref, low_col, high_col, run, key_rows, factor, acc_ref):
    width = q_block.shape[1]
    tile_width = width // PAIRS
    stacked = stacked_tiles(q_block)
    low2, high2 = twice(low_col), twice(high_col)
    ones = jnp.ones((key_rows, tile_width), bf16)

    def step(stored, index):
        base = pl.multiple_of(stored * key_rows, key_rows)
        key_pos = index * key_rows + lax.broadcasted_iota(jnp.int32, (1, key_rows), 1)
        allowed = (key_pos >= low2) & (key_pos <= high2)
        def read(pair, offset):
            start = offset + pair * tile_width
            return kv_ref[pl.ds(base, key_rows), start : start + tile_width]

        scores = [dot_nt(stacked[0], read(0, 0))]
        for pair in range(PAIRS):
            if pair + 1 < PAIRS:
                scores.append(dot_nt(stacked[pair + 1], read(pair + 1, 0)))
            weights = jnp.where(allowed, jnp.exp2(scores[pair] * factor), 0.0).astype(bf16)
            acc_ref[pair] += dot_nn(weights, jnp.concatenate([read(pair, width), ones], axis=1))

    run(step)


def weighted_rows(acc_ref):
    tile_width = acc_ref.shape[2] // 2
    tops = [merge_heads(acc_ref[pair, :, 0:tile_width]) for pair in range(PAIRS)]
    sums = [merge_heads(acc_ref[pair, :, tile_width:]) for pair in range(PAIRS)]
    return jnp.concatenate(tops, axis=1), jnp.concatenate(sums, axis=1)


def in_range(sums):
    return (jnp.min(sums) > 2.0**-100) & (jnp.max(sums) < 2.0**100)


def attend_running(q_block, parts, low_col, high_col, key_rows, factor, scratch):
    max_ref, sum_ref, acc_ref = scratch
    width = q_block.shape[1]
    tile_width = width // PAIRS
    stacked = stacked_tiles(q_block)
    low2, high2 = twice(low_col), twice(high_col)
    max_ref[...] = jnp.full(max_ref.shape, neg_fill, f32)
    sum_ref[...] = jnp.zeros(sum_ref.shape, f32)
    acc_ref[...] = jnp.zeros(acc_ref.shape, f32)
    for kv_ref, run in parts:

        def step(stored, index, kv_ref=kv_ref):
            base = pl.multiple_of(stored * key_rows, key_rows)
            key_pos = index * key_rows + lax.broadcasted_iota(jnp.int32, (1, key_rows), 1)
            allowed = (key_pos >= low2) & (key_pos <= high2)
            for pair in range(PAIRS):
                start = pair * tile_width
                keys = kv_ref[pl.ds(base, key_rows), start : start + tile_width]
                values = kv_ref[pl.ds(base, key_rows), width + start : width + start + tile_width]
                scores = jnp.where(allowed, dot_nt(stacked[pair], keys), neg_fill)
                old_max = max_ref[pair]
                new_max = jnp.maximum(old_max, jnp.max(scores, axis=1, keepdims=True))
                probs = jnp.exp2((scores - new_max) * factor)
                rescale = jnp.exp2((old_max - new_max) * factor)
                sum_ref[pair] = sum_ref[pair] * rescale + jnp.sum(probs, axis=1, keepdims=True)
                acc_ref[pair] = acc_ref[pair] * rescale + dot_nn(probs.astype(bf16), values)
                max_ref[pair] = new_max

        run(step)
    outputs, logs = [], []
    for pair in range(PAIRS):
        outputs.append(merge_heads(acc_ref[pair] / sum_ref[pair]))
        column = max_ref[pair] * factor + jnp.log2(sum_ref[pair])
        logs.append(merge_heads(jnp.broadcast_to(column, acc_ref.shape[1:])))
    return jnp.concatenate(outputs, axis=1), jnp.concatenate(logs, axis=1)


def log_rows_of(lane_logs):
    return head_sums(lane_logs) * (HEADS / lane_logs.shape[1])


def query_grads(
    q_block, g_block, kv_ref, low_col, high_col, log_ref, delta_ref, run, key_rows, factor, acc_ref
):
    width = q_block.shape[1]
    tile_width = width // PAIRS
    q2, g2 = stacked_tiles(q_block), stacked_tiles(g_block)
    low2, high2 = twice(low_col), twice(high_col)

    def step(stored, index):
        base = pl.multiple_of(stored * key_rows, key_rows)
        key_pos = index * key_rows + lax.broadcasted_iota(jnp.int32, (1, key_rows), 1)
        allowed = (key_pos >= low2) & (key_pos <= high2)
        def read(pair, offset):
            start = offset + pair * tile_width
            return kv_ref[pl.ds(base, key_rows), start : start + tile_width]

        def products(pair):
            return dot_nt(q2[pair], read(pair, 0)), dot_nt(g2[pair], read(pair, width))

        ahead = products(0)
        repeats = key_rows // log_ref.shape[2]
        for pair in range(PAIRS):
            scores, prob_grad = ahead
            if pair + 1 < PAIRS:
                ahead = products(pair + 1)
            logs = jnp.concatenate([log_ref[pair]] * repeats, axis=1)
            deltas = jnp.concatenate([delta_ref[pair]] * repeats, axis=1)
            probs = jnp.where(allowed, jnp.exp2(scores * factor - logs), 0.0)
            score_grad = (probs * (prob_grad - deltas)).astype(bf16)
            acc_ref[pair] += dot_nn(score_grad, read(pair, 0))

    run(step)


def key_grads(k_block, v_block, q_ref, g_ref, stats_ref, low_col, high_col, run, factor, dk_ref, dv_ref):
    width = k_block.shape[1]
    tile_width = width // PAIRS
    rows = k_block.shape[0]
    query_rows = self_block
    blocks = query_rows // rows
    k2, v2 = stacked_tiles(k_block), stacked_tiles(v_block)
    low2, high2 = twice(low_col), twice(high_col)

    def step(stored, index):
        base = pl.multiple_of(stored * query_rows, query_rows)
        q_base = pl.multiple_of(index * query_rows, query_rows)
        query_pos = q_base + lax.broadcasted_iota(jnp.int32, (1, query_rows), 1)
        allowed = (query_pos >= low2) & (query_pos <= high2)
        stats = jnp.concatenate([stats_ref[stored * blocks + u] for u in range(blocks)], axis=1)

        def two_rows(first_row):
            return jnp.concatenate(
                [
                    jnp.broadcast_to(stats[first_row : first_row + 1], (rows, query_rows)),
                    jnp.broadcast_to(stats[first_row + 1 : first_row + 2], (rows, query_rows)),
                ],
                axis=0,
            )

        def read(ref, start, pair):
            return ref[pl.ds(start, query_rows), pair * tile_width : (pair + 1) * tile_width]

        def products(pair):
            return dot_nt(k2[pair], read(q_ref, q_base, pair)), dot_nt(v2[pair], read(g_ref, base, pair))

        ahead = products(0)
        for pair in range(PAIRS):
            scores, prob_grad = ahead
            if pair + 1 < PAIRS:
                ahead = products(pair + 1)
            probs = jnp.where(allowed, jnp.exp2(scores * factor - two_rows(2 * pair)), 0.0)
            score_grad = (probs * (prob_grad - two_rows(HEADS + 2 * pair))).astype(bf16)
            dk_ref[pair] += dot_nn(score_grad, read(q_ref, q_base, pair))
            dv_ref[pair] += dot_nn(probs.astype(bf16), read(g_ref, base, pair))

    run(step)


def merged_rows(acc_ref):
    return jnp.concatenate([merge_heads(acc_ref[pair]) for pair in range(PAIRS)], axis=1)


def chunk_views(piece_refs, planes):
    for s in range(planes):
        for bits in range(4):
            yield s, bits, piece_refs[(bits >> 1) + 2 * (bits & 1)].at[s]


def fill_rows(target, parts, info, skip=0, lead=0):
    own, fetched, other = parts
    rows = own.shape[-2]
    core = info.me & 1
    starts = (
        info.side * rows,
        (1 - info.side) * rows + core * (rows // 2),
        (1 - info.side) * rows + (1 - core) * (rows // 2),
    )
    for number, (part, start) in enumerate(zip((own, fetched, other), starts)):
        size = rows // 2 if number else rows
        at = pl.ds(pl.multiple_of(start, rows // 2), size)
        if len(target.shape) == 3:
            for k in range(target.shape[0]):
                first = skip + k * size
                window = part[first : first + size] if number else part[lead + k]
                target[k, at, :] = window.astype(bf16)
        elif target.shape[1] == part.shape[1]:
            target[at, :] = (part[skip : skip + size] if number else part[...]).astype(bf16)
        elif not number:
            target[at, :] = part[...].astype(bf16)
        else:
            width = part.shape[1]
            for k in range(target.shape[1] // width):
                first = skip + k * size
                target[at, k * width : (k + 1) * width] = part[first : first + size]


def attend_back(
    q_block, g_block, kv_ref, dkv_ref, low_row, high_row, log_rows, delta_rows,
    first, last, key_rows, factor, scale, dq_ref, adding,
):
    width = q_block.shape[1]
    tile_width = width // PAIRS
    rows = q_block.shape[0]
    q2 = [stack_heads(tile_of(q_block, pair, tile_width)) for pair in range(PAIRS)]
    g2 = [stack_heads(tile_of(g_block, pair, tile_width)) for pair in range(PAIRS)]
    low2 = jnp.concatenate([low_row, low_row], axis=1)
    high2 = jnp.concatenate([high_row, high_row], axis=1)
    dq_ref[...] = jnp.zeros(dq_ref.shape, f32)

    def step(index, carry):
        base = pl.multiple_of(index * key_rows, key_rows)
        key_pos = base + lax.broadcasted_iota(jnp.int32, (key_rows, 1), 0)
        allowed = (key_pos >= low2) & (key_pos <= high2)
        for pair in range(PAIRS):
            key_at = (pl.ds(base, key_rows), slice(pair * tile_width, (pair + 1) * tile_width))
            value_at = (
                pl.ds(base, key_rows),
                slice(width + pair * tile_width, width + (pair + 1) * tile_width),
            )
            keys = kv_ref[key_at]
            values = kv_ref[value_at]
            scores = dot_nt(keys, q2[pair])
            probs = jnp.where(allowed, jnp.exp2(scores * factor - log_rows[pair]), 0.0)
            prob_grad = dot_nt(values, g2[pair])
            score_grad = (probs * (prob_grad - delta_rows[pair])).astype(bf16)
            key_grad = dot_nn(score_grad, q2[pair]) * scale
            value_grad = dot_nn(probs.astype(bf16), g2[pair])
            if adding:
                key_grad = key_grad + dkv_ref[key_at].astype(f32)
                value_grad = value_grad + dkv_ref[value_at].astype(f32)
            dkv_ref[key_at] = key_grad.astype(bf16)
            dkv_ref[value_at] = value_grad.astype(bf16)
            dq_ref[pair] += dot_tn(keys, score_grad)
        return carry

    lax.fori_loop(first, last, step, 0)
    tiles = []
    for pair in range(PAIRS):
        both = dq_ref[pair]
        feature = lax.broadcasted_iota(jnp.int32, (tile_width, rows), 0)
        picked = jnp.where(feature < tile_width // 2, both[:, :rows], both[:, rows:])
        tiles.append(jnp.transpose(picked) * scale)
    return jnp.concatenate(tiles, axis=1)


def split_three(value):
    one = value.astype(bf16)
    rest = value - one.astype(f32)
    two = rest.astype(bf16)
    three = (rest - two.astype(f32)).astype(bf16)
    return [one, two, three]


def side_by_side(stats):
    rows = stats.shape[0] // 2
    return jnp.concatenate([stats[:rows], stats[rows:]], axis=1)


class PieceSink:
    def __init__(self, keep_ref, send_ref, scratch_ref, me, side):
        self.keep, self.send, self.scratch, self.me, self.side = keep_ref, send_ref, scratch_ref, me, side

    def emit(self, block, stride, offset):
        planes = self.keep.shape[2]
        piece = half_rows // (4 * planes)
        at = slice(block * piece, (block + 1) * piece)
        for s in range(planes):
            for bits in range(4):
                dc, dx = bits & 1, bits >> 1
                owner = self.me ^ (4 * s + bits)
                for fy in range(2):
                    source = (self.side ^ fy) * stride + offset + owner * piece
                    rows = self.scratch[pl.ds(pl.multiple_of(source, piece), piece), :]
                    target = self.send if dc else self.keep
                    target[fy, dx, s, at, :] = rows.astype(bf16)

    def put(self, block, matrix):
        rows = matrix.shape[0]
        self.scratch[0:rows, :] = matrix.astype(f32)
        blocks = rows // (2 * half_rows)
        for b in range(blocks):
            self.emit(block + b, rows // 2, b * half_rows)


class PlainSink:
    def __init__(self, plain_ref):
        self.plain = plain_ref

    def put(self, block, matrix):
        size = 2 * half_rows
        for b in range(matrix.shape[0] // size):
            self.plain[block + b] = matrix[b * size : (b + 1) * size].astype(bf16)


def pair_rows(by_head, block, rows, pair):
    at = slice(block * rows, (block + 1) * rows)
    return jnp.concatenate(
        [by_head[2 * pair : 2 * pair + 1, at], by_head[2 * pair + 1 : 2 * pair + 2, at]], axis=1
    )


def norm_stats(residual):
    centre = residual - jnp.mean(residual, axis=1, keepdims=True)
    spread = jnp.mean(centre * centre, axis=1, keepdims=True)
    inverse = lax.rsqrt(spread + eps_norm)
    return centre * inverse, inverse


def norm_back(normed, inverse, gain_row, upstream):
    scaled = upstream * gain_row
    mean_one = jnp.mean(scaled, axis=1, keepdims=True)
    mean_two = jnp.mean(scaled * normed, axis=1, keepdims=True)
    return (scaled - mean_one - normed * mean_two) * inverse


def column_sum(matrix):
    return jnp.sum(matrix.astype(f32), axis=0, keepdims=True)


def piece_rows(pieces):
    for bits in range(4):
        ref = pieces[(bits >> 1) + 2 * (bits & 1)]
        yield bits, ref[...].reshape(ref.shape[0] * ref.shape[1], ref.shape[2])


def project_chunks(pieces, planes, kv_ref, w_ref, shift, info):
    width = w_ref.shape[2]
    rows = pieces[0].shape[1]
    for bits, block in piece_rows(pieces):
        keys = dot_nn(block, w_ref[1]).astype(bf16)
        values = (dot_nn(block, w_ref[2]) + shift).astype(bf16)
        for s in range(planes):
            start = 4 * rows * s + rows * ((info.me & 3) ^ bits)
            at = pl.ds(pl.multiple_of(start, rows), rows)
            kv_ref[at, 0:width] = keys[s * rows : (s + 1) * rows]
            kv_ref[at, width:] = values[s * rows : (s + 1) * rows]


def first_forward_kernel(info_ref, x_ref, bias_ref, cols_ref, *refs, factor, planes, shards):
    maps, refs = refs[:shards], refs[shards:]
    pieces, refs = refs[:4], refs[4:]
    q_ref, kv_rows_ref, kv_ref, w_ref, top_ref, sums_ref, acc_ref = refs
    info = RowInfo(info_ref)
    width = x_ref.shape[1]
    half = info.half
    if shards == 1:
        w_ref[...] = maps[0][0:3]
    else:
        fill_rows(w_ref, maps, info)
    shift = bias_ref[1:2, :]
    project_chunks(pieces, planes, kv_ref, w_ref, shift, info)
    x_rows = x_ref[...]
    q_rows = (dot_nn(x_rows, w_ref[0]) + bias_ref[0:1, :]).astype(bf16)
    q_ref[...] = q_rows
    kv_rows_ref[:, 0:width] = dot_nn(x_rows, w_ref[1]).astype(bf16)
    kv_rows_ref[:, width:] = (dot_nn(x_rows, w_ref[2]) + shift).astype(bf16)
    for block in range(2):
        at = slice(block * half, (block + 1) * half)
        acc_ref[...] = jnp.zeros(acc_ref.shape, f32)
        run = over_planes(info, 0, planes, *info.self_keys(block))
        attend_plain(
            q_rows[at], kv_ref, cols_ref[at, 0:1], cols_ref[at, 1:2], run, self_block, factor, acc_ref
        )
        top_ref[at, :], sums_ref[at, :] = weighted_rows(acc_ref)


def second_forward_kernel(
    info_ref, kv_near_ref, q_in_ref, bias_ref, cols_ref, w_ref, top_ref, sums_ref, *refs,
    factor, planes,
):
    pieces, refs = refs[:4], refs[4:]
    a_ref, log_ref, kv_ref, acc_ref, max_ref, sum_ref, run_ref, lane_ref, near_ref, near_sem = refs
    info = RowInfo(info_ref)
    half = info.half
    project_chunks(pieces, planes, kv_ref, w_ref, bias_ref[1:2, :], info)
    fine = None
    for block in range(2):
        at = slice(block * half, (block + 1) * half)
        acc_ref[...] = jnp.zeros(acc_ref.shape, f32)
        run = over_planes(info, planes, planes, *info.self_keys(block))
        attend_plain(
            q_in_ref[at, :], kv_ref, cols_ref[at, 0:1], cols_ref[at, 1:2], run, self_block, factor,
            acc_ref,
        )
        top, sums = weighted_rows(acc_ref)
        sums = sums + sums_ref[at, :]
        a_ref[at, :] = (top + top_ref[at, :]) / sums
        lane_ref[at, :] = jnp.log2(sums)
        fine = in_range(sums) if fine is None else fine & in_range(sums)

    @pl.when(jnp.logical_not(fine))
    def _():
        copy = pltpu.make_async_copy(kv_near_ref, near_ref, near_sem)
        copy.start()
        copy.wait()
        for block in range(2):
            at = slice(block * half, (block + 1) * half)
            keys = info.self_keys(block)
            a_ref[at, :], lane_ref[at, :] = attend_running(
                q_in_ref[at, :],
                [
                    (near_ref, over_planes(info, 0, planes, *keys)),
                    (kv_ref, over_planes(info, planes, planes, *keys)),
                ],
                cols_ref[at, 0:1], cols_ref[at, 1:2], self_block, factor, (max_ref, sum_ref, run_ref),
            )

    log_ref[...] = log_rows_of(lane_ref[...])


def project_kernel(info_ref, w_ref, bias_ref, *refs, planes):
    pieces, (q_ref,) = refs[:8], refs[8:]
    info = RowInfo(info_ref)
    for part in range(2):
        for bits, block in piece_rows(pieces[4 * part : 4 * part + 4]):
            queries = (dot_nn(block, w_ref[0]) + bias_ref[0:1, :]).astype(bf16)
            rows = pieces[0].shape[1]
            for s in range(planes):
                place = info.me ^ (4 * (part * planes + s) + bits)
                at = pl.ds(pl.multiple_of(place * rows, rows), rows)
                q_ref[at, :] = queries[s * rows : (s + 1) * rows]


def middle_forward_kernel(
    info_ref, x_ref, a_ref, g_ref, cols_ref, gain_ref, bias_ref, ffn_bias_ref, mem_ref, *refs,
    factor, shards, cross_rows,
):
    late, refs = (refs[:3], refs[3:]) if shards == 1 else (refs[:5], refs[5:])
    (
        out_ref, a_low_ref, h1_ref, h2_ref, f_ref, e3_ref, gu_ref, e2_ref, ac_ref, gr2_ref, r1_ref,
        qc_ref, cross_ref, cross_log_ref, kvc_ref, sums_ref, csum_ref, wc_ref,
        acc_ref, max_ref, sum_ref, run_ref, lane_ref, *whole_refs,
    ) = refs
    info = RowInfo(info_ref)
    if shards == 1:
        maps_ref, u_ref, v_ref = late
        wc_ref[...] = maps_ref[3:8]
    else:
        maps_ref, up_ref, down_ref, one, two = late
        u_ref, v_ref = whole_refs
        size = maps_ref.shape[1] // 2
        fill_rows(wc_ref, (maps_ref, one, two), info, 0, 3)
        fill_rows(v_ref, (down_ref, one, two), info, 5 * size)
        fill_rows(u_ref, (up_ref, one, two), info, 5 * size + down_ref.shape[0] // 2)
    rows, width = x_ref.shape
    half = rows // 2
    cross_block = cross_rows
    cross_range = [info.cross_keys(block, cross_block) for block in range(2)]
    live_first = jnp.minimum(cross_range[0][0], cross_range[1][0])
    live_last = jnp.maximum(cross_range[0][1], cross_range[1][1])

    def project(index, carry):
        at = pl.ds(pl.multiple_of(index * cross_block, cross_block), cross_block)
        block = mem_ref[at, :]
        kvc_ref[at, 0:width] = dot_nn(block, wc_ref[1]).astype(bf16)
        kvc_ref[at, width:] = (dot_nn(block, wc_ref[2]) + bias_ref[5:6, :]).astype(bf16)
        return carry

    lax.fori_loop(live_first, live_last, project, 0)
    attn_self = a_ref[...]
    a_low = attn_self.astype(bf16)
    a_low_ref[...] = a_low
    r1 = x_ref[...].astype(f32) + (dot_nn(a_low, wc_ref[3]) + bias_ref[2:3, :])
    r1_ref[...] = r1
    n1, inv1 = norm_stats(r1)
    h1 = n1 * gain_ref[0:1, :] + bias_ref[3:4, :]
    h1_low = h1.astype(bf16)
    h1_ref[...] = h1_low
    qc = (dot_nn(h1_low, wc_ref[0]) + bias_ref[4:5, :]).astype(bf16)
    qc_ref[...] = qc
    fine = None
    for block in range(2):
        at = slice(block * half, (block + 1) * half)
        acc_ref[...] = jnp.zeros(acc_ref.shape, f32)
        attend_plain(
            qc[at], kvc_ref, cols_ref[at, 2:3], cols_ref[at, 3:4], over_range(*cross_range[block]),
            cross_block, factor, acc_ref,
        )
        top, weights = weighted_rows(acc_ref)
        cross_ref[at, :] = top / weights
        lane_ref[at, :] = jnp.log2(weights)
        fine = in_range(weights) if fine is None else fine & in_range(weights)

    @pl.when(jnp.logical_not(fine))
    def _():
        for block in range(2):
            at = slice(block * half, (block + 1) * half)
            cross_ref[at, :], lane_ref[at, :] = attend_running(
                qc_ref[at, :], [(kvc_ref, over_range(*cross_range[block]))],
                cols_ref[at, 2:3], cols_ref[at, 3:4], cross_block, factor, (max_ref, sum_ref, run_ref),
            )

    cross_log_ref[...] = log_rows_of(lane_ref[...])
    attn_cross = cross_ref[...]
    ac_low = attn_cross.astype(bf16)
    ac_ref[...] = ac_low
    r2 = h1 + (dot_nn(ac_low, wc_ref[4]) + bias_ref[6:7, :])
    n2, inv2 = norm_stats(r2)
    h2 = n2 * gain_ref[1:2, :] + bias_ref[7:8, :]
    h2_low = h2.astype(bf16)
    h2_ref[...] = h2_low
    u = dot_nn(h2_low, u_ref[...]) + ffn_bias_ref[...]
    sig = 1.0 / (1.0 + jnp.exp(-u))
    act = (u / (1.0 + jnp.exp(-u))).astype(bf16)
    f_ref[...] = act
    slope = sig * (1.0 + u * (1.0 - sig))
    r3 = h2 + (dot_nn(act, v_ref[...]) + bias_ref[8:9, :])
    n3, inv3 = norm_stats(r3)
    out_ref[...] = n3 * gain_ref[2:3, :] + bias_ref[9:10, :]
    sums_ref[...] = jnp.zeros_like(sums_ref)
    upstream = g_ref[...].astype(f32)
    sums_ref[2:3, :] = column_sum(upstream * n3)
    sums_ref[12:13, :] = column_sum(upstream)
    gr3 = norm_back(n3, inv3, gain_ref[2:3, :], upstream)
    e3 = gr3.astype(bf16)
    e3_ref[...] = e3
    sums_ref[11:12, :] = column_sum(e3)
    gu = (dot_nt(e3, v_ref[...]) * slope).astype(bf16)
    gu_ref[...] = gu
    csum_ref[...] = column_sum(gu)
    gh2 = gr3 + dot_nt(gu, u_ref[...])
    sums_ref[1:2, :] = column_sum(gh2 * n2)
    sums_ref[10:11, :] = column_sum(gh2)
    gr2 = norm_back(n2, inv2, gain_ref[1:2, :], gh2)
    gr2_ref[...] = gr2
    e2 = gr2.astype(bf16)
    e2_ref[...] = e2
    sums_ref[9:10, :] = column_sum(e2)


def middle_backward_kernel(
    info_ref, a_ref, log_ref, rows_ref, gain_ref, wc_ref, e2_ref, gr2_ref, r1_ref, qc_ref,
    cross_ref, cross_log_ref, kvc_ref, sums_in_ref,
    e1_ref, dqc_ref, ga_ref, gr1_ref, delta_ref, dkvc_ref, sums_ref, dq_ref,
    *, factor, scale, cross_rows,
):
    info = RowInfo(info_ref)
    rows, width = a_ref.shape
    half = rows // 2
    cross_block = cross_rows
    cross_range = [info.cross_keys(block, cross_block) for block in range(2)]
    live_first = jnp.minimum(cross_range[0][0], cross_range[1][0])
    live_last = jnp.maximum(cross_range[0][1], cross_range[1][1])
    sums_ref[...] = sums_in_ref[...]
    n1, inv1 = norm_stats(r1_ref[...])
    attn_self, attn_cross = a_ref[...], cross_ref[...]
    gr2, e2, qc, cross_logs = gr2_ref[...], e2_ref[...], qc_ref[...], cross_log_ref[...]

    def clear(index, carry):
        at = pl.ds(pl.multiple_of(index * cross_block, cross_block), cross_block)
        dkvc_ref[at, :] = jnp.zeros((cross_block, 2 * width), bf16)
        return carry

    lax.fori_loop(live_first, live_last, clear, 0)
    gac = dot_nt(e2, wc_ref[4]).astype(bf16)
    sums_ref[8:9, :] = column_sum(gac)
    delta_cross = head_sums(gac.astype(f32) * attn_cross)
    grads = []
    for block in (1, 0):
        at = slice(block * half, (block + 1) * half)
        grads.append(
            attend_back(
                qc[at], gac[at], kvc_ref, dkvc_ref, rows_ref[2:3, at], rows_ref[3:4, at],
                [pair_rows(cross_logs, block, half, p) for p in range(PAIRS)],
                [pair_rows(delta_cross, block, half, p) for p in range(PAIRS)],
                *cross_range[block], cross_block, factor, scale,
                dq_ref, True,
            )
        )
    dqc = jnp.concatenate([grads[1], grads[0]], axis=0).astype(bf16)
    dqc_ref[...] = dqc
    sums_ref[7:8, :] = column_sum(dqc)
    gh1 = gr2 + dot_nt(dqc, wc_ref[0])
    sums_ref[0:1, :] = column_sum(gh1 * n1)
    sums_ref[6:7, :] = column_sum(gh1)
    gr1 = norm_back(n1, inv1, gain_ref[0:1, :], gh1)
    gr1_ref[...] = gr1
    e1 = gr1.astype(bf16)
    e1_ref[...] = e1
    sums_ref[5:6, :] = column_sum(e1)
    ga = dot_nt(e1, wc_ref[3]).astype(bf16)
    ga_ref[0:rows, :] = ga
    sums_ref[4:5, :] = column_sum(ga)
    delta = head_sums(ga.astype(f32) * attn_self)
    delta_ref[...] = delta
    extra = split_three(side_by_side(log_ref[...])) + split_three(side_by_side(delta))
    extra.append(jnp.zeros((2 * HEADS // 2, width), bf16))
    ga_ref[rows:, :] = jnp.concatenate([e.astype(f32) for e in extra], axis=0).astype(bf16)


def memory_grads_kernel(
    info_ref, mem_ref, wc_ref, dkvc_ref, pm_ref, dwc_ref, dw_acc_ref, *, cross_block
):
    info = RowInfo(info_ref)
    width = mem_ref.shape[1]
    cross_range = [info.cross_keys(block, cross_block) for block in range(2)]
    live_first = jnp.minimum(cross_range[0][0], cross_range[1][0])
    live_last = jnp.maximum(cross_range[0][1], cross_range[1][1])
    pm_ref[...] = jnp.zeros(pm_ref.shape, f32)
    dw_acc_ref[...] = jnp.zeros(dw_acc_ref.shape, f32)

    def memory_step(index, carry):
        at = pl.ds(pl.multiple_of(index * cross_block, cross_block), cross_block)
        grads_block = dkvc_ref[at, :]
        block = dot_nt(grads_block[:, :width], wc_ref[1]) + dot_nt(grads_block[:, width:], wc_ref[2])
        pm_ref[at, :] = block
        dw_acc_ref[...] += dot_tn(mem_ref[at, :], grads_block)
        return carry

    lax.fori_loop(live_first, live_last, memory_step, 0)
    dwc_ref[...] = dw_acc_ref[...].astype(bf16)


def query_backward_kernel(
    info_ref, q_ref, ga_ref, kv_near_ref, kv_far_ref, log_ref, delta_ref, cols_ref, dq_ref, acc_ref,
    log_rep_ref, delta_rep_ref, *, factor, scale, planes,
):
    info = RowInfo(info_ref)
    rows = q_ref.shape[0]
    half = info.half
    pad = jnp.zeros((128 - 2 * HEADS, rows), f32)
    stat_cols = jnp.transpose(jnp.concatenate([log_ref[...], delta_ref[...], pad], axis=0))

    def stat_column(at, head):
        return jnp.concatenate(
            [stat_cols[at, head : head + 1], stat_cols[at, head + 1 : head + 2]], axis=0
        )

    for block in range(2):
        at = slice(block * half, (block + 1) * half)
        acc_ref[...] = jnp.zeros(acc_ref.shape, f32)
        for p in range(PAIRS):
            log_rep_ref[p] = jnp.broadcast_to(stat_column(at, 2 * p), log_rep_ref.shape[1:])
            delta_rep_ref[p] = jnp.broadcast_to(stat_column(at, HEADS + 2 * p), log_rep_ref.shape[1:])
        for part, kv_ref in enumerate((kv_near_ref, kv_far_ref)):
            query_grads(
                q_ref[at, :], ga_ref[at, :], kv_ref, cols_ref[at, 0:1], cols_ref[at, 1:2],
                log_rep_ref, delta_rep_ref,
                over_planes(info, part * planes, planes, *info.self_keys(block)),
                self_block, factor, acc_ref,
            )
        dq_ref[at, :] = (merged_rows(acc_ref) * scale).astype(bf16)


def key_backward_kernel(
    info_ref, kv_rows_ref, q_all_ref, cols_ref, *refs, factor, scale, planes, part, last,
    total_planes,
):
    state_in, refs = (refs[:2], refs[2:]) if part else ((), refs)
    pieces, refs = refs[:4], refs[4:]
    if last:
        dk_out_ref, dv_out_ref, g_ref, stats_ref, dk_ref, dv_ref = refs
    else:
        dk_ref, dv_ref, g_ref, stats_ref = refs
    info = RowInfo(info_ref)
    half = info.half
    rows = 2 * half
    width = q_all_ref.shape[1]
    for s, bits, chunk in chunk_views(pieces, planes):
        place = (info.me & 3) ^ bits
        extra = chunk[rows : rows + chunk_rows, :].astype(f32)
        logs = extra[0:4] + extra[4:8] + extra[8:12]
        deltas = extra[12:16] + extra[16:20] + extra[20:24]
        for side in range(2):
            block = 8 * s + 4 * side + (place if side == 0 else 3 - place)
            lanes = slice(side * half, (side + 1) * half)
            high = slice(rows + side * half, rows + (side + 1) * half)
            g_ref[pl.ds(pl.multiple_of(block * half, half), half), :] = chunk[lanes, :]
            stats_ref[block] = jnp.concatenate(
                [logs[:, lanes], logs[:, high], deltas[:, lanes], deltas[:, high]], axis=0
            )

    def groups(first, stop):
        def run(step):
            def visit(stored, carry):
                plane = info.plane ^ (part * planes + (stored >> 1))
                index = jnp.where((stored & 1) == 0, plane, 2 * total_planes - 1 - plane)

                @pl.when((index >= first) & (index < stop))
                def _():
                    step(stored, index)

                return carry

            lax.fori_loop(0, 2 * planes, visit, 0)

        return run

    for block in range(2):
        at = slice(block * half, (block + 1) * half)
        if part:
            dk_ref[block] = state_in[0][block]
            dv_ref[block] = state_in[1][block]
        else:
            dk_ref[block] = jnp.zeros(dk_ref.shape[1:], f32)
            dv_ref[block] = jnp.zeros(dv_ref.shape[1:], f32)
        key_grads(
            kv_rows_ref[at, 0:width], kv_rows_ref[at, width:], q_all_ref, g_ref, stats_ref,
            cols_ref[at, 1:2], cols_ref[at, 4:5], groups(*info.queries(block)), factor,
            dk_ref.at[block], dv_ref.at[block],
        )
    if not last:
        return
    dk = jnp.concatenate([merged_rows(dk_ref.at[b]) for b in range(2)], axis=0) * scale
    dv = jnp.concatenate([merged_rows(dv_ref.at[b]) for b in range(2)], axis=0)
    dk_out_ref[...] = dk.astype(bf16)
    dv_out_ref[...] = dv.astype(bf16)


def self_grads_kernel(
    info_ref, x_ref, gr1_ref, dq_ref, dk_ref, dv_ref, w_ref, tok_ref, *refs, plain
):
    sink_refs, (dw_ref,) = (refs[:1], refs[1:]) if plain else (refs[:2], refs[2:])
    info = RowInfo(info_ref)
    dk, dv = dk_ref[...], dv_ref[...]
    tok = gr1_ref[...] + dot_nt(dq_ref[...], w_ref[0]) + dot_nt(dk, w_ref[1]) + dot_nt(dv, w_ref[2])
    tok_ref[...] = tok.astype(bf16)
    sink = PlainSink(*sink_refs) if plain else PieceSink(*sink_refs, dw_ref, info.me, info.side)
    x_rows = x_ref[...]
    sink.put(0, dot_tn(x_rows, dk))
    sink.put(1, dot_tn(x_rows, dv))


def feed_grads_kernel(info_ref, h2_ref, gu_ref, f_ref, e3_ref, *refs, plain):
    sink_refs, (dw_ref,) = (refs[:1], refs[1:]) if plain else (refs[:2], refs[2:])
    info = RowInfo(info_ref)
    sink = PlainSink(*sink_refs) if plain else PieceSink(*sink_refs, dw_ref, info.me, info.side)
    width = h2_ref.shape[1]
    parts = gu_ref.shape[1] // width
    for k in range(parts):
        sink.put(k, dot_tn(h2_ref[...], gu_ref[:, k * width : (k + 1) * width]))
    sink.put(parts, dot_tn(f_ref[...], e3_ref[...]))


def map_grads_kernel(
    info_ref, a_ref, e1_ref, ac_ref, e2_ref, h1_ref, dqc_ref, dwc_ref, x_ref, dq_ref, sums_ref,
    csum_ref, *refs, plain,
):
    sink_refs, (dw_ref,) = (refs[:1], refs[1:]) if plain else (refs[:2], refs[2:])
    info = RowInfo(info_ref)
    sink = PlainSink(*sink_refs) if plain else PieceSink(*sink_refs, dw_ref, info.me, info.side)
    width = a_ref.shape[1]
    sink.put(0, dot_tn(a_ref[...], e1_ref[...]))
    sink.put(1, dot_tn(ac_ref[...], e2_ref[...]))
    sink.put(2, dot_tn(h1_ref[...], dqc_ref[...]))
    sink.put(3, dwc_ref[:, :width])
    sink.put(4, dwc_ref[:, width:])
    sink.put(5, dot_tn(x_ref[...], dq_ref[...]))
    put_small(sink, 6, dw_ref, sums_ref[...], csum_ref, dq_ref[...])


def grads_project_kernel(info_ref, w_ref, bias_ref, *refs, planes, plain):
    pieces, refs = refs[:8], refs[8:]
    inputs, refs = refs[:11], refs[11:]
    q_ref, outs = refs[0], refs[1:]
    map_grads_kernel(info_ref, *inputs, *outs, plain=plain)
    project_kernel(info_ref, w_ref, bias_ref, *pieces, q_ref, planes=planes)


def put_small(sink, block, dw_ref, sums, csum_ref, dq):
    dw_ref[...] = jnp.zeros(dw_ref.shape, f32)
    row = lax.broadcasted_iota(jnp.int32, sums.shape, 0)
    sums = jnp.where(row == 3, column_sum(dq), sums)
    lanes = csum_ref.shape[1] // 8
    for yh in range(2):
        base = yh * half_rows
        dw_ref[base : base + 16, 0:lanes] = sums[:, yh * lanes : (yh + 1) * lanes]
        for k in range(4):
            start = yh * 4 * lanes + k * lanes
            dw_ref[base + 16 + k : base + 17 + k, 0:lanes] = csum_ref[:, start : start + lanes]
    if isinstance(sink, PlainSink):
        sink.plain[block] = dw_ref[...].astype(bf16)
    else:
        sink.emit(block, half_rows, 0)


def place_kernel(info_ref, *refs, places):
    sources, outs = refs[:4], refs[4:]
    info = RowInfo(info_ref)
    planes = sources[0].shape[0]
    piece = half_rows // (4 * planes)
    for s in range(planes):
        for bits in range(4):
            owner = info.me ^ (4 * s + bits)
            source = sources[(bits >> 1) + 2 * (bits & 1)]
            for block, (number, kind, k) in enumerate(places):
                rows = source[s, block * piece : (block + 1) * piece, :].astype(f32)
                width = rows.shape[1]
                base = k * half_rows if kind == "rows" else 0
                at = pl.ds(pl.multiple_of(base + owner * piece, piece), piece)
                if kind == "lead":
                    outs[number][k, at, :] = rows
                elif kind == "cols":
                    outs[number][at, k * width : (k + 1) * width] = rows
                else:
                    outs[number][at, :] = rows


def place_maps_kernel(
    info_ref, own_ref, other_ref, own_core_ref, other_core_ref, ins_ref, outs_ref, gain_ref, bias_ref,
    shift_ref, rest_ref,
):
    place_kernel(
        info_ref, own_ref, other_ref, own_core_ref, other_core_ref, ins_ref, outs_ref, rest_ref,
        places=[(1, "lead", 0), (1, "lead", 1)]
        + [(0, "lead", k) for k in (3, 4, 5, 0)]
        + [(2, "rows", 0), (0, "lead", 1), (0, "lead", 2)],
    )
    lanes = gain_ref.shape[1]
    gain_ref[...] = rest_ref[0:3, 0:lanes]
    bias_ref[...] = rest_ref[3:13, 0:lanes]
    shift_ref[...] = rest_ref[16:20, 0:lanes]


def call_kernel(kernel, inputs, outputs, scratch, name, micros, in_place=()):
    vmem = pl.BlockSpec(memory_space=pltpu.VMEM)
    smem = pl.BlockSpec(memory_space=pltpu.SMEM)
    return pl.pallas_call(
        kernel,
        in_specs=[smem]
        + [
            pl.BlockSpec(memory_space=pl.ANY) if index in in_place else vmem
            for index in range(1, len(inputs))
        ],
        out_specs=[vmem] * len(outputs),
        out_shape=[jax.ShapeDtypeStruct(*entry) for entry in outputs],
        scratch_shapes=[pltpu.VMEM(*entry) if isinstance(entry, tuple) else entry for entry in scratch],
        compiler_params=pltpu.CompilerParams(vmem_limit_bytes=vmem_bytes),
        cost_estimate=pl.CostEstimate(
            flops=int(micros * 1e9), transcendentals=0, bytes_accessed=int(micros * 1e4)
        ),
        name=name,
    )(*inputs)


def exchange(value, bits):
    count = lax.axis_size("ctx")
    return lax.ppermute(value, "ctx", [(i, i ^ bits) for i in range(count)])


def swap_side(value):
    return lax.ppermute(value, "fsdp", [(0, 1), (1, 0)])


def after(value, *others):
    return lax.optimization_barrier((value,) + others)[0]


def fetch_planes(value, first, last):
    return [exchange(value, 4 * s) if s else value for s in range(first, last)]


def fetch_chips(chunks):
    return [chunks, exchange(chunks, 2)]


def fetch_cores(pair):
    return pair + [exchange(chunks, 1) for chunks in pair]


def core_part(shard, axis):
    rows = shard.shape[axis] // 2
    return lax.dynamic_slice_in_dim(shard, (lax.axis_index("ctx") % 2) * rows, rows, axis)


def add_cores(keep, send):
    other = exchange(send, 1)
    return keep[0].astype(f32) + other[0].astype(f32), (
        keep[1].astype(f32) + other[1].astype(f32)
    ).astype(bf16)


def add_sides(kept, sent):
    return kept + swap_side(sent).astype(f32)


def add_chips(part, low):
    return part[0] + exchange(low, 2).astype(f32)


def low_planes(part):
    return [part[s].astype(bf16) for s in range(1, part.shape[0])]


def add_planes(part, low):
    total = part[0]
    for s, sent in enumerate(low):
        total = total + exchange(sent, 4 * (s + 1)).astype(f32)
    return total


def spread_planes(low):
    planes = lax.axis_size("ctx") // 4
    return [low] + [exchange(low, 4 * s) for s in range(1, planes)]


def spread_chips(chunks, before=None):
    own = jnp.stack(chunks)
    other = exchange(own, 2)
    sent = [own, other] if before is None else [after(own, before), after(other, before)]
    return [own, other] + [exchange(chunk, 1) for chunk in sent]


def zigzag_perms(count):
    def worker(block):
        return block if block < count else 2 * count - 1 - block

    first = [(owner, worker(2 * owner)) for owner in range(count)]
    second = [(owner, worker(2 * owner + 1)) for owner in range(count)]
    return first, second


def body(
    tokens, memory, token_seg, memory_seg, out_grad,
    in_proj, out_proj, ffn_in, ffn_out, norm_gain, bias_rows, ffn_bias,
):
    count = lax.axis_size("ctx")
    sides = lax.axis_size("fsdp")
    planes = count // 4
    plain = sides != 2
    me = lax.axis_index("ctx")
    side = lax.axis_index("fsdp")
    row_count, width = tokens.shape[1], tokens.shape[2]
    mem_count = memory.shape[1]
    half = row_count // 2
    scale = 1.0 / math.sqrt(width // HEADS)
    factor = scale * math.log2(math.e)
    total = row_count * count
    mem_total = mem_count * count
    near, far = planes // 2, planes - planes // 2

    x_planes = fetch_planes(tokens[0], 0, planes)
    small = jnp.concatenate(
        [norm_gain, bias_rows, ffn_bias.reshape(-1, norm_gain.shape[1])], axis=0
    ).astype(bf16)
    maps_low = jnp.concatenate([in_proj, out_proj], axis=0).astype(bf16)
    up_low, down_low = ffn_in.astype(bf16), ffn_out.astype(bf16)
    if plain:
        small = lax.all_gather(small, "fsdp").astype(f32)
        whole = lax.all_gather(maps_low, "fsdp", axis=1, tiled=True)
        self_maps = (whole,)
        late_maps = (
            whole, lax.all_gather(up_low, "fsdp", axis=0, tiled=True),
            lax.all_gather(down_low, "fsdp", axis=0, tiled=True),
        )
    else:
        small_rows = small.shape[0]
        pad = jnp.zeros((32 - small_rows, small.shape[1]), bf16)
        sent = jnp.concatenate(
            [
                core_part(in_proj[0:3], 1).astype(bf16).reshape(-1, width),
                jnp.concatenate([small, pad], axis=0).reshape(-1, width),
            ],
            axis=0,
        )
        fetched = swap_side(sent)
    x_near = fetch_chips(jnp.stack(x_planes[:near]))
    if not plain:
        ready = after(fetched, x_near[1])
        table_rows = ready[-pad.shape[1] * 32 // width :].reshape(32, -1)[:small_rows]
        small = jnp.stack([small, table_rows])
        small = jnp.where(side == 0, small, small[::-1]).astype(f32)
        self_maps = (maps_low, ready, exchange(ready, 1))
        up_part = core_part(after(ffn_in, sent), 0).astype(bf16)
        late_parts = [
            core_part(in_proj[3:6], 1).astype(bf16).reshape(-1, width),
            core_part(after(out_proj, sent), 1).astype(bf16).reshape(-1, width),
            core_part(after(ffn_out, sent), 0).astype(bf16),
        ]
        late_parts += [
            up_part[:, k * width : (k + 1) * width] for k in range(up_part.shape[1] // width)
        ]
        late_sent = jnp.concatenate(late_parts, axis=0)
        late = swap_side(after(late_sent, fetched))
    started = x_near[0] if plain else fetched
    x_far = fetch_chips(jnp.stack([after(chunk, started) for chunk in x_planes[near:]]))

    perm_first, perm_second = zigzag_perms(count)
    even = me % 2 == 0
    first_sent = small if plain else sent
    rows_in = jnp.stack([after(tokens[0], first_sent, x_near[0]), out_grad[0]])
    one = lax.ppermute(rows_in[:, :half], "ctx", perm_first)
    two = lax.ppermute(rows_in[:, half:], "ctx", perm_second)
    rows_in = jnp.where(
        even, jnp.concatenate([one, two], axis=1), jnp.concatenate([two, one], axis=1)
    )
    x_rows, g_rows = rows_in[0], rows_in[1]

    table = small[:, 0:13].transpose(1, 0, 2).reshape(13, width)
    gains, biases = table[0:3], table[3:13]
    ffn_shift = small[:, 13:].reshape(1, -1)

    m_all = lax.all_gather(memory[0], "ctx", axis=0, tiled=True)

    segs, mem_segs = after(token_seg[0], first_sent), after(memory_seg[0], first_sent)
    step = jnp.arange(half, dtype=jnp.int32)
    row_pos = jnp.concatenate([me * half + step, (2 * count - 1 - me) * half + step])
    row_seg = jnp.concatenate(
        [
            lax.dynamic_slice_in_dim(segs, me * half, half),
            lax.dynamic_slice_in_dim(segs, (2 * count - 1 - me) * half, half),
        ]
    )

    def below(keys, closed):
        hits = keys[None, :] <= row_seg[:, None] if closed else keys[None, :] < row_seg[:, None]
        return jnp.sum(hits, axis=1, dtype=jnp.int32)

    ones = jnp.ones_like(row_pos)
    info = jnp.stack(
        [
            below(segs, False), row_pos, below(mem_segs, False), below(mem_segs, True) - 1,
            below(segs, True) - 1, me * ones, side * ones, ones,
        ]
    )
    cols = info.T

    tile = width // PAIRS
    column = ((PAIRS, row_count, 1), f32)
    square = ((PAIRS, row_count, tile), f32)
    two_squares = ((2, PAIRS, row_count, tile), f32)
    rows_low = ((row_count, width), bf16)
    rows_full = ((row_count, width), f32)
    kv_rows_shape = ((row_count, 2 * width), bf16)

    x_near = fetch_cores(x_near)
    x_near[0] = after(x_near[0], x_far[0], up_low, down_low)
    wide = ((PAIRS, row_count, 2 * tile), f32)
    q_rows, kv_rows, kv_near, w_self, top, weights = call_kernel(
        lambda *refs: first_forward_kernel(
            *refs, factor=factor, planes=near, shards=len(self_maps)
        ),
        (info, x_rows, biases, cols, *self_maps, *x_near),
        (
            rows_low, kv_rows_shape, ((4 * near * row_count, 2 * width), bf16),
            ((3, width, width), bf16), rows_full, rows_full,
        ),
        [wide],
        "first_forward",
        10,
    )
    x_far = fetch_cores([after(chunks, top) for chunks in x_far])
    a_rows, log_rows, kv_far = call_kernel(
        lambda *refs: second_forward_kernel(*refs, factor=factor, planes=far),
        (info, kv_near, q_rows, biases, cols, w_self, top, weights, *x_far),
        (rows_full, ((HEADS, row_count), f32), ((4 * far * row_count, 2 * width), bf16)),
        [
            wide, column, column, square, rows_full, ((4 * near * row_count, 2 * width), bf16),
            pltpu.SemaphoreType.DMA,
        ],
        "second_forward",
        10,
        (1,),
    )
    if not plain:
        late = after(late, a_rows)
        late_maps = (maps_low, up_low, down_low, late, exchange(late, 1))
    ff_width = ffn_in.shape[1]
    ff_rows = ((row_count, ff_width), bf16)
    by_head = ((HEADS, row_count), f32)
    kvc_shape = ((mem_total, 2 * width), bf16)
    sums_shape = ((16, width), f32)
    whole_maps = [] if plain else [((width, ff_width), bf16), ((ff_width, width), bf16)]
    (
        out_rows, a_low, h1_low, h2_low, act, e3, gu, e2, ac_low, gr2, r1, qc, cross, cross_log,
        kvc, sums, csum, w_cross,
    ) = call_kernel(
        lambda *refs: middle_forward_kernel(
            *refs, factor=factor, shards=len(self_maps), cross_rows=2 * mem_count
        ),
        (info, x_rows, a_rows, g_rows, cols, gains, biases, ffn_shift, m_all, *late_maps),
        (
            rows_full, rows_low, rows_low, rows_low, ff_rows, rows_low, ff_rows, rows_low, rows_low,
            rows_full, rows_full, rows_low, rows_full, by_head, kvc_shape, sums_shape,
            ((1, ff_width), f32), ((5, width, width), bf16),
        ),
        [wide, column, column, square, rows_full, *whole_maps],
        "middle_forward",
        25,
    )

    def sink_shapes(blocks):
        if plain:
            return [((blocks, width, width), bf16)]
        return [((2, 2, planes, blocks * (half_rows // count), width), bf16)] * 2

    feed = call_kernel(
        lambda *refs: feed_grads_kernel(*refs, plain=plain),
        (info, h2_low, gu, act, e3),
        sink_shapes(8),
        [((ff_width, width), f32)],
        "feed_grads",
        5,
    )
    gr2 = after(gr2, *feed)
    e1, dqc, ga, gr1, delta, dkvc, sums = call_kernel(
        lambda *refs: middle_backward_kernel(
            *refs, factor=factor, scale=scale, cross_rows=2 * mem_count
        ),
        (
            info, a_rows, log_rows, info, gains, w_cross, e2, gr2, r1, qc, cross, cross_log, kvc,
            sums,
        ),
        (
            rows_low, rows_low, ((row_count + chunk_rows, width), bf16), rows_full, by_head,
            kvc_shape, sums_shape,
        ),
        [((PAIRS, tile, row_count), f32)],
        "middle_backward",
        14,
    )
    g_planes = fetch_planes(ga, 0, near)
    if not plain:
        feed = add_cores(*feed)
        dkvc = after(dkvc, feed[1])
    mem_part, dwc = call_kernel(
        lambda *refs: memory_grads_kernel(*refs, cross_block=2 * mem_count),
        (info, m_all, w_cross, dkvc),
        (((mem_total, width), f32), ((width, 2 * width), bf16)),
        [((width, 2 * width), f32)],
        "memory_grads",
        5,
    )
    g_near = fetch_chips(jnp.stack([after(chunk, mem_part) for chunk in g_planes]))
    g_planes = fetch_planes(after(ga, mem_part), near, planes)
    (dq,) = call_kernel(
        lambda *refs: query_backward_kernel(*refs, factor=factor, scale=scale, planes=near),
        (info, after(q_rows, g_near[0]), ga, kv_near, kv_far, log_rows, delta, cols),
        (rows_low,),
        [square, square, square],
        "query_backward",
        20,
    )
    g_far = fetch_chips(jnp.stack([after(chunk, dq) for chunk in g_planes]))
    g_near = fetch_cores([after(chunks, dq) for chunks in g_near])
    if not plain:
        feed = add_sides(*feed)
        feed_low = feed[1].astype(bf16)
        h1_low = after(h1_low, feed_low)
    q_all, *maps = call_kernel(
        lambda *refs: grads_project_kernel(*refs, planes=near, plain=plain),
        (
            info, w_self, biases, *x_near, *x_far, a_low, e1, ac_low, e2,
            after(h1_low, g_far[0], g_near[1]), dqc, dwc, x_rows, dq, sums, csum,
        ),
        [((total, width), bf16)] + sink_shapes(7),
        [((width, width), f32)],
        "grads_project",
        12,
    )
    if not plain:
        maps = add_cores(*maps)
        feed_low = after(feed_low, q_all)
        kv_rows = after(kv_rows, maps[1], feed_low)
    mem_part = after(mem_part, g_far[1])
    memory_grad = lax.psum_scatter(mem_part, "ctx", scatter_dimension=0, tiled=True)
    g_far = fetch_cores([after(chunks, q_all) for chunks in g_far])
    dk_part, dv_part = call_kernel(
        lambda *refs: key_backward_kernel(
            *refs, factor=factor, scale=scale, planes=near, part=0, last=False,
            total_planes=planes,
        ),
        (info, kv_rows, q_all, cols, *g_near),
        [two_squares, two_squares],
        [
            ((4 * near * row_count, width), bf16), ((8 * near, 2 * HEADS, half), f32),
        ],
        "key_backward",
        8,
    )
    if not plain:
        feed = feed[0] + after(exchange(feed_low, 2), dk_part).astype(f32)
        feed_low = low_planes(feed)
        dk_part = after(dk_part, *feed_low)
    dk, dv = call_kernel(
        lambda *refs: key_backward_kernel(
            *refs, factor=factor, scale=scale, planes=far, part=1, last=True, total_planes=planes
        ),
        (info, kv_rows, q_all, cols, dk_part, dv_part, *g_far),
        [rows_low, rows_low],
        [
            ((4 * far * row_count, width), bf16), ((8 * far, 2 * HEADS, half), f32),
            two_squares, two_squares,
        ],
        "key_backward_last",
        3,
    )
    if not plain:
        feed = add_planes(feed, feed_low).astype(bf16)
        maps = add_sides(*maps)
        maps_low = maps[1].astype(bf16)
        dk = after(dk, feed, maps_low)
    tok_rows, *last = call_kernel(
        lambda *refs: self_grads_kernel(*refs, plain=plain),
        (info, x_rows, gr1, dq, dk, dv, w_self),
        [rows_low] + sink_shapes(2),
        [((width, width), f32)],
        "self_grads",
        4,
    )

    back_first = [(to, owner) for owner, to in perm_first]
    back_second = [(to, owner) for owner, to in perm_second]

    rows_out = jnp.stack([out_rows.astype(bf16), tok_rows])
    half_one = jnp.where(even, rows_out[:, :half], rows_out[:, half:])
    half_two = jnp.where(even, rows_out[:, half:], rows_out[:, :half])
    rows_out = jnp.concatenate(
        [lax.ppermute(half_one, "ctx", back_first), lax.ppermute(half_two, "ctx", back_second)],
        axis=1,
    ).astype(f32)
    layer_out, tokens_grad = rows_out[0], rows_out[1]
    lanes = width // 2
    if plain:

        def owned(matrix, axis):
            part = lax.psum_scatter(matrix, "fsdp", scatter_dimension=axis, tiled=True)
            return lax.psum(part, "ctx").astype(f32)

        feed, maps, last = feed[0], maps[0], last[0]
        ins = owned(jnp.concatenate([maps[5:6], last, maps[2:5]], axis=0), 1)
        outs = owned(maps[0:2], 1)
        up = owned(jnp.concatenate([feed[k] for k in range(4)], axis=1), 0)
        down = owned(feed[4:8].reshape(-1, width), 0)
        rest = jnp.stack([maps[6, 0:half_rows, 0:lanes], maps[6, half_rows:, 0:lanes]], axis=1)
        table = owned(rest[0:13].reshape(13, width).astype(f32), 1)
        shift = owned(rest[16:20].transpose(1, 0, 2).reshape(-1).astype(f32), 0)
        gain_sums, bias_sums = table[0:3], table[3:13]
    else:
        feed_planes = spread_planes(feed)
        last = add_sides(*add_cores(*last))
        last_low = after(last[1].astype(bf16), *feed_planes[1:])
        feed_own = jnp.stack(feed_planes)
        feed_other = exchange(feed_own, 2)
        last = add_chips(last, last_low)
        maps = add_chips(maps, maps_low)
        maps = add_planes(maps, low_planes(maps)).astype(bf16)
        last = add_planes(last, [after(low, maps) for low in low_planes(last)]).astype(bf16)
        up, down = call_kernel(
            lambda *refs: place_kernel(
                *refs,
                places=[(0, "cols", k) for k in range(4)] + [(1, "rows", k) for k in range(4)],
            ),
            (info, feed_own, feed_other, exchange(feed_own, 1), exchange(feed_other, 1)),
            ((ffn_in.shape, f32), (ffn_out.shape, f32)),
            [],
            "place_feed",
            4,
        )
        maps = jnp.concatenate([maps, after(last, feed_other)], axis=0)
        ins, outs, gain_sums, bias_sums, shift = call_kernel(
            place_maps_kernel,
            (info, *spread_chips(spread_planes(maps), up)),
            (
                (in_proj.shape, f32), (out_proj.shape, f32), ((3, lanes), f32), ((10, lanes), f32),
                ((4, lanes), f32),
            ),
            [((half_rows, width), f32)],
            "place_maps",
            4,
        )
        shift = shift.reshape(-1)
    return (
        layer_out[None], tokens_grad[None], memory_grad[None], ins, outs, up, down,
        gain_sums, bias_sums, shift,
    )


def solution(mesh):
    rows = P("fsdp", "ctx", None)
    params = (
        P(None, "fsdp", None), P(None, "fsdp", None), P("fsdp", None), P("fsdp", None),
        P(None, "fsdp"), P(None, "fsdp"), P("fsdp"),
    )
    return jax.shard_map(
        body,
        mesh=mesh,
        in_specs=(rows, rows, P("fsdp", None), P("fsdp", None), rows) + params,
        out_specs=(rows, rows, rows) + params,
        check_vma=False,
    )
```

```python
import math

import jax
import jax.numpy as jnp
from jax import lax
from jax.experimental import pallas as pl
from jax.experimental.pallas import tpu as pltpu
from jax.sharding import PartitionSpec as P

HEADS = 8
PAIRS = HEADS // 2
neg_fill = -1e30
eps_norm = 1e-05
self_block = 512
bf16 = jnp.bfloat16
f32 = jnp.float32
vmem_bytes = 60 * 1024 * 1024
half_rows = 256
chunk_rows = 32


def dot_nn(first_op, second_op):
    return jnp.dot(first_op, second_op, preferred_element_type=f32)


def dot_nt(first_op, second_op):
    return lax.dot_general(
        first_op, second_op, (((1,), (1,)), ((), ())), preferred_element_type=f32
    )


def dot_tn(first_op, second_op):
    return lax.dot_general(
        first_op, second_op, (((0,), (0,)), ((), ())), preferred_element_type=f32
    )


def stack_heads(tile):
    lane = lax.broadcasted_iota(jnp.int32, tile.shape, 1)
    half = tile.shape[1] // 2
    zero = jnp.zeros_like(tile)
    return jnp.concatenate(
        [jnp.where(lane < half, tile, zero), jnp.where(lane >= half, tile, zero)], axis=0
    )


def merge_heads(stacked):
    rows = stacked.shape[0] // 2
    lane = lax.broadcasted_iota(jnp.int32, (rows, stacked.shape[1]), 1)
    return jnp.where(lane < stacked.shape[1] // 2, stacked[:rows], stacked[rows:])


def tile_of(value, pair, tile_width):
    return value[:, pair * tile_width : (pair + 1) * tile_width]


def head_sums(product):
    width = product.shape[1]
    head = lax.broadcasted_iota(jnp.int32, (HEADS, width), 0)
    lane = lax.broadcasted_iota(jnp.int32, (HEADS, width), 1)
    pick = (lane // (width // HEADS) == head).astype(f32)
    return lax.dot_general(
        pick,
        product,
        (((1,), (1,)), ((), ())),
        precision=lax.Precision.HIGHEST,
        preferred_element_type=f32,
    )


def over_range(first, last):
    def run(step):
        def visit(index, carry):
            step(index, index)
            return carry

        lax.fori_loop(first, last, visit, 0)

    return run


def over_planes(info, plane_first, plane_count, first, last):
    def run(step):
        def visit(stored, carry):
            index = 2 * (info.plane ^ (plane_first + (stored >> 1))) + (stored & 1)

            @pl.when((index >= first) & (index < last))
            def _():
                step(stored, index)

            return carry

        lax.fori_loop(0, 2 * plane_count, visit, 0)

    return run


class RowInfo:
    def __init__(self, info_ref):
        self.table = info_ref
        self.half = info_ref.shape[1] // 2
        self.me = info_ref[5, 0]
        self.side = info_ref[6, 0]
        self.plane = self.me >> 2

    def ends(self, block):
        return block * self.half, (block + 1) * self.half - 1

    def self_keys(self, block):
        start, stop = self.ends(block)
        return self.table[0, start] // self_block, self.table[1, stop] // self_block + 1

    def cross_keys(self, block, size):
        start, stop = self.ends(block)
        return self.table[2, start] // size, self.table[3, stop] // size + 1

    def queries(self, block):
        start, stop = self.ends(block)
        return self.table[1, start] // self_block, self.table[4, stop] // self_block + 1


def twice(column):
    return jnp.concatenate([column, column], axis=0)


def stacked_tiles(rows):
    tile_width = rows.shape[1] // PAIRS
    return [stack_heads(tile_of(rows, pair, tile_width)) for pair in range(PAIRS)]


def attend_plain(q_block, kv_ref, low_col, high_col, run, key_rows, factor, acc_ref):
    width = q_block.shape[1]
    tile_width = width // PAIRS
    stacked = stacked_tiles(q_block)
    low2, high2 = twice(low_col), twice(high_col)
    ones = jnp.ones((key_rows, tile_width), bf16)

    def step(stored, index):
        base = pl.multiple_of(stored * key_rows, key_rows)
        key_pos = index * key_rows + lax.broadcasted_iota(jnp.int32, (1, key_rows), 1)
        allowed = (key_pos >= low2) & (key_pos <= high2)
        def read(pair, offset):
            start = offset + pair * tile_width
            return kv_ref[pl.ds(base, key_rows), start : start + tile_width]

        scores = [dot_nt(stacked[0], read(0, 0))]
        for pair in range(PAIRS):
            if pair + 1 < PAIRS:
                scores.append(dot_nt(stacked[pair + 1], read(pair + 1, 0)))
            weights = jnp.where(allowed, jnp.exp2(scores[pair] * factor), 0.0).astype(bf16)
            acc_ref[pair] += dot_nn(weights, jnp.concatenate([read(pair, width), ones], axis=1))

    run(step)


def weighted_rows(acc_ref):
    tile_width = acc_ref.shape[2] // 2
    tops = [merge_heads(acc_ref[pair, :, 0:tile_width]) for pair in range(PAIRS)]
    sums = [merge_heads(acc_ref[pair, :, tile_width:]) for pair in range(PAIRS)]
    return jnp.concatenate(tops, axis=1), jnp.concatenate(sums, axis=1)


def in_range(sums):
    return (jnp.min(sums) > 2.0**-100) & (jnp.max(sums) < 2.0**100)


def attend_running(q_block, parts, low_col, high_col, key_rows, factor, scratch):
    max_ref, sum_ref, acc_ref = scratch
    width = q_block.shape[1]
    tile_width = width // PAIRS
    stacked = stacked_tiles(q_block)
    low2, high2 = twice(low_col), twice(high_col)
    max_ref[...] = jnp.full(max_ref.shape, neg_fill, f32)
    sum_ref[...] = jnp.zeros(sum_ref.shape, f32)
    acc_ref[...] = jnp.zeros(acc_ref.shape, f32)
    for kv_ref, run in parts:

        def step(stored, index, kv_ref=kv_ref):
            base = pl.multiple_of(stored * key_rows, key_rows)
            key_pos = index * key_rows + lax.broadcasted_iota(jnp.int32, (1, key_rows), 1)
            allowed = (key_pos >= low2) & (key_pos <= high2)
            for pair in range(PAIRS):
                start = pair * tile_width
                keys = kv_ref[pl.ds(base, key_rows), start : start + tile_width]
                values = kv_ref[pl.ds(base, key_rows), width + start : width + start + tile_width]
                scores = jnp.where(allowed, dot_nt(stacked[pair], keys), neg_fill)
                old_max = max_ref[pair]
                new_max = jnp.maximum(old_max, jnp.max(scores, axis=1, keepdims=True))
                probs = jnp.exp2((scores - new_max) * factor)
                rescale = jnp.exp2((old_max - new_max) * factor)
                sum_ref[pair] = sum_ref[pair] * rescale + jnp.sum(probs, axis=1, keepdims=True)
                acc_ref[pair] = acc_ref[pair] * rescale + dot_nn(probs.astype(bf16), values)
                max_ref[pair] = new_max

        run(step)
    outputs, logs = [], []
    for pair in range(PAIRS):
        outputs.append(merge_heads(acc_ref[pair] / sum_ref[pair]))
        column = max_ref[pair] * factor + jnp.log2(sum_ref[pair])
        logs.append(merge_heads(jnp.broadcast_to(column, acc_ref.shape[1:])))
    return jnp.concatenate(outputs, axis=1), jnp.concatenate(logs, axis=1)


def log_rows_of(lane_logs):
    return head_sums(lane_logs) * (HEADS / lane_logs.shape[1])


def query_grads(
    q_block, g_block, kv_ref, low_col, high_col, log_ref, delta_ref, run, key_rows, factor, acc_ref
):
    width = q_block.shape[1]
    tile_width = width // PAIRS
    q2, g2 = stacked_tiles(q_block), stacked_tiles(g_block)
    low2, high2 = twice(low_col), twice(high_col)

    def step(stored, index):
        base = pl.multiple_of(stored * key_rows, key_rows)
        key_pos = index * key_rows + lax.broadcasted_iota(jnp.int32, (1, key_rows), 1)
        allowed = (key_pos >= low2) & (key_pos <= high2)
        def read(pair, offset):
            start = offset + pair * tile_width
            return kv_ref[pl.ds(base, key_rows), start : start + tile_width]

        def products(pair):
            return dot_nt(q2[pair], read(pair, 0)), dot_nt(g2[pair], read(pair, width))

        ahead = products(0)
        repeats = key_rows // log_ref.shape[2]
        for pair in range(PAIRS):
            scores, prob_grad = ahead
            if pair + 1 < PAIRS:
                ahead = products(pair + 1)
            logs = jnp.concatenate([log_ref[pair]] * repeats, axis=1)
            deltas = jnp.concatenate([delta_ref[pair]] * repeats, axis=1)
            probs = jnp.where(allowed, jnp.exp2(scores * factor - logs), 0.0)
            score_grad = (probs * (prob_grad - deltas)).astype(bf16)
            acc_ref[pair] += dot_nn(score_grad, read(pair, 0))

    run(step)


def key_grads(k_block, v_block, q_ref, g_ref, stats_ref, low_col, high_col, run, factor, dk_ref, dv_ref):
    width = k_block.shape[1]
    tile_width = width // PAIRS
    rows = k_block.shape[0]
    query_rows = self_block
    blocks = query_rows // rows
    k2, v2 = stacked_tiles(k_block), stacked_tiles(v_block)
    low2, high2 = twice(low_col), twice(high_col)

    def step(stored, index):
        base = pl.multiple_of(stored * query_rows, query_rows)
        q_base = pl.multiple_of(index * query_rows, query_rows)
        query_pos = q_base + lax.broadcasted_iota(jnp.int32, (1, query_rows), 1)
        allowed = (query_pos >= low2) & (query_pos <= high2)
        stats = jnp.concatenate([stats_ref[stored * blocks + u] for u in range(blocks)], axis=1)

        def two_rows(first_row):
            return jnp.concatenate(
                [
                    jnp.broadcast_to(stats[first_row : first_row + 1], (rows, query_rows)),
                    jnp.broadcast_to(stats[first_row + 1 : first_row + 2], (rows, query_rows)),
                ],
                axis=0,
            )

        def read(ref, start, pair):
            return ref[pl.ds(start, query_rows), pair * tile_width : (pair + 1) * tile_width]

        def products(pair):
            return dot_nt(k2[pair], read(q_ref, q_base, pair)), dot_nt(v2[pair], read(g_ref, base, pair))

        ahead = products(0)
        for pair in range(PAIRS):
            scores, prob_grad = ahead
            if pair + 1 < PAIRS:
                ahead = products(pair + 1)
            probs = jnp.where(allowed, jnp.exp2(scores * factor - two_rows(2 * pair)), 0.0)
            score_grad = (probs * (prob_grad - two_rows(HEADS + 2 * pair))).astype(bf16)
            dk_ref[pair] += dot_nn(score_grad, read(q_ref, q_base, pair))
            dv_ref[pair] += dot_nn(probs.astype(bf16), read(g_ref, base, pair))

    run(step)


def merged_rows(acc_ref):
    return jnp.concatenate([merge_heads(acc_ref[pair]) for pair in range(PAIRS)], axis=1)


def chunk_views(piece_refs, planes):
    for s in range(planes):
        for bits in range(4):
            yield s, bits, piece_refs[(bits >> 1) + 2 * (bits & 1)].at[s]


def fill_rows(target, parts, info, skip=0, lead=0):
    own, fetched, other = parts
    rows = own.shape[-2]
    core = info.me & 1
    starts = (
        info.side * rows,
        (1 - info.side) * rows + core * (rows // 2),
        (1 - info.side) * rows + (1 - core) * (rows // 2),
    )
    for number, (part, start) in enumerate(zip((own, fetched, other), starts)):
        size = rows // 2 if number else rows
        at = pl.ds(pl.multiple_of(start, rows // 2), size)
        if len(target.shape) == 3:
            for k in range(target.shape[0]):
                first = skip + k * size
                window = part[first : first + size] if number else part[lead + k]
                target[k, at, :] = window.astype(bf16)
        elif target.shape[1] == part.shape[1]:
            target[at, :] = (part[skip : skip + size] if number else part[...]).astype(bf16)
        elif not number:
            target[at, :] = part[...].astype(bf16)
        else:
            width = part.shape[1]
            for k in range(target.shape[1] // width):
                first = skip + k * size
                target[at, k * width : (k + 1) * width] = part[first : first + size]


def attend_back(
    q_block, g_block, kv_ref, dkv_ref, low_row, high_row, log_rows, delta_rows,
    first, last, key_rows, factor, scale, dq_ref, adding,
):
    width = q_block.shape[1]
    tile_width = width // PAIRS
    rows = q_block.shape[0]
    q2 = [stack_heads(tile_of(q_block, pair, tile_width)) for pair in range(PAIRS)]
    g2 = [stack_heads(tile_of(g_block, pair, tile_width)) for pair in range(PAIRS)]
    low2 = jnp.concatenate([low_row, low_row], axis=1)
    high2 = jnp.concatenate([high_row, high_row], axis=1)
    dq_ref[...] = jnp.zeros(dq_ref.shape, f32)

    def step(index, carry):
        base = pl.multiple_of(index * key_rows, key_rows)
        key_pos = base + lax.broadcasted_iota(jnp.int32, (key_rows, 1), 0)
        allowed = (key_pos >= low2) & (key_pos <= high2)
        def tile_at(pair, offset):
            start = offset + pair * tile_width
            return pl.ds(base, key_rows), slice(start, start + tile_width)

        def products(pair):
            return (
                dot_nt(kv_ref[tile_at(pair, 0)], q2[pair]),
                dot_nt(kv_ref[tile_at(pair, width)], g2[pair]),
            )

        ahead = products(0)
        for pair in range(PAIRS):
            key_at, value_at = tile_at(pair, 0), tile_at(pair, width)
            scores, prob_grad = ahead
            if pair + 1 < PAIRS:
                ahead = products(pair + 1)
            probs = jnp.where(allowed, jnp.exp2(scores * factor - log_rows[pair]), 0.0)
            score_grad = (probs * (prob_grad - delta_rows[pair])).astype(bf16)
            key_grad = dot_nn(score_grad, q2[pair]) * scale
            value_grad = dot_nn(probs.astype(bf16), g2[pair])
            if adding:
                key_grad = key_grad + dkv_ref[key_at].astype(f32)
                value_grad = value_grad + dkv_ref[value_at].astype(f32)
            dkv_ref[key_at] = key_grad.astype(bf16)
            dkv_ref[value_at] = value_grad.astype(bf16)
            dq_ref[pair] += dot_tn(kv_ref[key_at], score_grad)
        return carry

    lax.fori_loop(first, last, step, 0)
    tiles = []
    for pair in range(PAIRS):
        both = dq_ref[pair]
        feature = lax.broadcasted_iota(jnp.int32, (tile_width, rows), 0)
        picked = jnp.where(feature < tile_width // 2, both[:, :rows], both[:, rows:])
        tiles.append(jnp.transpose(picked) * scale)
    return jnp.concatenate(tiles, axis=1)


def split_three(value):
    one = value.astype(bf16)
    rest = value - one.astype(f32)
    two = rest.astype(bf16)
    three = (rest - two.astype(f32)).astype(bf16)
    return [one, two, three]


def side_by_side(stats):
    rows = stats.shape[0] // 2
    return jnp.concatenate([stats[:rows], stats[rows:]], axis=1)


class PieceSink:
    def __init__(self, keep_ref, send_ref, scratch_ref, me, side):
        self.keep, self.send, self.scratch, self.me, self.side = keep_ref, send_ref, scratch_ref, me, side

    def emit(self, block, stride, offset):
        planes = self.keep.shape[2]
        piece = half_rows // (4 * planes)
        at = slice(block * piece, (block + 1) * piece)
        for s in range(planes):
            for bits in range(4):
                dc, dx = bits & 1, bits >> 1
                owner = self.me ^ (4 * s + bits)
                for fy in range(2):
                    source = (self.side ^ fy) * stride + offset + owner * piece
                    rows = self.scratch[pl.ds(pl.multiple_of(source, piece), piece), :]
                    target = self.send if dc else self.keep
                    target[fy, dx, s, at, :] = rows.astype(bf16)

    def put(self, block, matrix):
        rows = matrix.shape[0]
        self.scratch[0:rows, :] = matrix.astype(f32)
        blocks = rows // (2 * half_rows)
        for b in range(blocks):
            self.emit(block + b, rows // 2, b * half_rows)


class PlainSink:
    def __init__(self, plain_ref):
        self.plain = plain_ref

    def put(self, block, matrix):
        size = 2 * half_rows
        for b in range(matrix.shape[0] // size):
            self.plain[block + b] = matrix[b * size : (b + 1) * size].astype(bf16)


def pair_rows(by_head, block, rows, pair):
    at = slice(block * rows, (block + 1) * rows)
    return jnp.concatenate(
        [by_head[2 * pair : 2 * pair + 1, at], by_head[2 * pair + 1 : 2 * pair + 2, at]], axis=1
    )


def norm_stats(residual):
    centre = residual - jnp.mean(residual, axis=1, keepdims=True)
    spread = jnp.mean(centre * centre, axis=1, keepdims=True)
    inverse = lax.rsqrt(spread + eps_norm)
    return centre * inverse, inverse


def norm_back(normed, inverse, gain_row, upstream):
    scaled = upstream * gain_row
    mean_one = jnp.mean(scaled, axis=1, keepdims=True)
    mean_two = jnp.mean(scaled * normed, axis=1, keepdims=True)
    return (scaled - mean_one - normed * mean_two) * inverse


def column_sum(matrix):
    return jnp.sum(matrix.astype(f32), axis=0, keepdims=True)


def piece_rows(pieces):
    for bits in range(4):
        ref = pieces[(bits >> 1) + 2 * (bits & 1)]
        yield bits, ref[...].reshape(ref.shape[0] * ref.shape[1], ref.shape[2])


def project_chunks(pieces, planes, kv_ref, w_ref, shift, info):
    width = w_ref.shape[2]
    rows = pieces[0].shape[1]
    for bits, block in piece_rows(pieces):
        keys = dot_nn(block, w_ref[1]).astype(bf16)
        values = (dot_nn(block, w_ref[2]) + shift).astype(bf16)
        for s in range(planes):
            start = 4 * rows * s + rows * ((info.me & 3) ^ bits)
            at = pl.ds(pl.multiple_of(start, rows), rows)
            kv_ref[at, 0:width] = keys[s * rows : (s + 1) * rows]
            kv_ref[at, width:] = values[s * rows : (s + 1) * rows]


def first_forward_kernel(info_ref, x_ref, bias_ref, cols_ref, *refs, factor, planes, shards):
    maps, refs = refs[:shards], refs[shards:]
    pieces, refs = refs[:4], refs[4:]
    q_ref, kv_rows_ref, kv_ref, w_ref, top_ref, sums_ref, acc_ref = refs
    info = RowInfo(info_ref)
    width = x_ref.shape[1]
    half = info.half
    if shards == 1:
        w_ref[...] = maps[0][0:3]
    else:
        fill_rows(w_ref, maps, info)
    shift = bias_ref[1:2, :]
    project_chunks(pieces, planes, kv_ref, w_ref, shift, info)
    x_rows = x_ref[...]
    q_rows = (dot_nn(x_rows, w_ref[0]) + bias_ref[0:1, :]).astype(bf16)
    q_ref[...] = q_rows
    kv_rows_ref[:, 0:width] = dot_nn(x_rows, w_ref[1]).astype(bf16)
    kv_rows_ref[:, width:] = (dot_nn(x_rows, w_ref[2]) + shift).astype(bf16)
    for block in range(2):
        at = slice(block * half, (block + 1) * half)
        acc_ref[...] = jnp.zeros(acc_ref.shape, f32)
        run = over_planes(info, 0, planes, *info.self_keys(block))
        attend_plain(
            q_rows[at], kv_ref, cols_ref[at, 0:1], cols_ref[at, 1:2], run, self_block, factor, acc_ref
        )
        top_ref[at, :], sums_ref[at, :] = weighted_rows(acc_ref)


def second_forward_kernel(
    info_ref, kv_near_ref, q_in_ref, bias_ref, cols_ref, w_ref, top_ref, sums_ref, *refs,
    factor, planes,
):
    pieces, refs = refs[:4], refs[4:]
    a_ref, log_ref, kv_ref, acc_ref, max_ref, sum_ref, run_ref, lane_ref, near_ref, near_sem = refs
    info = RowInfo(info_ref)
    half = info.half
    project_chunks(pieces, planes, kv_ref, w_ref, bias_ref[1:2, :], info)
    fine = None
    for block in range(2):
        at = slice(block * half, (block + 1) * half)
        acc_ref[...] = jnp.zeros(acc_ref.shape, f32)
        run = over_planes(info, planes, planes, *info.self_keys(block))
        attend_plain(
            q_in_ref[at, :], kv_ref, cols_ref[at, 0:1], cols_ref[at, 1:2], run, self_block, factor,
            acc_ref,
        )
        top, sums = weighted_rows(acc_ref)
        sums = sums + sums_ref[at, :]
        a_ref[at, :] = (top + top_ref[at, :]) / sums
        lane_ref[at, :] = jnp.log2(sums)
        fine = in_range(sums) if fine is None else fine & in_range(sums)

    @pl.when(jnp.logical_not(fine))
    def _():
        copy = pltpu.make_async_copy(kv_near_ref, near_ref, near_sem)
        copy.start()
        copy.wait()
        for block in range(2):
            at = slice(block * half, (block + 1) * half)
            keys = info.self_keys(block)
            a_ref[at, :], lane_ref[at, :] = attend_running(
                q_in_ref[at, :],
                [
                    (near_ref, over_planes(info, 0, planes, *keys)),
                    (kv_ref, over_planes(info, planes, planes, *keys)),
                ],
                cols_ref[at, 0:1], cols_ref[at, 1:2], self_block, factor, (max_ref, sum_ref, run_ref),
            )

    log_ref[...] = log_rows_of(lane_ref[...])


def project_kernel(info_ref, w_ref, bias_ref, *refs, planes):
    pieces, (q_ref,) = refs[:8], refs[8:]
    info = RowInfo(info_ref)
    for part in range(2):
        for bits, block in piece_rows(pieces[4 * part : 4 * part + 4]):
            queries = (dot_nn(block, w_ref[0]) + bias_ref[0:1, :]).astype(bf16)
            rows = pieces[0].shape[1]
            for s in range(planes):
                place = info.me ^ (4 * (part * planes + s) + bits)
                at = pl.ds(pl.multiple_of(place * rows, rows), rows)
                q_ref[at, :] = queries[s * rows : (s + 1) * rows]


def middle_forward_kernel(
    info_ref, x_ref, a_ref, g_ref, cols_ref, gain_ref, bias_ref, ffn_bias_ref, mem_ref, *refs,
    factor, shards, cross_rows,
):
    late, refs = (refs[:3], refs[3:]) if shards == 1 else (refs[:5], refs[5:])
    (
        out_ref, a_low_ref, h1_ref, h2_ref, f_ref, e3_ref, gu_ref, e2_ref, ac_ref, gr2_ref, r1_ref,
        qc_ref, cross_ref, cross_log_ref, kvc_ref, sums_ref, csum_ref, wc_ref,
        acc_ref, max_ref, sum_ref, run_ref, lane_ref, *whole_refs,
    ) = refs
    info = RowInfo(info_ref)
    if shards == 1:
        maps_ref, u_ref, v_ref = late
        wc_ref[...] = maps_ref[3:8]
    else:
        maps_ref, up_ref, down_ref, one, two = late
        u_ref, v_ref = whole_refs
        size = maps_ref.shape[1] // 2
        fill_rows(wc_ref, (maps_ref, one, two), info, 0, 3)
        fill_rows(v_ref, (down_ref, one, two), info, 5 * size)
        fill_rows(u_ref, (up_ref, one, two), info, 5 * size + down_ref.shape[0] // 2)
    rows, width = x_ref.shape
    half = rows // 2
    cross_block = cross_rows
    cross_range = [info.cross_keys(block, cross_block) for block in range(2)]
    live_first = jnp.minimum(cross_range[0][0], cross_range[1][0])
    live_last = jnp.maximum(cross_range[0][1], cross_range[1][1])

    def project(index, carry):
        at = pl.ds(pl.multiple_of(index * cross_block, cross_block), cross_block)
        block = mem_ref[at, :]
        kvc_ref[at, 0:width] = dot_nn(block, wc_ref[1]).astype(bf16)
        kvc_ref[at, width:] = (dot_nn(block, wc_ref[2]) + bias_ref[5:6, :]).astype(bf16)
        return carry

    lax.fori_loop(live_first, live_last, project, 0)
    attn_self = a_ref[...]
    a_low = attn_self.astype(bf16)
    a_low_ref[...] = a_low
    r1 = x_ref[...].astype(f32) + (dot_nn(a_low, wc_ref[3]) + bias_ref[2:3, :])
    r1_ref[...] = r1
    n1, inv1 = norm_stats(r1)
    h1 = n1 * gain_ref[0:1, :] + bias_ref[3:4, :]
    h1_low = h1.astype(bf16)
    h1_ref[...] = h1_low
    qc = (dot_nn(h1_low, wc_ref[0]) + bias_ref[4:5, :]).astype(bf16)
    qc_ref[...] = qc
    fine = None
    for block in range(2):
        at = slice(block * half, (block + 1) * half)
        acc_ref[...] = jnp.zeros(acc_ref.shape, f32)
        attend_plain(
            qc[at], kvc_ref, cols_ref[at, 2:3], cols_ref[at, 3:4], over_range(*cross_range[block]),
            cross_block, factor, acc_ref,
        )
        top, weights = weighted_rows(acc_ref)
        cross_ref[at, :] = top / weights
        lane_ref[at, :] = jnp.log2(weights)
        fine = in_range(weights) if fine is None else fine & in_range(weights)

    @pl.when(jnp.logical_not(fine))
    def _():
        for block in range(2):
            at = slice(block * half, (block + 1) * half)
            cross_ref[at, :], lane_ref[at, :] = attend_running(
                qc_ref[at, :], [(kvc_ref, over_range(*cross_range[block]))],
                cols_ref[at, 2:3], cols_ref[at, 3:4], cross_block, factor, (max_ref, sum_ref, run_ref),
            )

    cross_log_ref[...] = log_rows_of(lane_ref[...])
    attn_cross = cross_ref[...]
    ac_low = attn_cross.astype(bf16)
    ac_ref[...] = ac_low
    r2 = h1 + (dot_nn(ac_low, wc_ref[4]) + bias_ref[6:7, :])
    n2, inv2 = norm_stats(r2)
    h2 = n2 * gain_ref[1:2, :] + bias_ref[7:8, :]
    h2_low = h2.astype(bf16)
    h2_ref[...] = h2_low
    u = dot_nn(h2_low, u_ref[...]) + ffn_bias_ref[...]
    sig = 1.0 / (1.0 + jnp.exp(-u))
    act = (u * sig).astype(bf16)
    f_ref[...] = act
    slope = sig * (1.0 + u * (1.0 - sig))
    r3 = h2 + (dot_nn(act, v_ref[...]) + bias_ref[8:9, :])
    n3, inv3 = norm_stats(r3)
    out_ref[...] = n3 * gain_ref[2:3, :] + bias_ref[9:10, :]
    sums_ref[...] = jnp.zeros_like(sums_ref)
    upstream = g_ref[...].astype(f32)
    sums_ref[2:3, :] = column_sum(upstream * n3)
    sums_ref[12:13, :] = column_sum(upstream)
    gr3 = norm_back(n3, inv3, gain_ref[2:3, :], upstream)
    e3 = gr3.astype(bf16)
    e3_ref[...] = e3
    sums_ref[11:12, :] = column_sum(e3)
    gu = (dot_nt(e3, v_ref[...]) * slope).astype(bf16)
    gu_ref[...] = gu
    csum_ref[...] = column_sum(gu)
    gh2 = gr3 + dot_nt(gu, u_ref[...])
    sums_ref[1:2, :] = column_sum(gh2 * n2)
    sums_ref[10:11, :] = column_sum(gh2)
    gr2 = norm_back(n2, inv2, gain_ref[1:2, :], gh2)
    gr2_ref[...] = gr2
    e2 = gr2.astype(bf16)
    e2_ref[...] = e2
    sums_ref[9:10, :] = column_sum(e2)


def middle_backward_kernel(
    info_ref, a_ref, log_ref, rows_ref, gain_ref, wc_ref, e2_ref, gr2_ref, r1_ref, qc_ref,
    cross_ref, cross_log_ref, kvc_ref, sums_in_ref,
    e1_ref, dqc_ref, ga_ref, gr1_ref, delta_ref, dkvc_ref, sums_ref, dq_ref,
    *, factor, scale, cross_rows,
):
    info = RowInfo(info_ref)
    rows, width = a_ref.shape
    half = rows // 2
    cross_block = cross_rows
    cross_range = [info.cross_keys(block, cross_block) for block in range(2)]
    live_first = jnp.minimum(cross_range[0][0], cross_range[1][0])
    live_last = jnp.maximum(cross_range[0][1], cross_range[1][1])
    sums_ref[...] = sums_in_ref[...]
    n1, inv1 = norm_stats(r1_ref[...])
    attn_self, attn_cross = a_ref[...], cross_ref[...]
    gr2, e2, qc, cross_logs = gr2_ref[...], e2_ref[...], qc_ref[...], cross_log_ref[...]

    def clear(index, carry):
        at = pl.ds(pl.multiple_of(index * cross_block, cross_block), cross_block)
        dkvc_ref[at, :] = jnp.zeros((cross_block, 2 * width), bf16)
        return carry

    lax.fori_loop(live_first, live_last, clear, 0)
    gac = dot_nt(e2, wc_ref[4]).astype(bf16)
    sums_ref[8:9, :] = column_sum(gac)
    delta_cross = head_sums(gac.astype(f32) * attn_cross)
    grads = []
    for block in (1, 0):
        at = slice(block * half, (block + 1) * half)
        grads.append(
            attend_back(
                qc[at], gac[at], kvc_ref, dkvc_ref, rows_ref[2:3, at], rows_ref[3:4, at],
                [pair_rows(cross_logs, block, half, p) for p in range(PAIRS)],
                [pair_rows(delta_cross, block, half, p) for p in range(PAIRS)],
                *cross_range[block], cross_block, factor, scale,
                dq_ref, True,
            )
        )
    dqc = jnp.concatenate([grads[1], grads[0]], axis=0).astype(bf16)
    dqc_ref[...] = dqc
    sums_ref[7:8, :] = column_sum(dqc)
    gh1 = gr2 + dot_nt(dqc, wc_ref[0])
    sums_ref[0:1, :] = column_sum(gh1 * n1)
    sums_ref[6:7, :] = column_sum(gh1)
    gr1 = norm_back(n1, inv1, gain_ref[0:1, :], gh1)
    gr1_ref[...] = gr1
    e1 = gr1.astype(bf16)
    e1_ref[...] = e1
    sums_ref[5:6, :] = column_sum(e1)
    ga = dot_nt(e1, wc_ref[3]).astype(bf16)
    ga_ref[0:rows, :] = ga
    sums_ref[4:5, :] = column_sum(ga)
    delta = head_sums(ga.astype(f32) * attn_self)
    delta_ref[...] = delta
    extra = split_three(side_by_side(log_ref[...])) + split_three(side_by_side(delta))
    extra.append(jnp.zeros((2 * HEADS // 2, width), bf16))
    ga_ref[rows:, :] = jnp.concatenate([e.astype(f32) for e in extra], axis=0).astype(bf16)


def memory_grads_kernel(
    info_ref, mem_ref, wc_ref, dkvc_ref, pm_ref, dwc_ref, dw_acc_ref, *, cross_block
):
    info = RowInfo(info_ref)
    width = mem_ref.shape[1]
    cross_range = [info.cross_keys(block, cross_block) for block in range(2)]
    live_first = jnp.minimum(cross_range[0][0], cross_range[1][0])
    live_last = jnp.maximum(cross_range[0][1], cross_range[1][1])
    pm_ref[...] = jnp.zeros(pm_ref.shape, bf16)
    dw_acc_ref[...] = jnp.zeros(dw_acc_ref.shape, f32)

    def memory_step(index, carry):
        at = pl.ds(pl.multiple_of(index * cross_block, cross_block), cross_block)
        grads_block = dkvc_ref[at, :]
        block = dot_nt(grads_block[:, :width], wc_ref[1]) + dot_nt(grads_block[:, width:], wc_ref[2])
        pm_ref[at, :] = block.astype(bf16)
        dw_acc_ref[...] += dot_tn(mem_ref[at, :], grads_block)
        return carry

    lax.fori_loop(live_first, live_last, memory_step, 0)
    dwc_ref[...] = dw_acc_ref[...].astype(bf16)


def query_backward_kernel(
    info_ref, q_ref, ga_ref, kv_near_ref, kv_far_ref, log_ref, delta_ref, cols_ref, dq_ref, acc_ref,
    log_rep_ref, delta_rep_ref, *, factor, scale, planes,
):
    info = RowInfo(info_ref)
    rows = q_ref.shape[0]
    half = info.half
    pad = jnp.zeros((128 - 2 * HEADS, rows), f32)
    stat_cols = jnp.transpose(jnp.concatenate([log_ref[...], delta_ref[...], pad], axis=0))

    def stat_column(at, head):
        return jnp.concatenate(
            [stat_cols[at, head : head + 1], stat_cols[at, head + 1 : head + 2]], axis=0
        )

    for block in range(2):
        at = slice(block * half, (block + 1) * half)
        acc_ref[...] = jnp.zeros(acc_ref.shape, f32)
        for p in range(PAIRS):
            log_rep_ref[p] = jnp.broadcast_to(stat_column(at, 2 * p), log_rep_ref.shape[1:])
            delta_rep_ref[p] = jnp.broadcast_to(stat_column(at, HEADS + 2 * p), log_rep_ref.shape[1:])
        for part, kv_ref in enumerate((kv_near_ref, kv_far_ref)):
            query_grads(
                q_ref[at, :], ga_ref[at, :], kv_ref, cols_ref[at, 0:1], cols_ref[at, 1:2],
                log_rep_ref, delta_rep_ref,
                over_planes(info, part * planes, planes, *info.self_keys(block)),
                self_block, factor, acc_ref,
            )
        dq_ref[at, :] = (merged_rows(acc_ref) * scale).astype(bf16)


def key_backward_kernel(
    info_ref, kv_rows_ref, q_all_ref, cols_ref, *refs, factor, scale, planes, part, last,
    total_planes,
):
    state_in, refs = (refs[:2], refs[2:]) if part else ((), refs)
    pieces, refs = refs[:4], refs[4:]
    if last:
        dk_out_ref, dv_out_ref, g_ref, stats_ref, dk_ref, dv_ref = refs
    else:
        dk_ref, dv_ref, g_ref, stats_ref = refs
    info = RowInfo(info_ref)
    half = info.half
    rows = 2 * half
    width = q_all_ref.shape[1]
    for s, bits, chunk in chunk_views(pieces, planes):
        place = (info.me & 3) ^ bits
        extra = chunk[rows : rows + chunk_rows, :].astype(f32)
        logs = extra[0:4] + extra[4:8] + extra[8:12]
        deltas = extra[12:16] + extra[16:20] + extra[20:24]
        for side in range(2):
            block = 8 * s + 4 * side + (place if side == 0 else 3 - place)
            lanes = slice(side * half, (side + 1) * half)
            high = slice(rows + side * half, rows + (side + 1) * half)
            g_ref[pl.ds(pl.multiple_of(block * half, half), half), :] = chunk[lanes, :]
            stats_ref[block] = jnp.concatenate(
                [logs[:, lanes], logs[:, high], deltas[:, lanes], deltas[:, high]], axis=0
            )

    def groups(first, stop):
        def run(step):
            def visit(stored, carry):
                plane = info.plane ^ (part * planes + (stored >> 1))
                index = jnp.where((stored & 1) == 0, plane, 2 * total_planes - 1 - plane)

                @pl.when((index >= first) & (index < stop))
                def _():
                    step(stored, index)

                return carry

            lax.fori_loop(0, 2 * planes, visit, 0)

        return run

    for block in range(2):
        at = slice(block * half, (block + 1) * half)
        if part:
            dk_ref[block] = state_in[0][block]
            dv_ref[block] = state_in[1][block]
        else:
            dk_ref[block] = jnp.zeros(dk_ref.shape[1:], f32)
            dv_ref[block] = jnp.zeros(dv_ref.shape[1:], f32)
        key_grads(
            kv_rows_ref[at, 0:width], kv_rows_ref[at, width:], q_all_ref, g_ref, stats_ref,
            cols_ref[at, 1:2], cols_ref[at, 4:5], groups(*info.queries(block)), factor,
            dk_ref.at[block], dv_ref.at[block],
        )
    if not last:
        return
    dk = jnp.concatenate([merged_rows(dk_ref.at[b]) for b in range(2)], axis=0) * scale
    dv = jnp.concatenate([merged_rows(dv_ref.at[b]) for b in range(2)], axis=0)
    dk_out_ref[...] = dk.astype(bf16)
    dv_out_ref[...] = dv.astype(bf16)


def self_grads_kernel(
    info_ref, x_ref, gr1_ref, dq_ref, dk_ref, dv_ref, w_ref, tok_ref, *refs, plain
):
    sink_refs, (dw_ref,) = (refs[:1], refs[1:]) if plain else (refs[:2], refs[2:])
    info = RowInfo(info_ref)
    dk, dv = dk_ref[...], dv_ref[...]
    tok = gr1_ref[...] + dot_nt(dq_ref[...], w_ref[0]) + dot_nt(dk, w_ref[1]) + dot_nt(dv, w_ref[2])
    tok_ref[...] = tok.astype(bf16)
    sink = PlainSink(*sink_refs) if plain else PieceSink(*sink_refs, dw_ref, info.me, info.side)
    x_rows = x_ref[...]
    sink.put(0, dot_tn(x_rows, dk))
    sink.put(1, dot_tn(x_rows, dv))


def feed_grads_kernel(info_ref, h2_ref, gu_ref, f_ref, e3_ref, *refs, plain):
    sink_refs, (dw_ref,) = (refs[:1], refs[1:]) if plain else (refs[:2], refs[2:])
    info = RowInfo(info_ref)
    sink = PlainSink(*sink_refs) if plain else PieceSink(*sink_refs, dw_ref, info.me, info.side)
    width = h2_ref.shape[1]
    parts = gu_ref.shape[1] // width
    for k in range(parts):
        sink.put(k, dot_tn(h2_ref[...], gu_ref[:, k * width : (k + 1) * width]))
    sink.put(parts, dot_tn(f_ref[...], e3_ref[...]))


def map_grads_kernel(
    info_ref, a_ref, e1_ref, ac_ref, e2_ref, h1_ref, dqc_ref, dwc_ref, x_ref, dq_ref, sums_ref,
    csum_ref, *refs, plain,
):
    sink_refs, (dw_ref,) = (refs[:1], refs[1:]) if plain else (refs[:2], refs[2:])
    info = RowInfo(info_ref)
    sink = PlainSink(*sink_refs) if plain else PieceSink(*sink_refs, dw_ref, info.me, info.side)
    width = a_ref.shape[1]
    sink.put(0, dot_tn(a_ref[...], e1_ref[...]))
    sink.put(1, dot_tn(ac_ref[...], e2_ref[...]))
    sink.put(2, dot_tn(h1_ref[...], dqc_ref[...]))
    sink.put(3, dwc_ref[:, :width])
    sink.put(4, dwc_ref[:, width:])
    sink.put(5, dot_tn(x_ref[...], dq_ref[...]))
    put_small(sink, 6, dw_ref, sums_ref[...], csum_ref, dq_ref[...])


def grads_project_kernel(info_ref, w_ref, bias_ref, *refs, planes, plain):
    pieces, refs = refs[:8], refs[8:]
    inputs, refs = refs[:11], refs[11:]
    q_ref, outs = refs[0], refs[1:]
    map_grads_kernel(info_ref, *inputs, *outs, plain=plain)
    project_kernel(info_ref, w_ref, bias_ref, *pieces, q_ref, planes=planes)


def put_small(sink, block, dw_ref, sums, csum_ref, dq):
    dw_ref[...] = jnp.zeros(dw_ref.shape, f32)
    row = lax.broadcasted_iota(jnp.int32, sums.shape, 0)
    sums = jnp.where(row == 3, column_sum(dq), sums)
    lanes = csum_ref.shape[1] // 8
    for yh in range(2):
        base = yh * half_rows
        dw_ref[base : base + 16, 0:lanes] = sums[:, yh * lanes : (yh + 1) * lanes]
        for k in range(4):
            start = yh * 4 * lanes + k * lanes
            dw_ref[base + 16 + k : base + 17 + k, 0:lanes] = csum_ref[:, start : start + lanes]
    if isinstance(sink, PlainSink):
        sink.plain[block] = dw_ref[...].astype(bf16)
    else:
        sink.emit(block, half_rows, 0)


def place_kernel(info_ref, *refs, places):
    sources, outs = refs[:4], refs[4:]
    info = RowInfo(info_ref)
    planes = sources[0].shape[0]
    piece = half_rows // (4 * planes)
    for s in range(planes):
        for bits in range(4):
            owner = info.me ^ (4 * s + bits)
            source = sources[(bits >> 1) + 2 * (bits & 1)]
            for block, (number, kind, k) in enumerate(places):
                rows = source[s, block * piece : (block + 1) * piece, :].astype(f32)
                width = rows.shape[1]
                base = k * half_rows if kind == "rows" else 0
                at = pl.ds(pl.multiple_of(base + owner * piece, piece), piece)
                if kind == "lead":
                    outs[number][k, at, :] = rows
                elif kind == "cols":
                    outs[number][at, k * width : (k + 1) * width] = rows
                else:
                    outs[number][at, :] = rows


def place_maps_kernel(
    info_ref, own_ref, other_ref, own_core_ref, other_core_ref, ins_ref, outs_ref, gain_ref, bias_ref,
    shift_ref, rest_ref,
):
    place_kernel(
        info_ref, own_ref, other_ref, own_core_ref, other_core_ref, ins_ref, outs_ref, rest_ref,
        places=[(1, "lead", 0), (1, "lead", 1)]
        + [(0, "lead", k) for k in (3, 4, 5, 0)]
        + [(2, "rows", 0), (0, "lead", 1), (0, "lead", 2)],
    )
    lanes = gain_ref.shape[1]
    gain_ref[...] = rest_ref[0:3, 0:lanes]
    bias_ref[...] = rest_ref[3:13, 0:lanes]
    for k in range(4):
        shift_ref[:, k * lanes : (k + 1) * lanes] = rest_ref[16 + k : 17 + k, 0:lanes]


def call_kernel(kernel, inputs, outputs, scratch, name, micros, in_place=()):
    vmem = pl.BlockSpec(memory_space=pltpu.VMEM)
    smem = pl.BlockSpec(memory_space=pltpu.SMEM)
    return pl.pallas_call(
        kernel,
        in_specs=[smem]
        + [
            pl.BlockSpec(memory_space=pl.ANY) if index in in_place else vmem
            for index in range(1, len(inputs))
        ],
        out_specs=[vmem] * len(outputs),
        out_shape=[jax.ShapeDtypeStruct(*entry) for entry in outputs],
        scratch_shapes=[pltpu.VMEM(*entry) if isinstance(entry, tuple) else entry for entry in scratch],
        compiler_params=pltpu.CompilerParams(vmem_limit_bytes=vmem_bytes),
        cost_estimate=pl.CostEstimate(
            flops=int(micros * 1e9), transcendentals=0, bytes_accessed=int(micros * 1e4)
        ),
        name=name,
    )(*inputs)


def exchange(value, bits):
    count = lax.axis_size("ctx")
    return lax.ppermute(value, "ctx", [(i, i ^ bits) for i in range(count)])


def swap_side(value):
    return lax.ppermute(value, "fsdp", [(0, 1), (1, 0)])


def after(value, *others):
    return lax.optimization_barrier((value,) + others)[0]


def fetch_planes(value, first, last):
    return [exchange(value, 4 * s) if s else value for s in range(first, last)]


def fetch_chips(chunks):
    return [chunks, exchange(chunks, 2)]


def fetch_cores(pair):
    return pair + [exchange(chunks, 1) for chunks in pair]


def core_part(shard, axis):
    rows = shard.shape[axis] // 2
    return lax.dynamic_slice_in_dim(shard, (lax.axis_index("ctx") % 2) * rows, rows, axis)


def add_cores(keep, send):
    other = exchange(send, 1)
    return keep[0].astype(f32) + other[0].astype(f32), (
        keep[1].astype(f32) + other[1].astype(f32)
    ).astype(bf16)


def add_sides(kept, sent):
    return kept + swap_side(sent).astype(f32)


def add_chips(part, low):
    return part[0] + exchange(low, 2).astype(f32)


def low_planes(part):
    return [part[s].astype(bf16) for s in range(1, part.shape[0])]


def add_planes(part, low):
    total = part[0]
    for s, sent in enumerate(low):
        total = total + exchange(sent, 4 * (s + 1)).astype(f32)
    return total


def spread_planes(low):
    planes = lax.axis_size("ctx") // 4
    return [low] + [exchange(low, 4 * s) for s in range(1, planes)]


def spread_chips(chunks, before=None):
    own = jnp.stack(chunks)
    other = exchange(own, 2)
    sent = [own, other] if before is None else [after(own, before), after(other, before)]
    return [own, other] + [exchange(chunk, 1) for chunk in sent]


def zigzag_perms(count):
    def worker(block):
        return block if block < count else 2 * count - 1 - block

    first = [(owner, worker(2 * owner)) for owner in range(count)]
    second = [(owner, worker(2 * owner + 1)) for owner in range(count)]
    return first, second


def body(
    tokens, memory, token_seg, memory_seg, out_grad,
    in_proj, out_proj, ffn_in, ffn_out, norm_gain, bias_rows, ffn_bias,
):
    count = lax.axis_size("ctx")
    sides = lax.axis_size("fsdp")
    planes = count // 4
    plain = sides != 2
    me = lax.axis_index("ctx")
    side = lax.axis_index("fsdp")
    row_count, width = tokens.shape[1], tokens.shape[2]
    mem_count = memory.shape[1]
    half = row_count // 2
    scale = 1.0 / math.sqrt(width // HEADS)
    factor = scale * math.log2(math.e)
    total = row_count * count
    mem_total = mem_count * count
    near, far = planes // 2, planes - planes // 2

    x_planes = fetch_planes(tokens[0], 0, planes)
    small = jnp.concatenate(
        [norm_gain, bias_rows, ffn_bias.reshape(-1, norm_gain.shape[1])], axis=0
    ).astype(bf16)
    maps_low = jnp.concatenate([in_proj, out_proj], axis=0).astype(bf16)
    up_low, down_low = ffn_in.astype(bf16), ffn_out.astype(bf16)
    if plain:
        small = lax.all_gather(small, "fsdp").astype(f32)
        whole = lax.all_gather(maps_low, "fsdp", axis=1, tiled=True)
        self_maps = (whole,)
        late_maps = (
            whole, lax.all_gather(up_low, "fsdp", axis=0, tiled=True),
            lax.all_gather(down_low, "fsdp", axis=0, tiled=True),
        )
    else:
        small_rows = small.shape[0]
        pad = jnp.zeros((32 - small_rows, small.shape[1]), bf16)
        sent = jnp.concatenate(
            [
                core_part(in_proj[0:3], 1).astype(bf16).reshape(-1, width),
                jnp.concatenate([small, pad], axis=0).reshape(-1, width),
            ],
            axis=0,
        )
        fetched = swap_side(sent)
    x_near = fetch_chips(jnp.stack(x_planes[:near]))
    if not plain:
        ready = after(fetched, x_near[1])
        table_rows = ready[-pad.shape[1] * 32 // width :].reshape(32, -1)[:small_rows]
        small = jnp.stack([small, table_rows])
        small = jnp.where(side == 0, small, small[::-1]).astype(f32)
        self_maps = (maps_low, ready, exchange(ready, 1))
        up_part = core_part(after(ffn_in, sent), 0).astype(bf16)
        late_parts = [
            core_part(in_proj[3:6], 1).astype(bf16).reshape(-1, width),
            core_part(after(out_proj, sent), 1).astype(bf16).reshape(-1, width),
            core_part(after(ffn_out, sent), 0).astype(bf16),
        ]
        late_parts += [
            up_part[:, k * width : (k + 1) * width] for k in range(up_part.shape[1] // width)
        ]
        late_sent = jnp.concatenate(late_parts, axis=0)
        late = swap_side(after(late_sent, fetched))
    started = x_near[0] if plain else fetched
    x_far = fetch_chips(jnp.stack([after(chunk, started) for chunk in x_planes[near:]]))

    perm_first, perm_second = zigzag_perms(count)
    even = me % 2 == 0
    first_sent = small if plain else sent
    rows_in = jnp.stack([after(tokens[0], first_sent, x_near[0]), out_grad[0]])
    one = lax.ppermute(rows_in[:, :half], "ctx", perm_first)
    two = lax.ppermute(rows_in[:, half:], "ctx", perm_second)
    rows_in = jnp.where(
        even, jnp.concatenate([one, two], axis=1), jnp.concatenate([two, one], axis=1)
    )
    x_rows, g_rows = rows_in[0], rows_in[1]

    table = small[:, 0:13].transpose(1, 0, 2).reshape(13, width)
    gains, biases = table[0:3], table[3:13]
    ffn_shift = small[:, 13:].reshape(1, -1)

    m_all = lax.all_gather(memory[0], "ctx", axis=0, tiled=True)

    segs, mem_segs = after(token_seg[0], first_sent), after(memory_seg[0], first_sent)
    step = jnp.arange(half, dtype=jnp.int32)
    row_pos = jnp.concatenate([me * half + step, (2 * count - 1 - me) * half + step])
    row_seg = jnp.concatenate(
        [
            lax.dynamic_slice_in_dim(segs, me * half, half),
            lax.dynamic_slice_in_dim(segs, (2 * count - 1 - me) * half, half),
        ]
    )

    def below(keys, closed):
        hits = keys[None, :] <= row_seg[:, None] if closed else keys[None, :] < row_seg[:, None]
        return jnp.sum(hits, axis=1, dtype=jnp.int32)

    ones = jnp.ones_like(row_pos)
    info = jnp.stack(
        [
            below(segs, False), row_pos, below(mem_segs, False), below(mem_segs, True) - 1,
            below(segs, True) - 1, me * ones, side * ones, ones,
        ]
    )
    cols = info.T

    tile = width // PAIRS
    column = ((PAIRS, row_count, 1), f32)
    square = ((PAIRS, row_count, tile), f32)
    two_squares = ((2, PAIRS, row_count, tile), f32)
    rows_low = ((row_count, width), bf16)
    rows_full = ((row_count, width), f32)
    kv_rows_shape = ((row_count, 2 * width), bf16)

    x_near = fetch_cores(x_near)
    x_near[0] = after(x_near[0], x_far[0], up_low, down_low)
    wide = ((PAIRS, row_count, 2 * tile), f32)
    q_rows, kv_rows, kv_near, w_self, top, weights = call_kernel(
        lambda *refs: first_forward_kernel(
            *refs, factor=factor, planes=near, shards=len(self_maps)
        ),
        (info, x_rows, biases, cols, *self_maps, *x_near),
        (
            rows_low, kv_rows_shape, ((4 * near * row_count, 2 * width), bf16),
            ((3, width, width), bf16), rows_full, rows_full,
        ),
        [wide],
        "first_forward",
        10,
    )
    x_far = fetch_cores([after(chunks, top) for chunks in x_far])
    a_rows, log_rows, kv_far = call_kernel(
        lambda *refs: second_forward_kernel(*refs, factor=factor, planes=far),
        (info, kv_near, q_rows, biases, cols, w_self, top, weights, *x_far),
        (rows_full, ((HEADS, row_count), f32), ((4 * far * row_count, 2 * width), bf16)),
        [
            wide, column, column, square, rows_full, ((4 * near * row_count, 2 * width), bf16),
            pltpu.SemaphoreType.DMA,
        ],
        "second_forward",
        10,
        (1,),
    )
    if not plain:
        late = after(late, a_rows)
        late_maps = (maps_low, up_low, down_low, late, exchange(late, 1))
    ff_width = ffn_in.shape[1]
    ff_rows = ((row_count, ff_width), bf16)
    by_head = ((HEADS, row_count), f32)
    kvc_shape = ((mem_total, 2 * width), bf16)
    sums_shape = ((16, width), f32)
    whole_maps = [] if plain else [((width, ff_width), bf16), ((ff_width, width), bf16)]
    (
        out_rows, a_low, h1_low, h2_low, act, e3, gu, e2, ac_low, gr2, r1, qc, cross, cross_log,
        kvc, sums, csum, w_cross,
    ) = call_kernel(
        lambda *refs: middle_forward_kernel(
            *refs, factor=factor, shards=len(self_maps), cross_rows=2 * mem_count
        ),
        (info, x_rows, a_rows, g_rows, cols, gains, biases, ffn_shift, m_all, *late_maps),
        (
            rows_full, rows_low, rows_low, rows_low, ff_rows, rows_low, ff_rows, rows_low, rows_low,
            rows_full, rows_full, rows_low, rows_full, by_head, kvc_shape, sums_shape,
            ((1, ff_width), f32), ((5, width, width), bf16),
        ),
        [wide, column, column, square, rows_full, *whole_maps],
        "middle_forward",
        25,
    )

    def sink_shapes(blocks):
        if plain:
            return [((blocks, width, width), bf16)]
        return [((2, 2, planes, blocks * (half_rows // count), width), bf16)] * 2

    feed = call_kernel(
        lambda *refs: feed_grads_kernel(*refs, plain=plain),
        (info, h2_low, gu, act, e3),
        sink_shapes(8),
        [((ff_width, width), f32)],
        "feed_grads",
        5,
    )
    gr2 = after(gr2, *feed)
    e1, dqc, ga, gr1, delta, dkvc, sums = call_kernel(
        lambda *refs: middle_backward_kernel(
            *refs, factor=factor, scale=scale, cross_rows=2 * mem_count
        ),
        (
            info, a_rows, log_rows, info, gains, w_cross, e2, gr2, r1, qc, cross, cross_log, kvc,
            sums,
        ),
        (
            rows_low, rows_low, ((row_count + chunk_rows, width), bf16), rows_full, by_head,
            kvc_shape, sums_shape,
        ),
        [((PAIRS, tile, row_count), f32)],
        "middle_backward",
        14,
    )
    g_planes = fetch_planes(ga, 0, near)
    if not plain:
        feed = add_cores(*feed)
        dkvc = after(dkvc, feed[1])
    mem_part, dwc = call_kernel(
        lambda *refs: memory_grads_kernel(*refs, cross_block=2 * mem_count),
        (info, m_all, w_cross, dkvc),
        (((mem_total, width), bf16), ((width, 2 * width), bf16)),
        [((width, 2 * width), f32)],
        "memory_grads",
        5,
    )
    g_near = fetch_chips(jnp.stack([after(chunk, mem_part) for chunk in g_planes]))
    g_planes = fetch_planes(after(ga, mem_part), near, planes)
    (dq,) = call_kernel(
        lambda *refs: query_backward_kernel(*refs, factor=factor, scale=scale, planes=near),
        (info, after(q_rows, g_near[0]), ga, kv_near, kv_far, log_rows, delta, cols),
        (rows_low,),
        [square, square, square],
        "query_backward",
        20,
    )
    g_far = fetch_chips(jnp.stack([after(chunk, dq) for chunk in g_planes]))
    g_near = fetch_cores([after(chunks, dq) for chunks in g_near])
    if not plain:
        feed = add_sides(*feed)
        feed_low = feed[1].astype(bf16)
        h1_low = after(h1_low, feed_low)
    q_all, *maps = call_kernel(
        lambda *refs: grads_project_kernel(*refs, planes=near, plain=plain),
        (
            info, w_self, biases, *x_near, *x_far, a_low, e1, ac_low, e2,
            after(h1_low, g_far[0], g_near[1]), dqc, dwc, x_rows, dq, sums, csum,
        ),
        [((total, width), bf16)] + sink_shapes(7),
        [((width, width), f32)],
        "grads_project",
        12,
    )
    if not plain:
        maps = add_cores(*maps)
        feed_low = after(feed_low, q_all)
        kv_rows = after(kv_rows, maps[1], feed_low)
    mem_part = after(mem_part, g_far[1])
    memory_grad = lax.psum_scatter(mem_part, "ctx", scatter_dimension=0, tiled=True).astype(f32)
    g_far = fetch_cores([after(chunks, q_all) for chunks in g_far])
    dk_part, dv_part = call_kernel(
        lambda *refs: key_backward_kernel(
            *refs, factor=factor, scale=scale, planes=near, part=0, last=False,
            total_planes=planes,
        ),
        (info, kv_rows, q_all, cols, *g_near),
        [two_squares, two_squares],
        [
            ((4 * near * row_count, width), bf16), ((8 * near, 2 * HEADS, half), f32),
        ],
        "key_backward",
        8,
    )
    if not plain:
        feed = feed[0] + after(exchange(feed_low, 2), dk_part).astype(f32)
        feed_low = low_planes(feed)
        dk_part = after(dk_part, *feed_low)
    dk, dv = call_kernel(
        lambda *refs: key_backward_kernel(
            *refs, factor=factor, scale=scale, planes=far, part=1, last=True, total_planes=planes
        ),
        (info, kv_rows, q_all, cols, dk_part, dv_part, *g_far),
        [rows_low, rows_low],
        [
            ((4 * far * row_count, width), bf16), ((8 * far, 2 * HEADS, half), f32),
            two_squares, two_squares,
        ],
        "key_backward_last",
        3,
    )
    if not plain:
        feed = add_planes(feed, feed_low).astype(bf16)
        maps = add_sides(*maps)
        maps_low = maps[1].astype(bf16)
        dk = after(dk, feed, maps_low)
    tok_rows, *last = call_kernel(
        lambda *refs: self_grads_kernel(*refs, plain=plain),
        (info, x_rows, gr1, dq, dk, dv, w_self),
        [rows_low] + sink_shapes(2),
        [((width, width), f32)],
        "self_grads",
        4,
    )

    back_first = [(to, owner) for owner, to in perm_first]
    back_second = [(to, owner) for owner, to in perm_second]

    rows_out = jnp.stack([out_rows.astype(bf16), tok_rows])
    half_one = jnp.where(even, rows_out[:, :half], rows_out[:, half:])
    half_two = jnp.where(even, rows_out[:, half:], rows_out[:, :half])
    rows_out = jnp.concatenate(
        [lax.ppermute(half_one, "ctx", back_first), lax.ppermute(half_two, "ctx", back_second)],
        axis=1,
    ).astype(f32)
    layer_out, tokens_grad = rows_out[0], rows_out[1]
    lanes = width // 2
    if plain:

        def owned(matrix, axis):
            part = lax.psum_scatter(matrix, "fsdp", scatter_dimension=axis, tiled=True)
            return lax.psum(part, "ctx").astype(f32)

        feed, maps, last = feed[0], maps[0], last[0]
        ins = owned(jnp.concatenate([maps[5:6], last, maps[2:5]], axis=0), 1)
        outs = owned(maps[0:2], 1)
        up = owned(jnp.concatenate([feed[k] for k in range(4)], axis=1), 0)
        down = owned(feed[4:8].reshape(-1, width), 0)
        rest = jnp.stack([maps[6, 0:half_rows, 0:lanes], maps[6, half_rows:, 0:lanes]], axis=1)
        table = owned(rest[0:13].reshape(13, width).astype(f32), 1)
        shift = owned(rest[16:20].transpose(1, 0, 2).reshape(-1).astype(f32), 0)
        gain_sums, bias_sums = table[0:3], table[3:13]
    else:
        feed_planes = spread_planes(feed)
        last = add_sides(*add_cores(*last))
        last_low = after(last[1].astype(bf16), *feed_planes[1:])
        feed_own = jnp.stack(feed_planes)
        feed_other = exchange(feed_own, 2)
        last = add_chips(last, last_low)
        maps = add_chips(maps, maps_low)
        maps = add_planes(maps, low_planes(maps)).astype(bf16)
        last = add_planes(last, [after(low, maps) for low in low_planes(last)]).astype(bf16)
        up, down = call_kernel(
            lambda *refs: place_kernel(
                *refs,
                places=[(0, "cols", k) for k in range(4)] + [(1, "rows", k) for k in range(4)],
            ),
            (info, feed_own, feed_other, exchange(feed_own, 1), exchange(feed_other, 1)),
            ((ffn_in.shape, f32), (ffn_out.shape, f32)),
            [],
            "place_feed",
            4,
        )
        maps = jnp.concatenate([maps, after(last, feed_other)], axis=0)
        ins, outs, gain_sums, bias_sums, shift = call_kernel(
            place_maps_kernel,
            (info, *spread_chips(spread_planes(maps), up)),
            (
                (in_proj.shape, f32), (out_proj.shape, f32), ((3, lanes), f32), ((10, lanes), f32),
                ((1, 4 * lanes), f32),
            ),
            [((half_rows, width), f32)],
            "place_maps",
            4,
        )
        shift = shift.reshape(-1)
    return (
        layer_out[None], tokens_grad[None], memory_grad[None], ins, outs, up, down,
        gain_sums, bias_sums, shift,
    )


def solution(mesh):
    rows = P("fsdp", "ctx", None)
    params = (
        P(None, "fsdp", None), P(None, "fsdp", None), P("fsdp", None), P("fsdp", None),
        P(None, "fsdp"), P(None, "fsdp"), P("fsdp"),
    )
    return jax.shard_map(
        body,
        mesh=mesh,
        in_specs=(rows, rows, P("fsdp", None), P("fsdp", None), rows) + params,
        out_specs=(rows, rows, rows) + params,
        check_vma=False,
    )
```
